32 devices in a mesh: lat: 4 (over z), lon: 8 (over y, x, core).
Axes of the slice: x: 2, y: 2, z: 4, core: 2. Of those that a mesh axis runs over, the one named last changes fastest.
Arguments:
- atmos_state: bfloat16 [128, 512, 256], P('lat', 'lon'), may hold values from -6 to 6
- ocean_state: bfloat16 [192, 512, 128], P('lat', 'lon'), may hold values from -6 to 6
- atmos_cotangent: bfloat16 [128, 512, 256], P('lat', 'lon'), may hold values from -0.011962891 to 0.011962891
- ocean_cotangent: bfloat16 [192, 512, 128], P('lat', 'lon'), may hold values from -0.011962891 to 0.011962891
- land_sea: int32 [192, 512], P('lat', 'lon'), may hold values 0 or 1
- fold_partner: int32 [512], replicated, may hold values from 0 to 511, as said below
- ocean_pairs: int32 [96, 8, 4], P('lat', 'lon'), may hold values from 0 to 511, as said below
- ocean_counts: int32 [96, 8], P('lat', 'lon'), may hold values from 1 to 4
- ocean_weights: bfloat16 [96, 8, 4, 128, 128], P('lat', 'lon'), may hold values from -0.25 to 0.25
- atmos_pairs: int32 [64, 8, 4], P('lat', 'lon'), may hold values from 0 to 767, as said below
- atmos_counts: int32 [64, 8], P('lat', 'lon'), may hold values from 1 to 4
- atmos_weights: bfloat16 [64, 8, 4, 128, 128], P('lat', 'lon'), may hold values from -0.25 to 0.25
- flux_map: bfloat16 [256, 16], replicated, may hold values from -0.375 to 0.375
- surface_map: bfloat16 [128, 16], replicated, may hold values from -0.5 to 0.5
- flux_inject: bfloat16 [16, 128], replicated, may hold values from -1.5 to 1.5
- surface_inject: bfloat16 [16, 256], replicated, may hold values from -1.5 to 1.5
- atmos_kernel: bfloat16 [49, 256], replicated, may hold values from -0.875 to 0.875
- atmos_gain: bfloat16 [256], replicated, may hold values from 0.25 to 1.75
- atmos_w_in: bfloat16 [256, 1024], replicated, may hold values from -0.375 to 0.375
- atmos_w_out: bfloat16 [1024, 256], replicated, may hold values from -0.1875 to 0.1875
- ocean_kernel: bfloat16 [49, 128], replicated, may hold values from -0.875 to 0.875
- ocean_gain: bfloat16 [128], replicated, may hold values from 0.25 to 1.75
- ocean_w_in: bfloat16 [128, 512], replicated, may hold values from -0.5 to 0.5
- ocean_w_out: bfloat16 [512, 128], replicated, may hold values from -0.25 to 0.25
Outputs:
- atmos_next: bfloat16 [128, 512, 256], P('lat', 'lon')
- ocean_next: bfloat16 [192, 512, 128], P('lat', 'lon')
- atmos_kernel_grad: float32 [49, 256], replicated
- atmos_gain_grad: float32 [256], replicated
- atmos_w_in_grad: float32 [256, 1024], replicated
- atmos_w_out_grad: float32 [1024, 256], replicated
- ocean_kernel_grad: float32 [49, 128], replicated
- ocean_gain_grad: float32 [128], replicated
- ocean_w_in_grad: float32 [128, 512], replicated
- ocean_w_out_grad: float32 [512, 128], replicated
The draws below stay inside these ranges and needn't reach their ends.
Inputs may be any that keep to these rules, and one draw needn't show every extreme that they name: `ocean_pairs`: each entry is (owner device) * 16 + (block index on that device), devices numbered lat-major; the owner lies in the same latitude band as the ocean block or an adjacent one, and in the same longitude sector or an adjacent one, sectors wrapping around. `atmos_pairs`: each entry is (owner device) * 24 + (block index on that device), devices numbered lat-major; the owner lies in the same latitude band as the atmosphere block or an adjacent one, and in the same longitude sector or an adjacent one, sectors wrapping around. `ocean_counts`: only the first count entries of a block's list are live. `atmos_counts`: only the first count entries of a block's list are live. `fold_partner`: an involution: the partner of a column's partner is the column. `land_sea`: 1 on ocean cells, 0 on land.
All inputs are finite; a program needn't handle non-finite values. No bound on the sum of `land_sea` on one device may be relied on, other than what follows from the above.
Results may differ from the reference program's by a relative error of at most 0.0075.
Values may be sent and summed in bfloat16 or wider, within the bound.
A program may use at most 128 MiB of HBM per device.

```python
from functools import partial
import jax
import jax.numpy as jnp
from jax import lax

CA = 256
CO = 128
HA = 1024
HO = 512
NFIELD = 16
BCELLS = 128
PAIRS = 4
COLS = 64
AR = 32
OR = 48
BROWS = 2
ABLK = 16
OBLK = 24
LAT_BANDS = 4
LON_SECTORS = 8
ALAT = 128
OLAT = 192
LON_CELLS = 512


def owner_entries(key_device, device_number, entries, source_blocks):
    key_lat, key_lon, key_local = jax.random.split(key_device, 3)
    band = device_number // LON_SECTORS
    sector = device_number % LON_SECTORS
    lat_step = jax.random.randint(key_lat, (entries,), -1, 2)
    lon_step = jax.random.randint(key_lon, (entries,), -1, 2)
    owner_band = jnp.clip(band + lat_step, 0, LAT_BANDS - 1)
    owner_sector = (sector + lon_step) % LON_SECTORS
    owners = (owner_band * LON_SECTORS + owner_sector).astype(jnp.int32)
    local_ids = jax.random.randint(key_local, (entries,), 0, source_blocks)
    return owners * source_blocks + local_ids


def pair_listing(key, salt, block_count, source_blocks):
    device_total = LAT_BANDS * LON_SECTORS
    device_keys = jax.random.split(jax.random.fold_in(key, salt), device_total)
    maker = partial(owner_entries, entries=block_count * PAIRS, source_blocks=source_blocks)
    listing = jax.vmap(maker)(device_keys, jnp.arange(device_total, dtype=jnp.int32))
    listing = listing.reshape(LAT_BANDS, LON_SECTORS, block_count, PAIRS).transpose(0, 2, 1, 3)
    return listing.reshape(LAT_BANDS * block_count, LON_SECTORS, PAIRS).astype(jnp.int32)


def draw_ocean_pairs(key, part):
    return pair_listing(key, 11, OBLK, ABLK)


def draw_atmos_pairs(key, part):
    return pair_listing(key, 23, ABLK, OBLK)


def draw_fold_partner(key, part):
    pole_column = jax.random.randint(jax.random.fold_in(key, 5), (), 0, LON_CELLS)
    return ((pole_column - 1 - jnp.arange(LON_CELLS, dtype=jnp.int32)) % LON_CELLS).astype(jnp.int32)


def set_ends(drawn, key, least, largest):
    longest = drawn.shape.index(max(drawn.shape))
    spots = []
    for shift in (0, 1):
        where = [jax.random.randint(jax.random.fold_in(key, axis), (), 0, length) for axis, length in enumerate(drawn.shape)]
        where[longest] = (where[longest] + shift) % drawn.shape[longest]
        spots.append(tuple(where))
    return drawn.at[spots[0]].set(least).at[spots[1]].set(largest)


def block_levels(stream_key, dims, pieces, smallest, largest):
    level, own = 1.0, jax.random.fold_in(stream_key, 6)
    for dim, blocks in pieces:
        heights = jnp.exp(jax.random.uniform(jax.random.fold_in(own, dim), (blocks,), jnp.float32, smallest / len(pieces), largest / len(pieces)))
        level = level * jnp.repeat(heights, dims[dim] // blocks).reshape([-1 if axis == dim else 1 for axis in range(len(dims))])
    return level


def noise(stream_key, extent, spread, most, cuts=(), held_as=jnp.bfloat16):
    values = jax.random.normal(stream_key, extent, jnp.float32) * spread
    if len(cuts) > 0:
        values = block_levels(stream_key, extent, cuts, -0.22, 0.18) * values
    return jnp.clip(values, min=-most, max=most).astype(held_as)


def setup_inputs(seed: int = 0) -> dict:
    keys = jax.random.split(jax.random.key(seed), 25)
    return {
        "atmos_state": noise(keys[0], (ALAT, LON_CELLS, CA), 1.0, 6.0, ((0, 4), (1, 8))),
        "ocean_state": noise(keys[1], (OLAT, LON_CELLS, CO), 1.0, 6.0, ((0, 4), (1, 8))),
        "atmos_cotangent": noise(keys[2], (ALAT, LON_CELLS, CA), 0.002, 0.011962891, ((0, 4), (1, 8))),
        "ocean_cotangent": noise(keys[3], (OLAT, LON_CELLS, CO), 0.002, 0.011962891, ((0, 4), (1, 8))),
        "land_sea": set_ends((jax.random.randint(keys[4], (OLAT, LON_CELLS), 0, 10) < 7).astype(jnp.int32), jax.random.fold_in(keys[4], 1), 0, 1),
        "fold_partner": draw_fold_partner(jax.random.fold_in(keys[24], 71), 0),
        "ocean_pairs": draw_ocean_pairs(jax.random.fold_in(keys[24], 71), 0),
        "ocean_counts": set_ends(jax.random.randint(keys[7], (OLAT // BROWS, LON_SECTORS), 1, PAIRS + 1), jax.random.fold_in(keys[7], 1), 1, PAIRS).astype(jnp.int32),
        "ocean_weights": noise(keys[8], (OLAT // BROWS, LON_SECTORS, PAIRS, BCELLS, BCELLS), (PAIRS * BCELLS) ** -0.5, 0.25, ((0, 4), (1, 8))),
        "atmos_pairs": draw_atmos_pairs(jax.random.fold_in(keys[24], 71), 0),
        "atmos_counts": set_ends(jax.random.randint(keys[10], (ALAT // BROWS, LON_SECTORS), 1, PAIRS + 1), jax.random.fold_in(keys[10], 1), 1, PAIRS).astype(jnp.int32),
        "atmos_weights": noise(keys[11], (ALAT // BROWS, LON_SECTORS, PAIRS, BCELLS, BCELLS), (PAIRS * BCELLS) ** -0.5, 0.25, ((0, 4), (1, 8))),
        "flux_map": noise(keys[12], (CA, NFIELD), CA ** -0.5, 0.375),
        "surface_map": noise(keys[13], (CO, NFIELD), CO ** -0.5, 0.5),
        "flux_inject": noise(keys[14], (NFIELD, CO), NFIELD ** -0.5, 1.5),
        "surface_inject": noise(keys[15], (NFIELD, CA), NFIELD ** -0.5, 1.5),
        "atmos_kernel": noise(keys[16], (49, CA), 49 ** -0.5, 0.875),
        "atmos_gain": jnp.clip(1.0 + 0.15 * jax.random.normal(keys[17], (CA,), jnp.float32), 0.25, 1.75).astype(jnp.bfloat16),
        "atmos_w_in": noise(keys[18], (CA, HA), CA ** -0.5, 0.375),
        "atmos_w_out": noise(keys[19], (HA, CA), HA ** -0.5, 0.1875),
        "ocean_kernel": noise(keys[20], (49, CO), 49 ** -0.5, 0.875),
        "ocean_gain": jnp.clip(1.0 + 0.15 * jax.random.normal(keys[21], (CO,), jnp.float32), 0.25, 1.75).astype(jnp.bfloat16),
        "ocean_w_in": noise(keys[22], (CO, HO), CO ** -0.5, 0.5),
        "ocean_w_out": noise(keys[23], (HO, CO), HO ** -0.5, 0.25),
    }


epsilon = 1e-06

def contract_rows(left, right):
    return lax.dot_general(left, right, (((0,), (0,)), ((), ())), preferred_element_type=jnp.float32)

def block_pass(padded, cotangent, keep_mask, kernel, gain, w_in, w_out):
    row_count = padded.shape[0] - 6
    col_count = padded.shape[1] - 6
    channels = padded.shape[2]
    convolved = jnp.zeros((row_count, col_count, channels), jnp.float32)
    for offset in range(49):
        tap_row = offset // 7
        tap_col = offset % 7
        window = padded[tap_row:tap_row + row_count, tap_col:tap_col + col_count, :].astype(jnp.float32)
        convolved = convolved + window * kernel[offset].astype(jnp.float32)
    centre = convolved - lax.optimization_barrier(jnp.mean(convolved, axis=-1, keepdims=True))
    inv_spread = lax.rsqrt(lax.optimization_barrier(jnp.mean(centre * centre, axis=-1, keepdims=True)) + epsilon)
    unit_part = centre * inv_spread
    gain_wide = gain.astype(jnp.float32)
    normed = (unit_part * gain_wide).astype(jnp.bfloat16).reshape(row_count * col_count, channels)
    pre_act = jnp.dot(normed, w_in, preferred_element_type=jnp.float32)
    hidden = jax.nn.gelu(pre_act).astype(jnp.bfloat16)
    update = jnp.dot(hidden, w_out, preferred_element_type=jnp.float32).reshape(row_count, col_count, channels)
    interior = padded[3:3 + row_count, 3:3 + col_count, :].astype(jnp.float32)
    result = ((interior + update) * keep_mask).astype(jnp.bfloat16)
    upstream = (cotangent.astype(jnp.float32) * keep_mask).astype(jnp.bfloat16).reshape(row_count * col_count, channels)
    grad_out = contract_rows(hidden, upstream)
    grad_hidden = lax.dot_general(upstream, w_out, (((1,), (1,)), ((), ())), preferred_element_type=jnp.float32)
    _, gelu_back = jax.vjp(jax.nn.gelu, pre_act)
    grad_pre = gelu_back(grad_hidden)[0].astype(jnp.bfloat16)
    grad_in = contract_rows(normed, grad_pre)
    grad_normed = lax.dot_general(grad_pre, w_in, (((1,), (1,)), ((), ())), preferred_element_type=jnp.float32)
    grad_normed = grad_normed.reshape(row_count, col_count, channels)
    grad_gain = lax.optimization_barrier(jnp.sum(grad_normed * unit_part, axis=(0, 1)))
    grad_unit = grad_normed * gain_wide
    grad_conv = inv_spread * (grad_unit - lax.optimization_barrier(jnp.mean(grad_unit, axis=-1, keepdims=True)) - unit_part * lax.optimization_barrier(jnp.mean(grad_unit * unit_part, axis=-1, keepdims=True)))
    tap_sums = []
    for offset in range(49):
        tap_row = offset // 7
        tap_col = offset % 7
        window = padded[tap_row:tap_row + row_count, tap_col:tap_col + col_count, :].astype(jnp.float32)
        tap_sums.append(lax.optimization_barrier(jnp.sum(grad_conv * window, axis=(0, 1))))
    grad_kernel = jnp.stack(tap_sums)
    return (result, (grad_kernel, grad_gain, grad_in, grad_out))

def make_blocks(source, projection, keep_cells, block_count):
    channels = source.shape[2]
    shaped = source.reshape(LAT_BANDS, block_count, BROWS, LON_SECTORS, COLS, channels)
    shaped = shaped.transpose(0, 3, 1, 2, 4, 5).reshape(-1, BCELLS, channels)
    kept = keep_cells.reshape(LAT_BANDS, block_count, BROWS, LON_SECTORS, COLS)
    kept = kept.transpose(0, 3, 1, 2, 4).reshape(-1, 1, BCELLS)
    values = jnp.einsum('nkc,cf->nfk', shaped.astype(jnp.float32), projection.astype(jnp.float32), precision=lax.Precision.HIGHEST)
    return (values * kept).astype(jnp.bfloat16)

def remap(listing, pairs, counts, weights):

    def one_row(items):
        row_pairs, row_counts, row_weights = items
        picked = jnp.take(listing, row_pairs, axis=0).astype(jnp.float32)
        in_use = (jnp.arange(PAIRS)[None, :] < row_counts[:, None]).astype(jnp.float32)
        picked = picked * in_use[:, :, None, None]
        return jnp.einsum('spfc,spcd->sfd', picked, row_weights.astype(jnp.float32), precision=lax.Precision.HIGHEST)
    return lax.map(one_row, (pairs, counts, weights)).astype(jnp.bfloat16)

def inject(state, remapped, block_count, projection):
    grid_rows = remapped.reshape(LAT_BANDS * block_count, LON_SECTORS, NFIELD, BROWS, COLS)
    grid_rows = grid_rows.transpose(0, 3, 1, 4, 2).reshape(LAT_BANDS * block_count * BROWS, LON_CELLS, NFIELD)
    added = jnp.einsum('ijf,fc->ijc', grid_rows.astype(jnp.float32), projection.astype(jnp.float32), precision=lax.Precision.HIGHEST)
    return (state.astype(jnp.float32) + added).astype(jnp.bfloat16)

def run_grid(padded, cotangent, keep_mask, kernel, gain, w_in, w_out, band_rows):
    channels = padded.shape[2]
    hidden_width = w_in.shape[1]
    initial = (jnp.zeros((49, channels), jnp.float32), jnp.zeros((channels,), jnp.float32), jnp.zeros((channels, hidden_width), jnp.float32), jnp.zeros((hidden_width, channels), jnp.float32))

    def one_band(totals, band_index):
        low_row = (band_index * band_rows).astype(jnp.int32)
        band_padded = lax.dynamic_slice_in_dim(padded, low_row, band_rows + 6, 0)
        band_cotangent = lax.dynamic_slice_in_dim(cotangent, low_row, band_rows, 0)
        band_mask = lax.dynamic_slice_in_dim(keep_mask, low_row, band_rows, 0)
        result, gradients = block_pass(band_padded, band_cotangent, band_mask, kernel, gain, w_in, w_out)
        return (tuple((first_sum + second_sum for first_sum, second_sum in zip(totals, gradients))), result)
    totals, results = lax.scan(one_band, initial, jnp.arange(LAT_BANDS, dtype=jnp.int32))
    return (results.reshape((LAT_BANDS * band_rows,) + results.shape[2:]), totals)

def reference(atmos_state, ocean_state, atmos_cotangent, ocean_cotangent, land_sea, fold_partner, ocean_pairs, ocean_counts, ocean_weights, atmos_pairs, atmos_counts, atmos_weights, flux_map, surface_map, flux_inject, surface_inject, atmos_kernel, atmos_gain, atmos_w_in, atmos_w_out, ocean_kernel, ocean_gain, ocean_w_in, ocean_w_out):
    wet_cells = land_sea.astype(jnp.float32)
    atmos_fields = make_blocks(atmos_state, flux_map, jnp.ones((ALAT, LON_CELLS), jnp.float32), ABLK)
    ocean_fields = make_blocks(ocean_state, surface_map, wet_cells, OBLK)
    to_ocean = remap(atmos_fields, ocean_pairs, ocean_counts, ocean_weights)
    to_atmos = remap(ocean_fields, atmos_pairs, atmos_counts, atmos_weights)
    ocean_input = inject(ocean_state, to_ocean, OBLK, flux_inject)
    atmos_input = inject(atmos_state, to_atmos, ABLK, surface_inject)
    atmos_wide = jnp.concatenate([atmos_input[:, -3:], atmos_input, atmos_input[:, :3]], axis=1)
    atmos_padded = jnp.pad(atmos_wide, ((3, 3), (0, 0), (0, 0)))
    ocean_wide = jnp.concatenate([ocean_input[:, -3:], ocean_input, ocean_input[:, :3]], axis=1)
    top_rows = jnp.stack([ocean_input[OLAT - 1], ocean_input[OLAT - 2], ocean_input[OLAT - 3]])
    fold_columns = jnp.take(fold_partner, (jnp.arange(-3, LON_CELLS + 3) % LON_CELLS).astype(jnp.int32))
    folded = jnp.take(top_rows, fold_columns, axis=1)
    ocean_padded = jnp.concatenate([jnp.zeros((3, LON_CELLS + 6, CO), jnp.bfloat16), ocean_wide, folded], axis=0)
    atmos_next, atmos_grads = run_grid(atmos_padded, atmos_cotangent, jnp.ones((ALAT, LON_CELLS, 1), jnp.float32), atmos_kernel, atmos_gain, atmos_w_in, atmos_w_out, AR)
    ocean_next, ocean_grads = run_grid(ocean_padded, ocean_cotangent, wet_cells[:, :, None], ocean_kernel, ocean_gain, ocean_w_in, ocean_w_out, OR)
    return (atmos_next, ocean_next, atmos_grads[0], atmos_grads[1], atmos_grads[2], atmos_grads[3], ocean_grads[0], ocean_grads[1], ocean_grads[2], ocean_grads[3])
```

```python
import functools

import jax
import jax.numpy as jnp
from jax import lax
from jax.experimental import pallas as pl
from jax.experimental.pallas import tpu as pltpu
from jax.sharding import PartitionSpec as P

NFIELD = 16
BCELLS = 128
PAIRS = 4
LANES = 128
SMALL = 64
MESH = pl.DeviceIdType.MESH
epsilon = 1e-06
TANH_SCALE = 0.7978845608028654
TANH_CUBIC = 0.044715


def dot(left, right, dims=((1,), (0,))):
    return lax.dot_general(left, right, (dims, ((), ())), preferred_element_type=jnp.float32)


def shift_phase(padded_ref, shifted, rows, cols):
    def one_row(row, carry):
        wide = padded_ref[row].astype(jnp.float32)
        for tap_col in range(7):
            shifted[tap_col, row] = wide[tap_col : tap_col + cols].astype(jnp.bfloat16)
        return carry

    lax.fori_loop(0, rows + 6, one_row, 0)


def conv_phase(shifted, kernel_ref, banded, conv, rows, cols, channels):
    pair_step = 8
    across = lax.broadcasted_iota(jnp.int32, (LANES, LANES), 0)
    down = lax.broadcasted_iota(jnp.int32, (LANES, LANES), 1)
    eye = across == down
    for lane in range(0, channels, LANES):
        for tap_col in range(7):
            for step in range(4):
                for low in range(2):
                    for out in range(2):
                        tap_row = 2 * step + low - out
                        if 0 <= tap_row < 7:
                            tap = kernel_ref[pl.ds(tap_row * 7 + tap_col, 1), lane : lane + LANES]
                            block = jnp.where(eye, tap, 0.0).astype(jnp.bfloat16)
                        else:
                            block = jnp.zeros((LANES, LANES), jnp.bfloat16)
                        banded[
                            tap_col * 4 + step,
                            low * LANES : low * LANES + LANES,
                            out * LANES : out * LANES + LANES,
                        ] = block

        def one_chunk(index, carry):
            total = None
            for tap_col in range(7):
                for step in range(4):
                    window = shifted[
                        tap_col,
                        pl.ds(2 * (index * pair_step + step), 2 * pair_step),
                        :,
                        lane : lane + LANES,
                    ].reshape(pair_step, 2, cols, LANES)
                    left = jnp.concatenate(
                        [
                            window[:, 0].reshape(pair_step * cols, LANES),
                            window[:, 1].reshape(pair_step * cols, LANES),
                        ],
                        axis=1,
                    )
                    part = dot(left, banded[tap_col * 4 + step])
                    total = part if total is None else total + part
            for out in range(2):
                conv[pl.ds(index * pair_step, pair_step), out, :, lane : lane + LANES] = total[
                    :, out * LANES : out * LANES + LANES
                ].reshape(pair_step, cols, LANES)
            return carry

        lax.fori_loop(0, rows // 2 // pair_step, one_chunk, 0)


def grid_kernel(*refs, rows, cols, channels, hidden_width, masked):
    if masked:
        padded_ref, cot_ref, mask_ref, before_ref, kernel_ref, gain_ref, w_in_ref, w_out_ref = refs[:8]
        rest, sem = refs[8:-1], refs[-1]
    else:
        padded_ref, cot_ref, kernel_ref, gain_ref, w_in_ref, w_out_ref = refs[:6]
        rest = refs[6:]
    next_ref, packed_ref, w_in_sum, w_out_sum, small_sum, shifted, banded, conv, slope = rest
    at_row = 0
    if masked:
        at_row = before_ref.shape[0]
        carry_copy = pltpu.make_async_copy(before_ref, packed_ref.at[0:at_row, :], sem)
        carry_copy.start()
    row_step = 8
    cells = row_step * cols
    chunk = 256
    shift_phase(padded_ref, shifted, rows, cols)
    conv_phase(shifted, kernel_ref, banded, conv, rows, cols, channels)
    w_in_sum[...] = jnp.zeros_like(w_in_sum)
    w_out_sum[...] = jnp.zeros_like(w_out_sum)
    small_sum[...] = jnp.zeros_like(small_sum)
    gain = gain_ref[...]

    def one_block(index, gain_total):
        value = conv[pl.ds(index * (row_step // 2), row_step // 2)].reshape(cells, channels)
        centre = value - jnp.mean(value, axis=-1, keepdims=True)
        inv = lax.rsqrt(jnp.mean(centre * centre, axis=-1, keepdims=True) + epsilon)
        unit = centre * inv
        normed = (unit * gain).astype(jnp.bfloat16)
        where = pl.ds(index * cells, cells)
        upstream = cot_ref[where, :]
        if masked:
            keep = mask_ref[where, :]
            keep = jnp.concatenate([keep] * (channels // LANES), axis=1)
            upstream = upstream * keep
        normed_t = normed.T
        upstream_t = upstream.T
        update = None
        back = None
        for at in range(0, hidden_width, chunk):
            w_in = w_in_ref[:, at : at + chunk]
            w_out = w_out_ref[at : at + chunk, :]
            pre = dot(normed, w_in)
            grad_hidden = dot(upstream, w_out, ((1,), (1,)))
            square = pre * pre
            gate = 0.5 + 0.5 * jnp.tanh(pre * (TANH_SCALE + (TANH_SCALE * TANH_CUBIC) * square))
            active = pre * gate
            slope_part = 2 * TANH_SCALE + (6 * TANH_SCALE * TANH_CUBIC) * square
            grad_pre = (grad_hidden * (gate + active * (1.0 - gate) * slope_part)).astype(jnp.bfloat16)
            active = active.astype(jnp.bfloat16)
            part = dot(active, w_out)
            update = part if update is None else update + part
            part = dot(grad_pre, w_in, ((1,), (1,)))
            back = part if back is None else back + part
            for total, part in (
                (w_out_sum, dot(upstream_t, active)),
                (w_in_sum, dot(normed_t, grad_pre)),
            ):
                for lane in range(0, chunk, LANES):
                    total[(at + lane) // LANES] += part[:, lane : lane + LANES]
        inside = shifted[3, pl.ds(index * row_step + 3, row_step)].reshape(cells, channels)
        result = inside.astype(jnp.float32) + update
        if masked:
            result = result * keep.astype(jnp.float32)
        next_ref[where, :] = result.astype(jnp.bfloat16)
        gain_total = gain_total + jnp.sum((back * unit).reshape(cells // 8, 8, channels), axis=0)
        back = back * gain
        level = jnp.mean(back, axis=-1, keepdims=True)
        tilt = jnp.mean(back * unit, axis=-1, keepdims=True)
        slope[pl.ds(index * row_step, row_step)] = (
            (inv * (back - level - unit * tilt)).astype(jnp.bfloat16).reshape(row_step, cols, channels)
        )
        return gain_total

    gain_total = lax.fori_loop(0, rows // row_step, one_block, jnp.zeros((8, channels), jnp.float32))
    small_sum[49:50, :] = jnp.sum(gain_total, axis=0, keepdims=True)
    for lane in range(0, channels, LANES):
        for tap_row in range(7):

            def one_row(row, totals):
                grad = slope[row, :, lane : lane + LANES]
                sums = []
                for tap_col in range(7):
                    product = grad * shifted[tap_col, row + tap_row, :, lane : lane + LANES]
                    pieces = [product[at : at + 16] for at in range(0, cols, 16)]
                    while len(pieces) > 1:
                        pieces = [a + b for a, b in zip(pieces[::2], pieces[1::2])]
                    wide = pieces[0].astype(jnp.float32)
                    sums.append(totals[tap_col] + wide[:8] + wide[8:])
                return tuple(sums)

            totals = lax.fori_loop(
                0, rows, one_row, tuple(jnp.zeros((8, LANES), jnp.float32) for _ in range(7)), unroll=4
            )
            for tap_col in range(7):
                small_sum[pl.ds(tap_row * 7 + tap_col, 1), lane : lane + LANES] = jnp.sum(
                    totals[tap_col], axis=0, keepdims=True
                )
    for total in (w_in_sum, w_out_sum):
        for block in range(hidden_width // LANES):
            packed_ref[at_row : at_row + channels, :] = total[block].astype(jnp.bfloat16)
            at_row += channels
    for lane in range(0, channels, LANES):
        packed_ref[at_row : at_row + SMALL, :] = small_sum[:, lane : lane + LANES].astype(jnp.bfloat16)
        at_row += SMALL
    if at_row < packed_ref.shape[0]:
        spare = packed_ref.shape[0] - at_row
        packed_ref[at_row:, :] = jnp.zeros((spare, LANES), jnp.bfloat16)
    if masked:
        carry_copy.wait()


def packed_rows(channels, hidden_width):
    return 2 * (hidden_width // LANES) * channels + channels // LANES * SMALL


def run_grid(padded, cotangent, mask, before, rows_out, kernel, gain, w_in, w_out):
    rows, cols, channels = cotangent.shape
    hidden_width = w_in.shape[1]
    cells = rows * cols
    masked = mask is not None
    args = [padded, cotangent.reshape(cells, channels)]
    vmem = pl.BlockSpec(memory_space=pltpu.VMEM)
    specs = [vmem, vmem]
    if masked:
        args += [mask, before]
        specs += [vmem, pl.BlockSpec(memory_space=pl.ANY)]
    args += [kernel.astype(jnp.float32), gain.astype(jnp.float32).reshape(1, channels), w_in, w_out]
    specs += [vmem] * 4
    result, packed = pl.pallas_call(
        functools.partial(
            grid_kernel,
            rows=rows,
            cols=cols,
            channels=channels,
            hidden_width=hidden_width,
            masked=masked,
        ),
        out_shape=(
            jax.ShapeDtypeStruct((cells, channels), jnp.bfloat16),
            jax.ShapeDtypeStruct((rows_out, LANES), jnp.bfloat16),
        ),
        in_specs=specs,
        out_specs=(vmem, vmem),
        scratch_shapes=[
            pltpu.VMEM((hidden_width // LANES, channels, LANES), jnp.float32),
            pltpu.VMEM((hidden_width // LANES, channels, LANES), jnp.float32),
            pltpu.VMEM((SMALL, channels), jnp.float32),
            pltpu.VMEM((7, rows + 6, cols, channels), jnp.bfloat16),
            pltpu.VMEM((28, 2 * LANES, 2 * LANES), jnp.bfloat16),
            pltpu.VMEM((rows // 2, 2, cols, channels), jnp.float32),
            pltpu.VMEM((rows, cols, channels), jnp.bfloat16),
        ]
        + ([pltpu.SemaphoreType.DMA] if masked else []),
        compiler_params=pltpu.CompilerParams(vmem_limit_bytes=60 * 1024 * 1024),
    )(*args)
    return result.reshape(rows, cols, channels), packed


def unpack_kernel(widths, packed_ref, *outs):
    at = 0
    for number, (channels, hidden_width) in enumerate(widths):
        kernel_out, gain_out, w_in_out, w_out_out = outs[4 * number : 4 * number + 4]
        for block in range(hidden_width // LANES):
            w_in_out[:, block * LANES : block * LANES + LANES] = packed_ref[at : at + channels, :].astype(
                jnp.float32
            )
            at += channels
        for block in range(hidden_width // LANES):
            w_out_out[block * LANES : block * LANES + LANES, :] = (
                packed_ref[at : at + channels, :].astype(jnp.float32).T
            )
            at += channels
        for lane in range(0, channels, LANES):
            small = packed_ref[at : at + SMALL, :].astype(jnp.float32)
            kernel_out[:, lane : lane + LANES] = small[:49]
            gain_out[:, lane : lane + LANES] = small[49:50]
            at += SMALL


def unpack(packed, widths):
    shapes = []
    for channels, hidden_width in widths:
        shapes += [(49, channels), (1, channels), (channels, hidden_width), (hidden_width, channels)]
    vmem = pl.BlockSpec(memory_space=pltpu.VMEM)
    outs = pl.pallas_call(
        functools.partial(unpack_kernel, widths),
        out_shape=tuple(jax.ShapeDtypeStruct(shape, jnp.float32) for shape in shapes),
        in_specs=[vmem],
        out_specs=(vmem,) * len(shapes),
        compiler_params=pltpu.CompilerParams(vmem_limit_bytes=40 * 1024 * 1024),
    )(packed)
    return [out.reshape(-1) if out.shape[0] == 1 else out for out in outs]


def aligned(index):
    return pl.multiple_of(index, 16)


def greet(partners):
    barrier = pltpu.get_barrier_semaphore()
    for partner in partners:
        pl.semaphore_signal(barrier, inc=1, device_id=partner, device_id_type=MESH)
    pl.semaphore_wait(barrier, len(partners))


def sum_plan(lon_count):
    spans = []
    span = 2
    while span < lon_count:
        spans.append(span)
        span *= 2
    return (spans, spans[::-1])


def sum_kernel(length, lat_count, lon_count, share_ref, full_ref, *scratch):
    plan = sum_plan(lon_count)
    steps = len(plan[0])
    half, quarter = length // 2, length // 4
    first, lat_send, lat_recv, comb = scratch[:4]
    sends = [scratch[4 + part * steps : 4 + part * steps + steps] for part in range(2)]
    recvs = [scratch[4 + (2 + part) * steps : 4 + (2 + part) * steps + steps] for part in range(2)]
    totals = [scratch[4 + (4 + part) * steps : 4 + (4 + part) * steps + steps] for part in range(2)]
    send_sem, recv_sem = scratch[-2:]
    lat, lon = lax.axis_index("lat"), lax.axis_index("lon")
    core = lon % 2

    def flipped(span):
        bit = (lon // span) % 2
        return (lat, lon + span - 2 * span * bit), bit

    peers = [((lat + step) % lat_count, lon) for step in range(1, lat_count)]
    greet([flipped(1)[0]] + [flipped(span)[0] for span in plan[0]] + peers)
    count = [0]

    def push(source, target, device):
        number = count[0]
        count[0] += 1
        copy = pltpu.make_async_remote_copy(
            src_ref=source,
            dst_ref=target,
            send_sem=send_sem.at[number],
            recv_sem=recv_sem.at[number],
            device_id=device,
            device_id_type=MESH,
        )
        copy.start()
        return copy

    pending = []
    opening = []
    for part in range(2):
        opening.append(
            push(
                share_ref.at[pl.ds(aligned((1 - core) * half + part * quarter), quarter), :],
                first.at[part],
                flipped(1)[0],
            )
        )
    active = [None, None]
    for part in range(2):
        opening[part].wait_recv()
        pending.append(opening[part])
        device, bit = flipped(plan[part][0])
        size = quarter // 2
        own = core * half + part * quarter

        def summed(start):
            return share_ref[pl.ds(aligned(own + start), size), :].astype(jnp.float32) + first[
                part, pl.ds(aligned(start), size), :
            ].astype(jnp.float32)

        sends[part][0][...] = summed((1 - bit) * size).astype(jnp.bfloat16)
        active[part] = push(sends[part][0], recvs[part][0], device)
        totals[part][0][...] = summed(bit * size)
    size = quarter // 2
    for step in range(steps):
        for part in range(2):
            active[part].wait_recv()
            pending.append(active[part])
            recv, total = recvs[part][step], totals[part][step]
            if step + 1 == steps:
                comb[part * size : part * size + size, :] = total[...] + recv[...].astype(jnp.float32)
                continue
            device, bit = flipped(plan[part][step + 1])
            rest = size // 2

            def joined(start):
                where = pl.ds(aligned(start), rest)
                return total[where, :] + recv[where, :].astype(jnp.float32)

            sends[part][step + 1][...] = joined((1 - bit) * rest).astype(jnp.bfloat16)
            active[part] = push(sends[part][step + 1], recvs[part][step + 1], device)
            totals[part][step + 1][...] = joined(bit * rest)
        if step + 1 < steps:
            size //= 2
    bases = []
    for part in range(2):
        base = core * half + part * quarter
        extent = quarter
        levels = []
        for span in plan[part]:
            extent //= 2
            base = base + ((lon // span) % 2) * extent
            levels.append((base, extent, span))
        bases.append(levels)
    chunk = 2 * size // lat_count
    lat_send[...] = comb[...].astype(jnp.bfloat16)
    arriving = []
    for step in range(1, lat_count):
        peer = (lat + step) % lat_count
        arriving.append(
            push(
                lat_send.at[pl.ds(aligned(peer * chunk), chunk), :],
                lat_recv.at[step - 1],
                (peer, lon),
            )
        )
    total = comb[pl.ds(aligned(lat * chunk), chunk), :]
    for step, copy in enumerate(arriving):
        copy.wait_recv()
        pending.append(copy)
        total = total + lat_recv[step].astype(jnp.float32)
    upper = (2 * lat) // lat_count
    low_base, high_base = bases[0][-1][0], bases[1][-1][0]
    place = low_base + upper * (high_base - low_base) + (lat - upper * (lat_count // 2)) * chunk
    mine = pl.ds(aligned(place), chunk)
    full_ref[mine, :] = total.astype(jnp.bfloat16)
    arriving = [push(full_ref.at[mine, :], full_ref.at[mine, :], peer) for peer in peers]
    for copy in arriving:
        copy.wait_recv()
        pending.append(copy)
    for step in reversed(range(steps)):
        arriving = []
        for part in range(2):
            base, extent, span = bases[part][step]
            region = full_ref.at[pl.ds(aligned(base), extent), :]
            arriving.append(push(region, region, flipped(span)[0]))
        for copy in arriving:
            copy.wait_recv()
            pending.append(copy)
    arriving = []
    for part in range(2):
        region = full_ref.at[pl.ds(aligned(core * half + part * quarter), quarter), :]
        arriving.append(push(region, region, flipped(1)[0]))
    for copy in arriving:
        copy.wait_recv()
        pending.append(copy)
    for copy in pending:
        copy.wait_send()


def sum_over_devices(share):
    lat_count, lon_count = lax.axis_size("lat"), lax.axis_size("lon")
    length = share.shape[0]
    plan = sum_plan(lon_count)
    steps = len(plan[0])
    sizes = [length // 4 // 2 ** (step + 1) for step in range(steps)]
    chunk = 2 * sizes[-1] // lat_count
    copies = 2 + 2 * steps + (lat_count - 1) * 2 + 2 * steps + 2
    narrow = [pltpu.VMEM((size, LANES), jnp.bfloat16) for size in sizes]
    wide = [pltpu.VMEM((size, LANES), jnp.float32) for size in sizes]
    vmem = pl.BlockSpec(memory_space=pltpu.VMEM)
    return pl.pallas_call(
        functools.partial(sum_kernel, length, lat_count, lon_count),
        out_shape=jax.ShapeDtypeStruct((length, LANES), jnp.bfloat16),
        in_specs=[vmem],
        out_specs=vmem,
        scratch_shapes=[
            pltpu.VMEM((2, length // 4, LANES), jnp.bfloat16),
            pltpu.VMEM((2 * sizes[-1], LANES), jnp.bfloat16),
            pltpu.VMEM((lat_count - 1, chunk, LANES), jnp.bfloat16),
            pltpu.VMEM((2 * sizes[-1], LANES), jnp.float32),
            *narrow,
            *narrow,
            *narrow,
            *narrow,
            *wide,
            *wide,
            pltpu.SemaphoreType.DMA((copies,)),
            pltpu.SemaphoreType.DMA((copies,)),
        ],
        compiler_params=pltpu.CompilerParams(
            collective_id=2, has_side_effects=True, vmem_limit_bytes=40 * 1024 * 1024
        ),
    )(share)


def extended(shard, sides, width):
    for axis, dim in sides:
        devices, length = (lax.axis_size(axis), shard.shape[dim])
        up = [(i, (i + 1) % devices) for i in range(devices)]
        down = [(j, i) for i, j in up]
        last = lax.slice_in_dim(shard, length - width, length, axis=dim)
        initial = lax.slice_in_dim(shard, 0, width, axis=dim)
        before = lax.ppermute(last, axis, up)
        after = lax.ppermute(initial, axis, down)
        shard = jnp.concatenate([before, shard, after], axis=dim)
    return shard


def make_blocks(source, projection, keep_cells):
    channels = source.shape[2]
    shaped = source.reshape(-1, BCELLS, channels)
    values = jnp.einsum("nkc,cf->nfk", shaped, projection, preferred_element_type=jnp.float32)
    return (values * keep_cells.reshape(-1, 1, BCELLS)).astype(jnp.bfloat16)


def fetch_remap(source_blocks, pair_ids, pair_counts, remap_weights):
    lon_count = lax.axis_size("lon")
    lat_index = lax.axis_index("lat")
    lon_index = lax.axis_index("lon")
    source_count = source_blocks.shape[0]
    target_count = pair_ids.shape[0]
    placed = source_blocks[None, None]
    nearby = extended(placed, (("lat", 0), ("lon", 1)), 1)
    nearby = nearby.reshape(9 * source_count, NFIELD, BCELLS)
    flat_ids = pair_ids.reshape(-1)
    owners = flat_ids // source_count
    local_ids = flat_ids % source_count
    band_step = owners // lon_count - lat_index + 1
    sector_step = (owners % lon_count - lon_index + 1) % lon_count
    positions = (band_step * 3 + sector_step) * source_count + local_ids
    in_use = (jnp.arange(PAIRS)[None, :] < pair_counts).reshape(-1, 1)
    chosen = positions[:, None] == jnp.arange(9 * source_count)[None, :]
    chosen = (chosen & in_use).astype(jnp.bfloat16)
    picked = jnp.dot(chosen, nearby.reshape(9 * source_count, -1), preferred_element_type=jnp.float32)
    picked = picked.astype(jnp.bfloat16).reshape(target_count, PAIRS, NFIELD, BCELLS)
    remapped = jnp.einsum(
        "nkfc,nkcd->nfd",
        picked,
        remap_weights.reshape(target_count, PAIRS, BCELLS, BCELLS),
        preferred_element_type=jnp.float32,
    )
    return remapped.astype(jnp.bfloat16)


def inject(state, remapped, projection):
    added = jnp.einsum("nfk,fc->nkc", remapped, projection, preferred_element_type=jnp.float32)
    return (state.astype(jnp.float32) + added.reshape(state.shape)).astype(jnp.bfloat16)


def pad_tile(source):
    padded = extended(source, (("lat", 0), ("lon", 1)), 3)
    lat_index = lax.axis_index("lat")
    lat_count = lax.axis_size("lat")
    rim_rows = jnp.arange(padded.shape[0])
    outside = (rim_rows < 3) & (lat_index == 0) | (rim_rows >= padded.shape[0] - 3) & (
        lat_index == lat_count - 1
    )
    padded = jnp.where(outside[:, None, None], jnp.zeros_like(padded), padded)
    return padded


def shards(
    atmos_state,
    ocean_state,
    atmos_cotangent,
    ocean_cotangent,
    land_sea,
    fold_partner,
    ocean_pairs,
    ocean_counts,
    ocean_weights,
    atmos_pairs,
    atmos_counts,
    atmos_weights,
    flux_map,
    surface_map,
    flux_inject,
    surface_inject,
    atmos_kernel,
    atmos_gain,
    atmos_w_in,
    atmos_w_out,
    ocean_kernel,
    ocean_gain,
    ocean_w_in,
    ocean_w_out,
):
    wet_cells = land_sea.astype(jnp.float32)
    col_count = atmos_state.shape[1]
    atmos_fields = make_blocks(atmos_state, flux_map, jnp.ones(atmos_state.shape[:2], jnp.float32))
    ocean_fields = make_blocks(ocean_state, surface_map, wet_cells)
    to_ocean = fetch_remap(atmos_fields, ocean_pairs, ocean_counts, ocean_weights)
    to_atmos = fetch_remap(ocean_fields, atmos_pairs, atmos_counts, atmos_weights)
    ocean_input = inject(ocean_state, to_ocean, flux_inject)
    atmos_input = inject(atmos_state, to_atmos, surface_inject)
    atmos_padded = pad_tile(atmos_input)
    ocean_padded = pad_tile(ocean_input)
    top_rows = jnp.stack([ocean_input[-1], ocean_input[-2], ocean_input[-3]])
    whole_rows = lax.all_gather(top_rows, "lon", axis=1, tiled=True)
    first_column = lax.axis_index("lon") * col_count
    columns = (first_column - 3 + jnp.arange(col_count + 6, dtype=jnp.int32)) % whole_rows.shape[1]
    circle = jnp.arange(whole_rows.shape[1], dtype=jnp.int32)
    partners = jnp.sum(jnp.where(columns[:, None] == circle[None, :], fold_partner[None, :], 0), axis=1)
    chosen = (partners[:, None] == circle[None, :]).astype(jnp.bfloat16)
    folded = lax.dot_general(
        chosen, whole_rows, (((1,), (1,)), ((), ())), preferred_element_type=jnp.float32
    )
    folded = folded.astype(jnp.bfloat16).transpose(1, 0, 2)
    is_top = lax.axis_index("lat") == lax.axis_size("lat") - 1
    ocean_padded = jnp.where(
        is_top, jnp.concatenate([ocean_padded[:-3], folded], axis=0), ocean_padded
    )
    widths = tuple(w_in.shape for w_in in (atmos_w_in, ocean_w_in))
    atmos_rows = packed_rows(*widths[0])
    total_rows = atmos_rows + packed_rows(*widths[1])
    total_rows += -total_rows % (16 * lax.axis_size("lat") * lax.axis_size("lon"))
    atmos_next, packed = run_grid(
        atmos_padded,
        atmos_cotangent,
        None,
        None,
        atmos_rows,
        atmos_kernel,
        atmos_gain,
        atmos_w_in,
        atmos_w_out,
    )
    wet_lanes = jnp.broadcast_to(wet_cells.reshape(-1, 1), (wet_cells.size, LANES)).astype(jnp.bfloat16)
    ocean_next, packed = run_grid(
        ocean_padded,
        ocean_cotangent,
        wet_lanes,
        packed,
        total_rows,
        ocean_kernel,
        ocean_gain,
        ocean_w_in,
        ocean_w_out,
    )
    return (atmos_next, ocean_next, *unpack(sum_over_devices(packed), widths))


def solution(mesh):
    return jax.shard_map(
        shards,
        mesh=mesh,
        in_specs=(
            P("lat", "lon", None),
            P("lat", "lon", None),
            P("lat", "lon", None),
            P("lat", "lon", None),
            P("lat", "lon"),
            P(),
            P("lat", "lon", None),
            P("lat", "lon"),
            P("lat", "lon", None, None, None),
            P("lat", "lon", None),
            P("lat", "lon"),
            P("lat", "lon", None, None, None),
            P(),
            P(),
            P(),
            P(),
            P(),
            P(),
            P(),
            P(),
            P(),
            P(),
            P(),
            P(),
        ),
        out_specs=(
            P("lat", "lon", None),
            P("lat", "lon", None),
            P(),
            P(),
            P(),
            P(),
            P(),
            P(),
            P(),
            P(),
        ),
        check_vma=False,
    )
```

```python
import functools

import jax
import jax.numpy as jnp
from jax import lax
from jax.experimental import pallas as pl
from jax.experimental.pallas import tpu as pltpu
from jax.sharding import PartitionSpec as P

NFIELD = 16
BCELLS = 128
PAIRS = 4
LANES = 128
SMALL = 64
EDGE = 4
MESH = pl.DeviceIdType.MESH
epsilon = 1e-06
TANH_SCALE = 0.7978845608028654
TANH_CUBIC = 0.044715


def dot(left, right, dims=((1,), (0,))):
    return lax.dot_general(left, right, (dims, ((), ())), preferred_element_type=jnp.float32)


def shift_phase(halo, shifted, rows, cols):
    inner, south, north, west, east = halo

    def one_tile(tile, line_of, live):
        left = west[tile].astype(jnp.float32)
        right = east[tile].astype(jnp.float32)
        for slot in live:
            wide = jnp.concatenate(
                [
                    left[4 * slot : 4 * slot + 4],
                    line_of(slot).astype(jnp.float32),
                    right[4 * slot : 4 * slot + 4],
                ],
                axis=0,
            )
            for tap_col in range(7):
                shifted[tap_col, 4 * tile + slot - 1] = wide[tap_col + 1 : tap_col + 1 + cols].astype(
                    jnp.bfloat16
                )

    def middle_tile(tile, carry):
        one_tile(tile, lambda slot: inner[4 * tile + slot - 4], range(4))
        return carry

    one_tile(0, lambda slot: south[slot - 1], range(1, 4))
    lax.fori_loop(1, rows // 4 + 1, middle_tile, 0)
    one_tile(rows // 4 + 1, lambda slot: north[slot], range(3))


def conv_phase(shifted, kernel_ref, banded, conv, rows, cols, channels):
    pair_step = 8
    across = lax.broadcasted_iota(jnp.int32, (LANES, LANES), 0)
    down = lax.broadcasted_iota(jnp.int32, (LANES, LANES), 1)
    eye = across == down
    for lane in range(0, channels, LANES):
        for tap_col in range(7):
            for step in range(4):
                for low in range(2):
                    for out in range(2):
                        tap_row = 2 * step + low - out
                        if 0 <= tap_row < 7:
                            tap = kernel_ref[pl.ds(tap_row * 7 + tap_col, 1), lane : lane + LANES]
                            block = jnp.where(eye, tap, 0.0).astype(jnp.bfloat16)
                        else:
                            block = jnp.zeros((LANES, LANES), jnp.bfloat16)
                        banded[
                            tap_col * 4 + step,
                            low * LANES : low * LANES + LANES,
                            out * LANES : out * LANES + LANES,
                        ] = block

        def one_chunk(index, carry):
            total = None
            for tap_col in range(7):
                for step in range(4):
                    window = shifted[
                        tap_col,
                        pl.ds(2 * (index * pair_step + step), 2 * pair_step),
                        :,
                        lane : lane + LANES,
                    ].reshape(pair_step, 2, cols, LANES)
                    left = jnp.concatenate(
                        [
                            window[:, 0].reshape(pair_step * cols, LANES),
                            window[:, 1].reshape(pair_step * cols, LANES),
                        ],
                        axis=1,
                    )
                    part = dot(left, banded[tap_col * 4 + step])
                    total = part if total is None else total + part
            for out in range(2):
                conv[pl.ds(index * pair_step, pair_step), out, :, lane : lane + LANES] = total[
                    :, out * LANES : out * LANES + LANES
                ].reshape(pair_step, cols, LANES)
            return carry

        lax.fori_loop(0, rows // 2 // pair_step, one_chunk, 0)


def grid_kernel(*refs, rows, cols, channels, hidden_width, masked):
    if masked:
        cot_ref, mask_ref, before_ref, kernel_ref, gain_ref, w_in_ref, w_out_ref = refs[5:12]
        rest, sem = refs[12:-1], refs[-1]
    else:
        cot_ref, kernel_ref, gain_ref, w_in_ref, w_out_ref = refs[5:10]
        rest = refs[10:]
    next_ref, packed_ref, w_in_sum, w_out_sum, small_sum, shifted, banded, conv, slope = rest
    at_row = 0
    if masked:
        at_row = before_ref.shape[0]
        carry_copy = pltpu.make_async_copy(before_ref, packed_ref.at[0:at_row, :], sem)
        carry_copy.start()
    row_step = 8
    cells = row_step * cols
    chunk = 256
    shift_phase(refs[:5], shifted, rows, cols)
    conv_phase(shifted, kernel_ref, banded, conv, rows, cols, channels)
    w_in_sum[...] = jnp.zeros_like(w_in_sum)
    w_out_sum[...] = jnp.zeros_like(w_out_sum)
    small_sum[...] = jnp.zeros_like(small_sum)
    gain = gain_ref[...]

    def one_block(index, gain_total):
        value = conv[pl.ds(index * (row_step // 2), row_step // 2)].reshape(cells, channels)
        centre = value - jnp.mean(value, axis=-1, keepdims=True)
        inv = lax.rsqrt(jnp.mean(centre * centre, axis=-1, keepdims=True) + epsilon)
        unit = centre * inv
        normed = (unit * gain).astype(jnp.bfloat16)
        where = pl.ds(index * cells, cells)
        upstream = cot_ref[where, :]
        if masked:
            keep = mask_ref[where, :]
            keep = jnp.concatenate([keep] * (channels // LANES), axis=1)
            upstream = upstream * keep
        normed_t = normed.T
        upstream_t = upstream.T
        update = None
        back = None
        for at in range(0, hidden_width, chunk):
            w_in = w_in_ref[:, at : at + chunk]
            w_out = w_out_ref[at : at + chunk, :]
            pre = dot(normed, w_in)
            grad_hidden = dot(upstream, w_out, ((1,), (1,)))
            square = pre * pre
            gate = 0.5 + 0.5 * jnp.tanh(pre * (TANH_SCALE + (TANH_SCALE * TANH_CUBIC) * square))
            active = pre * gate
            slope_part = 2 * TANH_SCALE + (6 * TANH_SCALE * TANH_CUBIC) * square
            grad_pre = (grad_hidden * (gate + active * (1.0 - gate) * slope_part)).astype(jnp.bfloat16)
            active = active.astype(jnp.bfloat16)
            part = dot(active, w_out)
            update = part if update is None else update + part
            part = dot(grad_pre, w_in, ((1,), (1,)))
            back = part if back is None else back + part
            for total, part in (
                (w_out_sum, dot(upstream_t, active)),
                (w_in_sum, dot(normed_t, grad_pre)),
            ):
                for lane in range(0, chunk, LANES):
                    total[(at + lane) // LANES] += part[:, lane : lane + LANES]
        inside = shifted[3, pl.ds(index * row_step + 3, row_step)].reshape(cells, channels)
        result = inside.astype(jnp.float32) + update
        if masked:
            result = result * keep.astype(jnp.float32)
        next_ref[where, :] = result.astype(jnp.bfloat16)
        gain_total = gain_total + jnp.sum((back * unit).reshape(cells // 8, 8, channels), axis=0)
        back = back * gain
        level = jnp.mean(back, axis=-1, keepdims=True)
        tilt = jnp.mean(back * unit, axis=-1, keepdims=True)
        slope[pl.ds(index * row_step, row_step)] = (
            (inv * (back - level - unit * tilt)).astype(jnp.bfloat16).reshape(row_step, cols, channels)
        )
        return gain_total

    gain_total = lax.fori_loop(0, rows // row_step, one_block, jnp.zeros((8, channels), jnp.float32))
    small_sum[49:50, :] = jnp.sum(gain_total, axis=0, keepdims=True)
    for lane in range(0, channels, LANES):
        for tap_row in range(7):

            def one_row(row, totals):
                grad = slope[row, :, lane : lane + LANES]
                sums = []
                for tap_col in range(7):
                    product = grad * shifted[tap_col, row + tap_row, :, lane : lane + LANES]
                    pieces = [product[at : at + 16] for at in range(0, cols, 16)]
                    while len(pieces) > 1:
                        pieces = [a + b for a, b in zip(pieces[::2], pieces[1::2])]
                    wide = pieces[0].astype(jnp.float32)
                    sums.append(totals[tap_col] + wide[:8] + wide[8:])
                return tuple(sums)

            totals = lax.fori_loop(
                0, rows, one_row, tuple(jnp.zeros((8, LANES), jnp.float32) for _ in range(7)), unroll=4
            )
            for tap_col in range(7):
                small_sum[pl.ds(tap_row * 7 + tap_col, 1), lane : lane + LANES] = jnp.sum(
                    totals[tap_col], axis=0, keepdims=True
                )
    for total in (w_in_sum, w_out_sum):
        for block in range(hidden_width // LANES):
            packed_ref[at_row : at_row + channels, :] = total[block].astype(jnp.bfloat16)
            at_row += channels
    for lane in range(0, channels, LANES):
        packed_ref[at_row : at_row + SMALL, :] = small_sum[:, lane : lane + LANES].astype(jnp.bfloat16)
        at_row += SMALL
    if at_row < packed_ref.shape[0]:
        spare = packed_ref.shape[0] - at_row
        packed_ref[at_row:, :] = jnp.zeros((spare, LANES), jnp.bfloat16)
    if masked:
        carry_copy.wait()


def packed_rows(channels, hidden_width):
    return 2 * (hidden_width // LANES) * channels + channels // LANES * SMALL


def run_grid(halo, cotangent, mask, before, rows_out, kernel, gain, w_in, w_out):
    rows, cols, channels = cotangent.shape
    hidden_width = w_in.shape[1]
    cells = rows * cols
    masked = mask is not None
    args = [*halo, cotangent.reshape(cells, channels)]
    vmem = pl.BlockSpec(memory_space=pltpu.VMEM)
    specs = [vmem] * 6
    if masked:
        args += [mask, before]
        specs += [vmem, pl.BlockSpec(memory_space=pl.ANY)]
    args += [kernel.astype(jnp.float32), gain.astype(jnp.float32).reshape(1, channels), w_in, w_out]
    specs += [vmem] * 4
    result, packed = pl.pallas_call(
        functools.partial(
            grid_kernel,
            rows=rows,
            cols=cols,
            channels=channels,
            hidden_width=hidden_width,
            masked=masked,
        ),
        out_shape=(
            jax.ShapeDtypeStruct((cells, channels), jnp.bfloat16),
            jax.ShapeDtypeStruct((rows_out, LANES), jnp.bfloat16),
        ),
        in_specs=specs,
        out_specs=(vmem, vmem),
        scratch_shapes=[
            pltpu.VMEM((hidden_width // LANES, channels, LANES), jnp.float32),
            pltpu.VMEM((hidden_width // LANES, channels, LANES), jnp.float32),
            pltpu.VMEM((SMALL, channels), jnp.float32),
            pltpu.VMEM((7, rows + 6, cols, channels), jnp.bfloat16),
            pltpu.VMEM((28, 2 * LANES, 2 * LANES), jnp.bfloat16),
            pltpu.VMEM((rows // 2, 2, cols, channels), jnp.float32),
            pltpu.VMEM((rows, cols, channels), jnp.bfloat16),
        ]
        + ([pltpu.SemaphoreType.DMA] if masked else []),
        compiler_params=pltpu.CompilerParams(vmem_limit_bytes=60 * 1024 * 1024),
    )(*args)
    return result.reshape(rows, cols, channels), packed


def unpack_kernel(widths, packed_ref, *outs):
    at = 0
    for number, (channels, hidden_width) in enumerate(widths):
        kernel_out, gain_out, w_in_out, w_out_out = outs[4 * number : 4 * number + 4]
        for block in range(hidden_width // LANES):
            w_in_out[:, block * LANES : block * LANES + LANES] = packed_ref[at : at + channels, :].astype(
                jnp.float32
            )
            at += channels
        for block in range(hidden_width // LANES):
            w_out_out[block * LANES : block * LANES + LANES, :] = (
                packed_ref[at : at + channels, :].astype(jnp.float32).T
            )
            at += channels
        for lane in range(0, channels, LANES):
            small = packed_ref[at : at + SMALL, :].astype(jnp.float32)
            kernel_out[:, lane : lane + LANES] = small[:49]
            gain_out[:, lane : lane + LANES] = small[49:50]
            at += SMALL


def unpack(packed, widths):
    shapes = []
    for channels, hidden_width in widths:
        shapes += [(49, channels), (1, channels), (channels, hidden_width), (hidden_width, channels)]
    vmem = pl.BlockSpec(memory_space=pltpu.VMEM)
    outs = pl.pallas_call(
        functools.partial(unpack_kernel, widths),
        out_shape=tuple(jax.ShapeDtypeStruct(shape, jnp.float32) for shape in shapes),
        in_specs=[vmem],
        out_specs=(vmem,) * len(shapes),
        compiler_params=pltpu.CompilerParams(vmem_limit_bytes=40 * 1024 * 1024),
    )(packed)
    return [out.reshape(-1) if out.shape[0] == 1 else out for out in outs]


def aligned(index):
    return pl.multiple_of(index, 16)


def greet(partners):
    barrier = pltpu.get_barrier_semaphore()
    for partner in partners:
        pl.semaphore_signal(barrier, inc=1, device_id=partner, device_id_type=MESH)
    pl.semaphore_wait(barrier, len(partners))


def sum_plan(lon_count):
    spans = []
    span = 2
    while span < lon_count:
        spans.append(span)
        span *= 2
    return (spans, spans[::-1])


def sum_kernel(length, lat_count, lon_count, share_ref, full_ref, *scratch):
    plan = sum_plan(lon_count)
    steps = len(plan[0])
    half, quarter = length // 2, length // 4
    first, lat_send, lat_recv, comb = scratch[:4]
    sends = [scratch[4 + part * steps : 4 + part * steps + steps] for part in range(2)]
    recvs = [scratch[4 + (2 + part) * steps : 4 + (2 + part) * steps + steps] for part in range(2)]
    totals = [scratch[4 + (4 + part) * steps : 4 + (4 + part) * steps + steps] for part in range(2)]
    send_sem, recv_sem = scratch[-2:]
    lat, lon = lax.axis_index("lat"), lax.axis_index("lon")
    core = lon % 2

    def flipped(span):
        bit = (lon // span) % 2
        return (lat, lon + span - 2 * span * bit), bit

    peers = [((lat + step) % lat_count, lon) for step in range(1, lat_count)]
    greet([flipped(1)[0]] + [flipped(span)[0] for span in plan[0]] + peers)
    count = [0]

    def push(source, target, device):
        number = count[0]
        count[0] += 1
        copy = pltpu.make_async_remote_copy(
            src_ref=source,
            dst_ref=target,
            send_sem=send_sem.at[number],
            recv_sem=recv_sem.at[number],
            device_id=device,
            device_id_type=MESH,
        )
        copy.start()
        return copy

    pending = []
    opening = []
    for part in range(2):
        opening.append(
            push(
                share_ref.at[pl.ds(aligned((1 - core) * half + part * quarter), quarter), :],
                first.at[part],
                flipped(1)[0],
            )
        )
    active = [None, None]
    for part in range(2):
        opening[part].wait_recv()
        pending.append(opening[part])
        device, bit = flipped(plan[part][0])
        size = quarter // 2
        own = core * half + part * quarter

        def summed(start):
            return share_ref[pl.ds(aligned(own + start), size), :].astype(jnp.float32) + first[
                part, pl.ds(aligned(start), size), :
            ].astype(jnp.float32)

        sends[part][0][...] = summed((1 - bit) * size).astype(jnp.bfloat16)
        active[part] = push(sends[part][0], recvs[part][0], device)
        totals[part][0][...] = summed(bit * size)
    size = quarter // 2
    for step in range(steps):
        for part in range(2):
            active[part].wait_recv()
            pending.append(active[part])
            recv, total = recvs[part][step], totals[part][step]
            if step + 1 == steps:
                comb[part * size : part * size + size, :] = total[...] + recv[...].astype(jnp.float32)
                continue
            device, bit = flipped(plan[part][step + 1])
            rest = size // 2

            def joined(start):
                where = pl.ds(aligned(start), rest)
                return total[where, :] + recv[where, :].astype(jnp.float32)

            sends[part][step + 1][...] = joined((1 - bit) * rest).astype(jnp.bfloat16)
            active[part] = push(sends[part][step + 1], recvs[part][step + 1], device)
            totals[part][step + 1][...] = joined(bit * rest)
        if step + 1 < steps:
            size //= 2
    bases = []
    for part in range(2):
        base = core * half + part * quarter
        extent = quarter
        levels = []
        for span in plan[part]:
            extent //= 2
            base = base + ((lon // span) % 2) * extent
            levels.append((base, extent, span))
        bases.append(levels)
    chunk = 2 * size // lat_count
    lat_send[...] = comb[...].astype(jnp.bfloat16)
    arriving = []
    for step in range(1, lat_count):
        peer = (lat + step) % lat_count
        arriving.append(
            push(
                lat_send.at[pl.ds(aligned(peer * chunk), chunk), :],
                lat_recv.at[step - 1],
                (peer, lon),
            )
        )
    total = comb[pl.ds(aligned(lat * chunk), chunk), :]
    for step, copy in enumerate(arriving):
        copy.wait_recv()
        pending.append(copy)
        total = total + lat_recv[step].astype(jnp.float32)
    upper = (2 * lat) // lat_count
    low_base, high_base = bases[0][-1][0], bases[1][-1][0]
    place = low_base + upper * (high_base - low_base) + (lat - upper * (lat_count // 2)) * chunk
    mine = pl.ds(aligned(place), chunk)
    full_ref[mine, :] = total.astype(jnp.bfloat16)
    arriving = [push(full_ref.at[mine, :], full_ref.at[mine, :], peer) for peer in peers]
    for copy in arriving:
        copy.wait_recv()
        pending.append(copy)
    for step in reversed(range(steps)):
        arriving = []
        for part in range(2):
            base, extent, span = bases[part][step]
            region = full_ref.at[pl.ds(aligned(base), extent), :]
            arriving.append(push(region, region, flipped(span)[0]))
        for copy in arriving:
            copy.wait_recv()
            pending.append(copy)
    arriving = []
    for part in range(2):
        region = full_ref.at[pl.ds(aligned(core * half + part * quarter), quarter), :]
        arriving.append(push(region, region, flipped(1)[0]))
    for copy in arriving:
        copy.wait_recv()
        pending.append(copy)
    for copy in pending:
        copy.wait_send()


def sum_over_devices(share):
    lat_count, lon_count = lax.axis_size("lat"), lax.axis_size("lon")
    length = share.shape[0]
    plan = sum_plan(lon_count)
    steps = len(plan[0])
    sizes = [length // 4 // 2 ** (step + 1) for step in range(steps)]
    chunk = 2 * sizes[-1] // lat_count
    copies = 2 + 2 * steps + (lat_count - 1) * 2 + 2 * steps + 2
    narrow = [pltpu.VMEM((size, LANES), jnp.bfloat16) for size in sizes]
    wide = [pltpu.VMEM((size, LANES), jnp.float32) for size in sizes]
    vmem = pl.BlockSpec(memory_space=pltpu.VMEM)
    return pl.pallas_call(
        functools.partial(sum_kernel, length, lat_count, lon_count),
        out_shape=jax.ShapeDtypeStruct((length, LANES), jnp.bfloat16),
        in_specs=[vmem],
        out_specs=vmem,
        scratch_shapes=[
            pltpu.VMEM((2, length // 4, LANES), jnp.bfloat16),
            pltpu.VMEM((2 * sizes[-1], LANES), jnp.bfloat16),
            pltpu.VMEM((lat_count - 1, chunk, LANES), jnp.bfloat16),
            pltpu.VMEM((2 * sizes[-1], LANES), jnp.float32),
            *narrow,
            *narrow,
            *narrow,
            *narrow,
            *wide,
            *wide,
            pltpu.SemaphoreType.DMA((copies,)),
            pltpu.SemaphoreType.DMA((copies,)),
        ],
        compiler_params=pltpu.CompilerParams(
            collective_id=2, has_side_effects=True, vmem_limit_bytes=40 * 1024 * 1024
        ),
    )(share)


def to_tiles(pieces):
    return jnp.concatenate([piece.astype(jnp.float32) for piece in pieces], axis=0).astype(jnp.bfloat16)


def front_kernel(lat_count, lon_count, *refs):
    (
        atmos_ref,
        ocean_ref,
        land_ref,
        fold_ref,
        ocean_pairs,
        ocean_counts,
        ocean_weights_hbm,
        atmos_pairs,
        atmos_counts,
        atmos_weights_hbm,
        flux_map,
        surface_map,
        flux_inject,
        surface_inject,
    ) = refs[:14]
    atmos_out, ocean_out = refs[14:19], refs[19:24]
    (
        near_atmos,
        near_ocean,
        ocean_weights,
        atmos_weights,
        atmos_first,
        atmos_last,
        ocean_first,
        ocean_last,
        top_rows,
        circle_rows,
        send_sem,
        recv_sem,
        local_sem,
    ) = refs[24:]
    lat, lon = lax.axis_index("lat"), lax.axis_index("lon")
    east, west = (lon + 1) % lon_count, (lon + lon_count - 1) % lon_count
    has_south, has_north = lat > 0, lat < lat_count - 1
    beside = {-1: west, 0: lon, 1: east}
    cols = atmos_ref.shape[1]

    weight_copies = [
        pltpu.make_async_copy(ocean_weights_hbm, ocean_weights, local_sem.at[0]),
        pltpu.make_async_copy(atmos_weights_hbm, atmos_weights, local_sem.at[1]),
    ]
    for copy in weight_copies:
        copy.start()

    barrier = pltpu.get_barrier_semaphore()
    for step in range(1, lon_count):
        pl.semaphore_signal(
            barrier, inc=1, device_id=(lat, (lon + step) % lon_count), device_id_type=MESH
        )
    for band, there in ((-1, has_south), (1, has_north)):

        @pl.when(there)
        def _():
            for sector in (-1, 0, 1):
                pl.semaphore_signal(
                    barrier, inc=1, device_id=(lat + band, beside[sector]), device_id_type=MESH
                )

    pl.semaphore_wait(
        barrier, lon_count - 1 + 3 * has_south.astype(jnp.int32) + 3 * has_north.astype(jnp.int32)
    )

    numbers = {}

    def remote(name, source, target, device):
        number = numbers.setdefault(name, len(numbers))
        return pltpu.make_async_remote_copy(
            src_ref=source,
            dst_ref=target,
            send_sem=send_sem.at[number],
            recv_sem=recv_sem.at[number],
            device_id=device,
            device_id_type=MESH,
        )

    def each_neighbour(action):
        for band, there in ((-1, has_south), (0, None), (1, has_north)):
            for sector in (-1, 0, 1):
                if band == 0 and sector == 0:
                    continue
                if there is None:
                    action(band, sector)
                else:
                    pl.when(there)(functools.partial(action, band, sector))

    def field_copy(name, near, band, sector, waiting):
        own = near.at[4]
        return remote(
            (name, band, sector),
            own,
            near.at[(1 - band) * 3 + 1 - sector],
            (lat + band, beside[sector]),
        )

    def send_fields(name, near):
        each_neighbour(lambda band, sector: field_copy(name, near, band, sector, False).start())

    def await_fields(name, near):
        each_neighbour(
            lambda band, sector: remote(
                (name, -band, -sector),
                near.at[4],
                near.at[(1 + band) * 3 + 1 + sector],
                (lat + band, beside[sector]),
            ).wait_recv()
        )

    def fields(source, projection, near, masked):
        channels = source.shape[2]
        turned = projection[...].astype(jnp.float32).T.astype(jnp.bfloat16)

        def one_block(block, carry):
            cells = source[pl.ds(2 * block, 2)].reshape(BCELLS, channels)
            values = dot(turned, cells, ((1,), (1,)))
            if masked:
                keep = jnp.concatenate(
                    [land_ref[pl.ds(2 * block, 1), :], land_ref[pl.ds(2 * block + 1, 1), :]], axis=1
                )
                values = values * keep.astype(jnp.float32)
            near[4, block] = values.astype(jnp.bfloat16)
            return carry

        lax.fori_loop(0, source.shape[0] // 2, one_block, 0, unroll=4)

    fields(atmos_ref, flux_map, near_atmos, False)
    send_fields("atmos_fields", near_atmos)
    fields(ocean_ref, surface_map, near_ocean, True)
    send_fields("ocean_fields", near_ocean)

    def remap(near, pairs, counts, weights, state, projection, target):
        source_count = near.shape[1]
        channels = state.shape[2]
        inject = projection[...]

        def one_block(block, carry):
            count = counts[block, 0]
            picked = []
            for entry in range(PAIRS):
                number = pairs[block, 0, entry]
                owner = number // source_count
                local = number - owner * source_count
                band = owner // lon_count
                sector = owner - band * lon_count - lon + 1 + lon_count
                sector = lax.rem(sector, lon_count)
                slot = jnp.clip((band - lat + 1) * 3 + sector, 0, 8)
                value = near[slot, local]
                if entry:
                    value = jnp.where(entry < count, value, jnp.zeros_like(value))
                picked.append(value)
            left = jnp.concatenate(picked, axis=1)
            mixed = dot(left, weights[block, 0].reshape(PAIRS * BCELLS, BCELLS))
            mixed = mixed.astype(jnp.bfloat16).astype(jnp.float32).T.astype(jnp.bfloat16)
            added = dot(mixed, inject)
            cells = state[pl.ds(2 * block, 2)].reshape(BCELLS, channels).astype(jnp.float32)
            target[pl.ds(2 * block, 2)] = (
                (cells + added).astype(jnp.bfloat16).reshape(2, state.shape[1], channels)
            )
            return carry

        lax.fori_loop(0, state.shape[0] // 2, one_block, 0, unroll=2)

    def edges(target, first, last):
        channels = target.shape[2]

        def one_tile(tile, carry):
            rows = target[pl.ds(4 * tile, 4)].astype(jnp.float32)
            first[tile] = to_tiles([rows[row, :EDGE] for row in range(4)])
            last[tile] = to_tiles([rows[row, cols - EDGE :] for row in range(4)])
            return carry

        lax.fori_loop(0, target.shape[0] // 4, one_tile, 0, unroll=2)

    def halo_copy(name, out, first, last, band, sector, to_neighbour):
        target, south, north, west_edge, east_edge = out
        rows = target.shape[0]
        tiles = rows // 4
        if sector == 0:
            source = target.at[rows - 3 : rows] if band == 1 else target.at[0:3]
            place = south if band == 1 else north
        else:
            edge = last if sector == 1 else first
            place = west_edge if sector == 1 else east_edge
            if band == 0:
                source, place = edge, place.at[1 : tiles + 1]
            elif band == 1:
                source, place = edge.at[tiles - 1], place.at[0]
            else:
                source, place = edge.at[0], place.at[tiles + 1]
        flip = 1 if to_neighbour else -1
        return remote(
            (name, band, sector), source, place, (lat + flip * band, beside[flip * sector])
        )

    def send_halo(name, out, first, last):
        each_neighbour(
            lambda band, sector: halo_copy(name, out, first, last, band, sector, True).start()
        )

    def await_halo(name, out, first, last):
        each_neighbour(
            lambda band, sector: halo_copy(name, out, first, last, -band, -sector, False).wait_recv()
        )

    def blank(out, at_north):
        target, south, north, west_edge, east_edge = out
        rim = north if at_north else south
        tile = target.shape[0] // 4 + 1 if at_north else 0
        rim[...] = jnp.zeros_like(rim)
        west_edge[tile] = jnp.zeros(west_edge.shape[1:], jnp.bfloat16)
        east_edge[tile] = jnp.zeros(east_edge.shape[1:], jnp.bfloat16)

    pl.when(jnp.logical_not(has_south))(lambda: blank(atmos_out, False))
    pl.when(jnp.logical_not(has_south))(lambda: blank(ocean_out, False))
    pl.when(jnp.logical_not(has_north))(lambda: blank(atmos_out, True))

    await_fields("atmos_fields", near_atmos)
    weight_copies[0].wait()
    remap(near_atmos, ocean_pairs, ocean_counts, ocean_weights, ocean_ref, flux_inject, ocean_out[0])
    edges(ocean_out[0], ocean_first, ocean_last)
    send_halo("ocean_halo", ocean_out, ocean_first, ocean_last)
    is_top = jnp.logical_not(has_north)
    top_at = ocean_out[0].shape[0] - 3

    def fold_copy(step, to_peer):
        flip = step if to_peer else lon_count - step
        return remote(
            ("fold", step),
            top_rows,
            circle_rows.at[:, pl.ds(pl.multiple_of(((lon if to_peer else (lon + flip) % lon_count)) * cols, 16), cols), :],
            (lat, (lon + flip) % lon_count),
        )

    @pl.when(is_top)
    def _():
        for row in range(3):
            top_rows[row] = ocean_out[0][top_at + 2 - row]
        for step in range(1, lon_count):
            fold_copy(step, True).start()
        own = pl.ds(pl.multiple_of(lon * cols, 16), cols)
        for row in range(3):
            circle_rows[row, own, :] = top_rows[row]

    await_fields("ocean_fields", near_ocean)
    weight_copies[1].wait()
    remap(near_ocean, atmos_pairs, atmos_counts, atmos_weights, atmos_ref, surface_inject, atmos_out[0])
    edges(atmos_out[0], atmos_first, atmos_last)
    send_halo("atmos_halo", atmos_out, atmos_first, atmos_last)

    @pl.when(is_top)
    def _():
        for step in range(1, lon_count):
            fold_copy(step, False).wait_recv()
        length = lon_count * cols
        partner = fold_ref[...]

        def chosen(first, count, repeat):
            place = lax.broadcasted_iota(jnp.int32, (count, length), 0)
            if repeat is not None:
                wanted = lax.rem(lon * cols + first + length + lax.rem(place, EDGE), length)
                live = place // EDGE == repeat
                return jnp.where(live & (partner == wanted), 1.0, 0.0).astype(jnp.bfloat16)
            return jnp.where(partner == lon * cols + place, 1.0, 0.0).astype(jnp.bfloat16)

        _, _, north, west_edge, east_edge = ocean_out
        tile = ocean_out[0].shape[0] // 4 + 1
        middle = chosen(0, cols, None)
        sides = [None, None]
        for row in range(3):
            line = circle_rows[row]
            north[row] = dot(middle, line).astype(jnp.bfloat16)
            for side, first in enumerate((-EDGE, cols)):
                part = dot(chosen(first, 16, row), line)
                sides[side] = part if row == 0 else sides[side] + part
        west_edge[tile] = sides[0].astype(jnp.bfloat16)
        east_edge[tile] = sides[1].astype(jnp.bfloat16)

    await_halo("ocean_halo", ocean_out, ocean_first, ocean_last)
    await_halo("atmos_halo", atmos_out, atmos_first, atmos_last)
    for name, near in (("atmos_fields", near_atmos), ("ocean_fields", near_ocean)):
        each_neighbour(
            lambda band, sector: field_copy(name, near, band, sector, False).wait_send()
        )
    for name, out, first, last in (
        ("ocean_halo", ocean_out, ocean_first, ocean_last),
        ("atmos_halo", atmos_out, atmos_first, atmos_last),
    ):
        each_neighbour(
            lambda band, sector: halo_copy(name, out, first, last, band, sector, True).wait_send()
        )

    @pl.when(is_top)
    def _():
        for step in range(1, lon_count):
            fold_copy(step, True).wait_send()


def front(
    atmos_state,
    ocean_state,
    land_sea,
    fold_partner,
    ocean_pairs,
    ocean_counts,
    ocean_weights,
    atmos_pairs,
    atmos_counts,
    atmos_weights,
    flux_map,
    surface_map,
    flux_inject,
    surface_inject,
):
    lat_count, lon_count = lax.axis_size("lat"), lax.axis_size("lon")
    vmem = pl.BlockSpec(memory_space=pltpu.VMEM)
    smem = pl.BlockSpec(memory_space=pltpu.SMEM)
    anywhere = pl.BlockSpec(memory_space=pl.ANY)

    def out_shapes(state):
        rows, cols, channels = state.shape
        return [
            jax.ShapeDtypeStruct(shape, jnp.bfloat16)
            for shape in (
                (rows, cols, channels),
                (3, cols, channels),
                (3, cols, channels),
                (rows // 4 + 2, 16, channels),
                (rows // 4 + 2, 16, channels),
            )
        ]

    def edge_scratch(state):
        return pltpu.VMEM((state.shape[0] // 4, 16, state.shape[2]), jnp.bfloat16)

    copies = 32 + lon_count - 1
    cols = atmos_state.shape[1]
    ocean_channels = ocean_state.shape[2]
    outs = pl.pallas_call(
        functools.partial(front_kernel, lat_count, lon_count),
        out_shape=tuple(out_shapes(atmos_state) + out_shapes(ocean_state)),
        in_specs=[vmem, vmem, vmem, vmem, smem, smem, anywhere, smem, smem, anywhere] + [vmem] * 4,
        out_specs=(vmem,) * 10,
        scratch_shapes=[
            pltpu.VMEM((9, atmos_state.shape[0] // 2, NFIELD, BCELLS), jnp.bfloat16),
            pltpu.VMEM((9, ocean_state.shape[0] // 2, NFIELD, BCELLS), jnp.bfloat16),
            pltpu.VMEM(ocean_weights.shape, jnp.bfloat16),
            pltpu.VMEM(atmos_weights.shape, jnp.bfloat16),
            edge_scratch(atmos_state),
            edge_scratch(atmos_state),
            edge_scratch(ocean_state),
            edge_scratch(ocean_state),
            pltpu.VMEM((3, cols, ocean_channels), jnp.bfloat16),
            pltpu.VMEM((3, lon_count * cols, ocean_channels), jnp.bfloat16),
            pltpu.SemaphoreType.DMA((copies,)),
            pltpu.SemaphoreType.DMA((copies,)),
            pltpu.SemaphoreType.DMA((2,)),
        ],
        compiler_params=pltpu.CompilerParams(
            collective_id=1, has_side_effects=True, vmem_limit_bytes=48 * 1024 * 1024
        ),
    )(
        atmos_state,
        ocean_state,
        land_sea,
        fold_partner.reshape(1, -1),
        ocean_pairs,
        ocean_counts,
        ocean_weights,
        atmos_pairs,
        atmos_counts,
        atmos_weights,
        flux_map,
        surface_map,
        flux_inject,
        surface_inject,
    )
    return outs[:5], outs[5:]


def shards(
    atmos_state,
    ocean_state,
    atmos_cotangent,
    ocean_cotangent,
    land_sea,
    fold_partner,
    ocean_pairs,
    ocean_counts,
    ocean_weights,
    atmos_pairs,
    atmos_counts,
    atmos_weights,
    flux_map,
    surface_map,
    flux_inject,
    surface_inject,
    atmos_kernel,
    atmos_gain,
    atmos_w_in,
    atmos_w_out,
    ocean_kernel,
    ocean_gain,
    ocean_w_in,
    ocean_w_out,
):
    atmos_halo, ocean_halo = front(
        atmos_state,
        ocean_state,
        land_sea,
        fold_partner,
        ocean_pairs,
        ocean_counts,
        ocean_weights,
        atmos_pairs,
        atmos_counts,
        atmos_weights,
        flux_map,
        surface_map,
        flux_inject,
        surface_inject,
    )
    widths = tuple(w_in.shape for w_in in (atmos_w_in, ocean_w_in))
    atmos_rows = packed_rows(*widths[0])
    total_rows = atmos_rows + packed_rows(*widths[1])
    total_rows += -total_rows % (16 * lax.axis_size("lat") * lax.axis_size("lon"))
    atmos_next, packed = run_grid(
        atmos_halo,
        atmos_cotangent,
        None,
        None,
        atmos_rows,
        atmos_kernel,
        atmos_gain,
        atmos_w_in,
        atmos_w_out,
    )
    wet_cells = land_sea.astype(jnp.float32)
    wet_lanes = jnp.broadcast_to(wet_cells.reshape(-1, 1), (wet_cells.size, LANES)).astype(jnp.bfloat16)
    ocean_next, packed = run_grid(
        ocean_halo,
        ocean_cotangent,
        wet_lanes,
        packed,
        total_rows,
        ocean_kernel,
        ocean_gain,
        ocean_w_in,
        ocean_w_out,
    )
    return (atmos_next, ocean_next, *unpack(sum_over_devices(packed), widths))


def solution(mesh):
    return jax.shard_map(
        shards,
        mesh=mesh,
        in_specs=(
            P("lat", "lon", None),
            P("lat", "lon", None),
            P("lat", "lon", None),
            P("lat", "lon", None),
            P("lat", "lon"),
            P(),
            P("lat", "lon", None),
            P("lat", "lon"),
            P("lat", "lon", None, None, None),
            P("lat", "lon", None),
            P("lat", "lon"),
            P("lat", "lon", None, None, None),
            P(),
            P(),
            P(),
            P(),
            P(),
            P(),
            P(),
            P(),
            P(),
            P(),
            P(),
            P(),
        ),
        out_specs=(
            P("lat", "lon", None),
            P("lat", "lon", None),
            P(),
            P(),
            P(),
            P(),
            P(),
            P(),
            P(),
            P(),
        ),
        check_vma=False,
    )
```

```python
import functools

import jax
import jax.numpy as jnp
from jax import lax
from jax.experimental import pallas as pl
from jax.experimental.pallas import tpu as pltpu
from jax.sharding import PartitionSpec as P

NFIELD = 16
BCELLS = 128
PAIRS = 4
LANES = 128
SMALL = 64
EDGE = 4
MESH = pl.DeviceIdType.MESH
epsilon = 1e-06
TANH_SCALE = 0.7978845608028654
TANH_CUBIC = 0.044715


def dot(left, right, dims=((1,), (0,))):
    return lax.dot_general(left, right, (dims, ((), ())), preferred_element_type=jnp.float32)


def shift_phase(halo, shifted, rows, cols):
    inner, south, north, west, east = halo

    def one_tile(tile, line_of, live):
        left = west[tile].astype(jnp.float32)
        right = east[tile].astype(jnp.float32)
        for slot in live:
            wide = jnp.concatenate(
                [
                    left[4 * slot : 4 * slot + 4],
                    line_of(slot).astype(jnp.float32),
                    right[4 * slot : 4 * slot + 4],
                ],
                axis=0,
            )
            for tap_col in range(7):
                shifted[tap_col, 4 * tile + slot - 1] = wide[tap_col + 1 : tap_col + 1 + cols].astype(
                    jnp.bfloat16
                )

    def middle_tile(tile, carry):
        one_tile(tile, lambda slot: inner[4 * tile + slot - 4], range(4))
        return carry

    one_tile(0, lambda slot: south[slot - 1], range(1, 4))
    lax.fori_loop(1, rows // 4 + 1, middle_tile, 0)
    one_tile(rows // 4 + 1, lambda slot: north[slot], range(3))


def conv_phase(shifted, kernel_ref, banded, conv, rows, cols, channels):
    pair_step = 8
    across = lax.broadcasted_iota(jnp.int32, (LANES, LANES), 0)
    down = lax.broadcasted_iota(jnp.int32, (LANES, LANES), 1)
    eye = across == down
    for lane in range(0, channels, LANES):
        for tap_col in range(7):
            for step in range(4):
                for low in range(2):
                    for out in range(2):
                        tap_row = 2 * step + low - out
                        if 0 <= tap_row < 7:
                            tap = kernel_ref[pl.ds(tap_row * 7 + tap_col, 1), lane : lane + LANES]
                            block = jnp.where(eye, tap, 0.0).astype(jnp.bfloat16)
                        else:
                            block = jnp.zeros((LANES, LANES), jnp.bfloat16)
                        banded[
                            tap_col * 4 + step,
                            low * LANES : low * LANES + LANES,
                            out * LANES : out * LANES + LANES,
                        ] = block

        def one_chunk(index, carry):
            total = None
            for tap_col in range(7):
                for step in range(4):
                    window = shifted[
                        tap_col,
                        pl.ds(2 * (index * pair_step + step), 2 * pair_step),
                        :,
                        lane : lane + LANES,
                    ].reshape(pair_step, 2, cols, LANES)
                    left = jnp.concatenate(
                        [
                            window[:, 0].reshape(pair_step * cols, LANES),
                            window[:, 1].reshape(pair_step * cols, LANES),
                        ],
                        axis=1,
                    )
                    part = dot(left, banded[tap_col * 4 + step])
                    total = part if total is None else total + part
            for out in range(2):
                conv[pl.ds(index * pair_step, pair_step), out, :, lane : lane + LANES] = total[
                    :, out * LANES : out * LANES + LANES
                ].reshape(pair_step, cols, LANES)
            return carry

        lax.fori_loop(0, rows // 2 // pair_step, one_chunk, 0)
        yield


def grid_work(
    halo, cot_ref, land_ref, kernel_ref, gain_ref, w_in_ref, w_out_ref, next_ref, packed_ref, scratch
):
    taps, w_in_sum, w_out_sum, small_sum, shifted, banded, conv, slope = scratch
    rows, cols, channels = halo[0].shape
    hidden_width = w_in_ref.shape[1]
    row_step = 8
    cells = row_step * cols
    chunk = 256
    shift_phase(halo, shifted, rows, cols)
    yield
    taps[...] = kernel_ref[...].astype(jnp.float32)
    yield from conv_phase(shifted, taps, banded, conv, rows, cols, channels)
    w_in_sum[...] = jnp.zeros_like(w_in_sum)
    w_out_sum[...] = jnp.zeros_like(w_out_sum)
    small_sum[...] = jnp.zeros_like(small_sum)
    gain = gain_ref[...].astype(jnp.float32)

    def one_block(index, gain_total):
        value = conv[pl.ds(index * (row_step // 2), row_step // 2)].reshape(cells, channels)
        centre = value - jnp.mean(value, axis=-1, keepdims=True)
        inv = lax.rsqrt(jnp.mean(centre * centre, axis=-1, keepdims=True) + epsilon)
        unit = centre * inv
        normed = (unit * gain).astype(jnp.bfloat16)
        where = pl.ds(index * cells, cells)
        upstream = cot_ref[where, :]
        if land_ref is not None:
            turned = land_ref[pl.ds(pl.multiple_of(index * row_step, 8), row_step), :].astype(jnp.float32).T
            keep = jnp.concatenate(
                [jnp.broadcast_to(turned[:, row : row + 1], (cols, channels)) for row in range(row_step)],
                axis=0,
            )
            upstream = upstream * keep.astype(jnp.bfloat16)
        normed_t = normed.T
        upstream_t = upstream.T
        update = None
        back = None
        for at in range(0, hidden_width, chunk):
            w_in = w_in_ref[:, at : at + chunk]
            w_out = w_out_ref[at : at + chunk, :]
            pre = dot(normed, w_in)
            grad_hidden = dot(upstream, w_out, ((1,), (1,)))
            square = pre * pre
            gate = 0.5 + 0.5 * jnp.tanh(pre * (TANH_SCALE + (TANH_SCALE * TANH_CUBIC) * square))
            active = pre * gate
            slope_part = 2 * TANH_SCALE + (6 * TANH_SCALE * TANH_CUBIC) * square
            grad_pre = (grad_hidden * (gate + active * (1.0 - gate) * slope_part)).astype(jnp.bfloat16)
            active = active.astype(jnp.bfloat16)
            part = dot(active, w_out)
            update = part if update is None else update + part
            part = dot(grad_pre, w_in, ((1,), (1,)))
            back = part if back is None else back + part
            for total, part in (
                (w_out_sum, dot(upstream_t, active)),
                (w_in_sum, dot(normed_t, grad_pre)),
            ):
                for lane in range(0, chunk, LANES):
                    total[(at + lane) // LANES] += part[:, lane : lane + LANES]
        inside = shifted[3, pl.ds(index * row_step + 3, row_step)].reshape(cells, channels)
        result = inside.astype(jnp.float32) + update
        if land_ref is not None:
            result = result * keep
        next_ref[where, :] = result.astype(jnp.bfloat16)
        gain_total = gain_total + jnp.sum((back * unit).reshape(cells // 8, 8, channels), axis=0)
        back = back * gain
        level = jnp.mean(back, axis=-1, keepdims=True)
        tilt = jnp.mean(back * unit, axis=-1, keepdims=True)
        slope[pl.ds(index * row_step, row_step)] = (
            (inv * (back - level - unit * tilt)).astype(jnp.bfloat16).reshape(row_step, cols, channels)
        )
        return gain_total

    blocks = rows // row_step
    gain_total = jnp.zeros((8, channels), jnp.float32)
    for start in range(0, blocks, 2):
        gain_total = lax.fori_loop(start, min(start + 2, blocks), one_block, gain_total)
        yield
    small_sum[49:50, :] = jnp.sum(gain_total, axis=0, keepdims=True)
    for lane in range(0, channels, LANES):
        for tap_row in range(7):

            def one_row(row, totals):
                grad = slope[row, :, lane : lane + LANES]
                sums = []
                for tap_col in range(7):
                    product = grad * shifted[tap_col, row + tap_row, :, lane : lane + LANES]
                    pieces = [product[at : at + 16] for at in range(0, cols, 16)]
                    while len(pieces) > 1:
                        pieces = [a + b for a, b in zip(pieces[::2], pieces[1::2])]
                    wide = pieces[0].astype(jnp.float32)
                    sums.append(totals[tap_col] + wide[:8] + wide[8:])
                return tuple(sums)

            totals = lax.fori_loop(
                0, rows, one_row, tuple(jnp.zeros((8, LANES), jnp.float32) for _ in range(7)), unroll=4
            )
            for tap_col in range(7):
                small_sum[pl.ds(tap_row * 7 + tap_col, 1), lane : lane + LANES] = jnp.sum(
                    totals[tap_col], axis=0, keepdims=True
                )
            if tap_row % 3 == 2:
                yield
    at_row = 0
    for total in (w_in_sum, w_out_sum):
        for block in range(hidden_width // LANES):
            packed_ref[at_row : at_row + channels, :] = total[block].astype(jnp.bfloat16)
            at_row += channels
    for lane in range(0, channels, LANES):
        packed_ref[at_row : at_row + SMALL, :] = small_sum[:, lane : lane + LANES].astype(jnp.bfloat16)
        at_row += SMALL
    if at_row < packed_ref.shape[0]:
        spare = packed_ref.shape[0] - at_row
        packed_ref[at_row:, :] = jnp.zeros((spare, LANES), jnp.bfloat16)


def grid_scratch(state, hidden_width):
    rows, cols, channels = state.shape
    return [
        pltpu.VMEM((49, channels), jnp.float32),
        pltpu.VMEM((hidden_width // LANES, channels, LANES), jnp.float32),
        pltpu.VMEM((hidden_width // LANES, channels, LANES), jnp.float32),
        pltpu.VMEM((SMALL, channels), jnp.float32),
        pltpu.VMEM((7, rows + 6, cols, channels), jnp.bfloat16),
        pltpu.VMEM((28, 2 * LANES, 2 * LANES), jnp.bfloat16),
        pltpu.VMEM((rows // 2, 2, cols, channels), jnp.float32),
        pltpu.VMEM((rows, cols, channels), jnp.bfloat16),
    ]


def packed_rows(channels, hidden_width, devices):
    rows = 2 * (hidden_width // LANES) * channels + channels // LANES * SMALL
    return rows + -rows % (16 * devices)


def first_kernel(*refs):
    halo, (cot, kernel, gain, w_in, w_out, result, packed) = refs[:5], refs[5:12]
    for _ in grid_work(halo, cot, None, kernel, gain, w_in, w_out, result, packed, refs[12:]):
        pass


def first_grid(halo, cotangent, kernel, gain, w_in, w_out, devices):
    rows, cols, channels = cotangent.shape
    cells = rows * cols
    vmem = pl.BlockSpec(memory_space=pltpu.VMEM)
    args = (*halo, cotangent.reshape(cells, channels), kernel, gain.reshape(1, channels), w_in, w_out)
    result, packed = pl.pallas_call(
        first_kernel,
        out_shape=(
            jax.ShapeDtypeStruct((cells, channels), jnp.bfloat16),
            jax.ShapeDtypeStruct((packed_rows(*w_in.shape, devices), LANES), jnp.bfloat16),
        ),
        in_specs=[vmem] * len(args),
        out_specs=(vmem, vmem),
        scratch_shapes=grid_scratch(cotangent, w_in.shape[1]),
        compiler_params=pltpu.CompilerParams(vmem_limit_bytes=60 * 1024 * 1024),
    )(*args)
    return result.reshape(cotangent.shape), packed


def unpack_kernel(widths, state_ref, *refs):
    outs = refs[len(widths) : -2]
    carried = pltpu.make_async_copy(state_ref, refs[-2], refs[-1])
    carried.start()
    for number, (channels, hidden_width) in enumerate(widths):
        packed_ref, at = refs[number], 0
        kernel_out, gain_out, w_in_out, w_out_out = outs[4 * number : 4 * number + 4]
        for block in range(hidden_width // LANES):
            w_in_out[:, block * LANES : block * LANES + LANES] = packed_ref[at : at + channels, :].astype(
                jnp.float32
            )
            at += channels
        for block in range(hidden_width // LANES):
            w_out_out[block * LANES : block * LANES + LANES, :] = (
                packed_ref[at : at + channels, :].astype(jnp.float32).T
            )
            at += channels
        for lane in range(0, channels, LANES):
            small = packed_ref[at : at + SMALL, :].astype(jnp.float32)
            kernel_out[:, lane : lane + LANES] = small[:49]
            gain_out[:, lane : lane + LANES] = small[49:50]
            at += SMALL
    carried.wait()


def unpack(state, packed, widths):
    shapes = []
    for channels, hidden_width in widths:
        shapes += [(49, channels), (1, channels), (channels, hidden_width), (hidden_width, channels)]
    vmem = pl.BlockSpec(memory_space=pltpu.VMEM)
    anywhere = pl.BlockSpec(memory_space=pl.ANY)
    *outs, state = pl.pallas_call(
        functools.partial(unpack_kernel, widths),
        out_shape=(
            *(jax.ShapeDtypeStruct(shape, jnp.float32) for shape in shapes),
            jax.ShapeDtypeStruct(state.shape, state.dtype),
        ),
        in_specs=[anywhere] + [vmem] * len(widths),
        out_specs=(*([vmem] * len(shapes)), anywhere),
        scratch_shapes=[pltpu.SemaphoreType.DMA],
        compiler_params=pltpu.CompilerParams(vmem_limit_bytes=60 * 1024 * 1024),
    )(state, *packed)
    return (state, *(out.reshape(-1) if out.shape[0] == 1 else out for out in outs))


def aligned(index):
    return pl.multiple_of(index, 16)


def greet(partners):
    barrier = pltpu.get_barrier_semaphore()
    for partner in partners:
        pl.semaphore_signal(barrier, inc=1, device_id=partner, device_id_type=MESH)
    pl.semaphore_wait(barrier, len(partners))


def sum_plan(lon_count):
    spans = []
    span = 2
    while span < lon_count:
        spans.append(span)
        span *= 2
    return (spans, spans[::-1])


def sum_work(lat_count, lon_count, share_ref, full_ref, scratch):
    length = share_ref.shape[0]
    plan = sum_plan(lon_count)
    steps = len(plan[0])
    half, quarter = length // 2, length // 4
    first, lat_send, lat_recv, comb = scratch[:4]
    sends = [scratch[4 + part * steps : 4 + part * steps + steps] for part in range(2)]
    recvs = [scratch[4 + (2 + part) * steps : 4 + (2 + part) * steps + steps] for part in range(2)]
    totals = [scratch[4 + (4 + part) * steps : 4 + (4 + part) * steps + steps] for part in range(2)]
    send_sem, recv_sem = scratch[-2:]
    lat, lon = lax.axis_index("lat"), lax.axis_index("lon")
    core = lon % 2

    def flipped(span):
        bit = (lon // span) % 2
        return (lat, lon + span - 2 * span * bit), bit

    peers = [((lat + step) % lat_count, lon) for step in range(1, lat_count)]
    count = [0]

    def push(source, target, device):
        number = count[0]
        count[0] += 1
        copy = pltpu.make_async_remote_copy(
            src_ref=source,
            dst_ref=target,
            send_sem=send_sem.at[number],
            recv_sem=recv_sem.at[number],
            device_id=device,
            device_id_type=MESH,
        )
        copy.start()
        return copy

    pending = []
    opening = []
    for part in range(2):
        opening.append(
            push(
                share_ref.at[pl.ds(aligned((1 - core) * half + part * quarter), quarter), :],
                first.at[part],
                flipped(1)[0],
            )
        )
    active = [None, None]
    yield
    for part in range(2):
        opening[part].wait_recv()
        pending.append(opening[part])
        device, bit = flipped(plan[part][0])
        size = quarter // 2
        own = core * half + part * quarter

        def summed(start):
            return share_ref[pl.ds(aligned(own + start), size), :].astype(jnp.float32) + first[
                part, pl.ds(aligned(start), size), :
            ].astype(jnp.float32)

        sends[part][0][...] = summed((1 - bit) * size).astype(jnp.bfloat16)
        active[part] = push(sends[part][0], recvs[part][0], device)
        totals[part][0][...] = summed(bit * size)
    size = quarter // 2
    for step in range(steps):
        yield
        for part in range(2):
            active[part].wait_recv()
            pending.append(active[part])
            recv, total = recvs[part][step], totals[part][step]
            if step + 1 == steps:
                comb[part * size : part * size + size, :] = total[...] + recv[...].astype(jnp.float32)
                continue
            device, bit = flipped(plan[part][step + 1])
            rest = size // 2

            def joined(start):
                where = pl.ds(aligned(start), rest)
                return total[where, :] + recv[where, :].astype(jnp.float32)

            sends[part][step + 1][...] = joined((1 - bit) * rest).astype(jnp.bfloat16)
            active[part] = push(sends[part][step + 1], recvs[part][step + 1], device)
            totals[part][step + 1][...] = joined(bit * rest)
        if step + 1 < steps:
            size //= 2
    bases = []
    for part in range(2):
        base = core * half + part * quarter
        extent = quarter
        levels = []
        for span in plan[part]:
            extent //= 2
            base = base + ((lon // span) % 2) * extent
            levels.append((base, extent, span))
        bases.append(levels)
    chunk = 2 * size // lat_count
    lat_send[...] = comb[...].astype(jnp.bfloat16)
    arriving = []
    for step in range(1, lat_count):
        peer = (lat + step) % lat_count
        arriving.append(
            push(
                lat_send.at[pl.ds(aligned(peer * chunk), chunk), :],
                lat_recv.at[step - 1],
                (peer, lon),
            )
        )
    yield
    total = comb[pl.ds(aligned(lat * chunk), chunk), :]
    for step, copy in enumerate(arriving):
        copy.wait_recv()
        pending.append(copy)
        total = total + lat_recv[step].astype(jnp.float32)
    upper = (2 * lat) // lat_count
    low_base, high_base = bases[0][-1][0], bases[1][-1][0]
    place = low_base + upper * (high_base - low_base) + (lat - upper * (lat_count // 2)) * chunk
    mine = pl.ds(aligned(place), chunk)
    full_ref[mine, :] = total.astype(jnp.bfloat16)
    arriving = [push(full_ref.at[mine, :], full_ref.at[mine, :], peer) for peer in peers]
    yield
    for copy in arriving:
        copy.wait_recv()
        pending.append(copy)
    for step in reversed(range(steps)):
        arriving = []
        for part in range(2):
            base, extent, span = bases[part][step]
            region = full_ref.at[pl.ds(aligned(base), extent), :]
            arriving.append(push(region, region, flipped(span)[0]))
        yield
        for copy in arriving:
            copy.wait_recv()
            pending.append(copy)
    arriving = []
    for part in range(2):
        region = full_ref.at[pl.ds(aligned(core * half + part * quarter), quarter), :]
        arriving.append(push(region, region, flipped(1)[0]))
    yield
    for copy in arriving:
        copy.wait_recv()
        pending.append(copy)
    for copy in pending:
        copy.wait_send()


def sum_scratch(length, lat_count, lon_count):
    steps = len(sum_plan(lon_count)[0])
    sizes = [length // 4 // 2 ** (step + 1) for step in range(steps)]
    chunk = 2 * sizes[-1] // lat_count
    copies = 2 + 2 * steps + (lat_count - 1) * 2 + 2 * steps + 2
    narrow = [pltpu.VMEM((size, LANES), jnp.bfloat16) for size in sizes]
    wide = [pltpu.VMEM((size, LANES), jnp.float32) for size in sizes]
    return [
        pltpu.VMEM((2, length // 4, LANES), jnp.bfloat16),
        pltpu.VMEM((2 * sizes[-1], LANES), jnp.bfloat16),
        pltpu.VMEM((lat_count - 1, chunk, LANES), jnp.bfloat16),
        pltpu.VMEM((2 * sizes[-1], LANES), jnp.float32),
        *(narrow * 4),
        *(wide * 2),
        pltpu.SemaphoreType.DMA((copies,)),
        pltpu.SemaphoreType.DMA((copies,)),
    ]


def last_kernel(lat_count, lon_count, sizes, *refs):
    halo = refs[:5]
    cot, land, kernel, gain, w_in, w_out, share, result, full, last_full = refs[5:15]
    rest = refs[15:]
    grid_part, sum_part, last_part = (
        rest[: sizes[0]],
        rest[sizes[0] : sizes[0] + sizes[1]],
        rest[sizes[0] + sizes[1] : sizes[0] + 2 * sizes[1]],
    )
    packed = rest[-1]
    lat, lon = lax.axis_index("lat"), lax.axis_index("lon")
    partners = [((lat + step) % lat_count, lon) for step in range(1, lat_count)]
    span = 1
    while span < lon_count:
        partners.append((lat, lon + span - 2 * span * ((lon // span) % 2)))
        span *= 2
    greet(partners)
    summing = sum_work(lat_count, lon_count, share, full, sum_part)
    next(summing)
    for _ in grid_work(halo, cot, land, kernel, gain, w_in, w_out, result, packed, grid_part):
        next(summing, None)
    ending = sum_work(lat_count, lon_count, packed, last_full, last_part)
    next(ending)
    for _ in summing:
        pass
    for _ in ending:
        pass


def last_grid(halo, cotangent, land_sea, share, kernel, gain, w_in, w_out):
    lat_count, lon_count = lax.axis_size("lat"), lax.axis_size("lon")
    rows, cols, channels = cotangent.shape
    cells = rows * cols
    length = packed_rows(*w_in.shape, lat_count * lon_count)
    vmem = pl.BlockSpec(memory_space=pltpu.VMEM)
    args = (
        *halo,
        cotangent.reshape(cells, channels),
        land_sea,
        kernel,
        gain.reshape(1, channels),
        w_in,
        w_out,
        share,
    )
    grid_part = grid_scratch(cotangent, w_in.shape[1])
    sum_part = sum_scratch(share.shape[0], lat_count, lon_count)
    last_part = sum_scratch(length, lat_count, lon_count)
    outs = pl.pallas_call(
        functools.partial(last_kernel, lat_count, lon_count, (len(grid_part), len(sum_part))),
        out_shape=(
            jax.ShapeDtypeStruct((cells, channels), jnp.bfloat16),
            jax.ShapeDtypeStruct(share.shape, jnp.bfloat16),
            jax.ShapeDtypeStruct((length, LANES), jnp.bfloat16),
        ),
        in_specs=[vmem] * len(args),
        out_specs=(vmem,) * 3,
        scratch_shapes=[*grid_part, *sum_part, *last_part, pltpu.VMEM((length, LANES), jnp.bfloat16)],
        compiler_params=pltpu.CompilerParams(
            collective_id=2, has_side_effects=True, vmem_limit_bytes=60 * 1024 * 1024
        ),
    )(*args)
    return outs[0].reshape(cotangent.shape), outs[1:]


def to_tiles(pieces):
    return jnp.concatenate([piece.astype(jnp.float32) for piece in pieces], axis=0).astype(jnp.bfloat16)


def front_kernel(lat_count, lon_count, *refs):
    (
        atmos_ref,
        ocean_ref,
        land_ref,
        fold_ref,
        ocean_pairs,
        ocean_counts,
        ocean_weights_hbm,
        atmos_pairs,
        atmos_counts,
        atmos_weights_hbm,
        flux_map,
        surface_map,
        flux_inject,
        surface_inject,
    ) = refs[:14]
    atmos_out, ocean_out = refs[14:19], refs[19:24]
    (
        near_atmos,
        near_ocean,
        ocean_weights,
        atmos_weights,
        atmos_first,
        atmos_last,
        ocean_first,
        ocean_last,
        top_rows,
        circle_rows,
        send_sem,
        recv_sem,
        local_sem,
    ) = refs[24:]
    lat, lon = lax.axis_index("lat"), lax.axis_index("lon")
    east, west = (lon + 1) % lon_count, (lon + lon_count - 1) % lon_count
    has_south, has_north = lat > 0, lat < lat_count - 1
    beside = {-1: west, 0: lon, 1: east}
    cols = atmos_ref.shape[1]

    weight_copies = [
        pltpu.make_async_copy(ocean_weights_hbm, ocean_weights, local_sem.at[0]),
        pltpu.make_async_copy(atmos_weights_hbm, atmos_weights, local_sem.at[1]),
    ]
    for copy in weight_copies:
        copy.start()

    barrier = pltpu.get_barrier_semaphore()
    for step in range(1, lon_count):
        pl.semaphore_signal(
            barrier, inc=1, device_id=(lat, (lon + step) % lon_count), device_id_type=MESH
        )
    for band, there in ((-1, has_south), (1, has_north)):

        @pl.when(there)
        def _():
            for sector in (-1, 0, 1):
                pl.semaphore_signal(
                    barrier, inc=1, device_id=(lat + band, beside[sector]), device_id_type=MESH
                )

    pl.semaphore_wait(
        barrier, lon_count - 1 + 3 * has_south.astype(jnp.int32) + 3 * has_north.astype(jnp.int32)
    )

    numbers = {}

    def remote(name, source, target, device):
        number = numbers.setdefault(name, len(numbers))
        return pltpu.make_async_remote_copy(
            src_ref=source,
            dst_ref=target,
            send_sem=send_sem.at[number],
            recv_sem=recv_sem.at[number],
            device_id=device,
            device_id_type=MESH,
        )

    def each_neighbour(action):
        for band, there in ((-1, has_south), (0, None), (1, has_north)):
            for sector in (-1, 0, 1):
                if band == 0 and sector == 0:
                    continue
                if there is None:
                    action(band, sector)
                else:
                    pl.when(there)(functools.partial(action, band, sector))

    def field_copy(name, near, band, sector, waiting):
        own = near.at[4]
        return remote(
            (name, band, sector),
            own,
            near.at[(1 - band) * 3 + 1 - sector],
            (lat + band, beside[sector]),
        )

    def send_fields(name, near):
        each_neighbour(lambda band, sector: field_copy(name, near, band, sector, False).start())

    def await_fields(name, near):
        each_neighbour(
            lambda band, sector: remote(
                (name, -band, -sector),
                near.at[4],
                near.at[(1 + band) * 3 + 1 + sector],
                (lat + band, beside[sector]),
            ).wait_recv()
        )

    def fields(source, projection, near, masked):
        channels = source.shape[2]
        turned = projection[...]

        def one_block(block, carry):
            cells = source[pl.ds(2 * block, 2)].reshape(BCELLS, channels)
            values = dot(turned, cells, ((1,), (1,)))
            if masked:
                keep = jnp.concatenate(
                    [land_ref[pl.ds(2 * block, 1), :], land_ref[pl.ds(2 * block + 1, 1), :]], axis=1
                )
                values = values * keep.astype(jnp.float32)
            near[4, block] = values.astype(jnp.bfloat16)
            return carry

        lax.fori_loop(0, source.shape[0] // 2, one_block, 0, unroll=4)

    fields(atmos_ref, flux_map, near_atmos, False)
    send_fields("atmos_fields", near_atmos)
    fields(ocean_ref, surface_map, near_ocean, True)
    send_fields("ocean_fields", near_ocean)

    def remap(near, pairs, counts, weights, state, projection, target):
        source_count = near.shape[1]
        channels = state.shape[2]
        inject = projection[...]

        def one_block(block, carry):
            count = counts[0, block]
            picked = []
            for entry in range(PAIRS):
                number = pairs[entry, block]
                owner = number // source_count
                local = number - owner * source_count
                band = owner // lon_count
                sector = owner - band * lon_count - lon + 1 + lon_count
                sector = lax.rem(sector, lon_count)
                slot = jnp.clip((band - lat + 1) * 3 + sector, 0, 8)
                value = near[slot, local]
                if entry:
                    value = jnp.where(entry < count, value, jnp.zeros_like(value))
                picked.append(value)
            left = jnp.concatenate(picked, axis=1)
            mixed = dot(left, weights[block, 0].reshape(PAIRS * BCELLS, BCELLS))
            mixed = mixed.astype(jnp.bfloat16).astype(jnp.float32).T.astype(jnp.bfloat16)
            added = dot(mixed, inject)
            cells = state[pl.ds(2 * block, 2)].reshape(BCELLS, channels).astype(jnp.float32)
            target[pl.ds(2 * block, 2)] = (
                (cells + added).astype(jnp.bfloat16).reshape(2, state.shape[1], channels)
            )
            return carry

        lax.fori_loop(0, state.shape[0] // 2, one_block, 0, unroll=2)

    def edges(target, first, last):
        channels = target.shape[2]

        def one_tile(tile, carry):
            rows = target[pl.ds(4 * tile, 4)].astype(jnp.float32)
            first[tile] = to_tiles([rows[row, :EDGE] for row in range(4)])
            last[tile] = to_tiles([rows[row, cols - EDGE :] for row in range(4)])
            return carry

        lax.fori_loop(0, target.shape[0] // 4, one_tile, 0, unroll=2)

    def halo_copy(name, out, first, last, band, sector, to_neighbour):
        target, south, north, west_edge, east_edge = out
        rows = target.shape[0]
        tiles = rows // 4
        if sector == 0:
            source = target.at[rows - 3 : rows] if band == 1 else target.at[0:3]
            place = south if band == 1 else north
        else:
            edge = last if sector == 1 else first
            place = west_edge if sector == 1 else east_edge
            if band == 0:
                source, place = edge, place.at[1 : tiles + 1]
            elif band == 1:
                source, place = edge.at[tiles - 1], place.at[0]
            else:
                source, place = edge.at[0], place.at[tiles + 1]
        flip = 1 if to_neighbour else -1
        return remote(
            (name, band, sector), source, place, (lat + flip * band, beside[flip * sector])
        )

    def send_halo(name, out, first, last):
        each_neighbour(
            lambda band, sector: halo_copy(name, out, first, last, band, sector, True).start()
        )

    def await_halo(name, out, first, last):
        each_neighbour(
            lambda band, sector: halo_copy(name, out, first, last, -band, -sector, False).wait_recv()
        )

    def blank(out, at_north):
        target, south, north, west_edge, east_edge = out
        rim = north if at_north else south
        tile = target.shape[0] // 4 + 1 if at_north else 0
        rim[...] = jnp.zeros_like(rim)
        west_edge[tile] = jnp.zeros(west_edge.shape[1:], jnp.bfloat16)
        east_edge[tile] = jnp.zeros(east_edge.shape[1:], jnp.bfloat16)

    pl.when(jnp.logical_not(has_south))(lambda: blank(atmos_out, False))
    pl.when(jnp.logical_not(has_south))(lambda: blank(ocean_out, False))
    pl.when(jnp.logical_not(has_north))(lambda: blank(atmos_out, True))

    await_fields("atmos_fields", near_atmos)
    weight_copies[0].wait()
    remap(near_atmos, ocean_pairs, ocean_counts, ocean_weights, ocean_ref, flux_inject, ocean_out[0])
    edges(ocean_out[0], ocean_first, ocean_last)
    send_halo("ocean_halo", ocean_out, ocean_first, ocean_last)
    is_top = jnp.logical_not(has_north)
    top_at = ocean_out[0].shape[0] - 3

    def fold_copy(step, to_peer):
        flip = step if to_peer else lon_count - step
        return remote(
            ("fold", step),
            top_rows,
            circle_rows.at[:, pl.ds(pl.multiple_of(((lon if to_peer else (lon + flip) % lon_count)) * cols, 16), cols), :],
            (lat, (lon + flip) % lon_count),
        )

    @pl.when(is_top)
    def _():
        for row in range(3):
            top_rows[row] = ocean_out[0][top_at + 2 - row]
        for step in range(1, lon_count):
            fold_copy(step, True).start()
        own = pl.ds(pl.multiple_of(lon * cols, 16), cols)
        for row in range(3):
            circle_rows[row, own, :] = top_rows[row]

    await_fields("ocean_fields", near_ocean)
    weight_copies[1].wait()
    remap(near_ocean, atmos_pairs, atmos_counts, atmos_weights, atmos_ref, surface_inject, atmos_out[0])
    edges(atmos_out[0], atmos_first, atmos_last)
    send_halo("atmos_halo", atmos_out, atmos_first, atmos_last)

    @pl.when(is_top)
    def _():
        for step in range(1, lon_count):
            fold_copy(step, False).wait_recv()
        length = lon_count * cols
        partner = fold_ref[...]

        def chosen(first, count, repeat):
            place = lax.broadcasted_iota(jnp.int32, (count, length), 0)
            if repeat is not None:
                wanted = lax.rem(lon * cols + first + length + lax.rem(place, EDGE), length)
                live = place // EDGE == repeat
                return jnp.where(live & (partner == wanted), 1.0, 0.0).astype(jnp.bfloat16)
            return jnp.where(partner == lon * cols + place, 1.0, 0.0).astype(jnp.bfloat16)

        _, _, north, west_edge, east_edge = ocean_out
        tile = ocean_out[0].shape[0] // 4 + 1
        middle = chosen(0, cols, None)
        sides = [None, None]
        for row in range(3):
            line = circle_rows[row]
            north[row] = dot(middle, line).astype(jnp.bfloat16)
            for side, first in enumerate((-EDGE, cols)):
                part = dot(chosen(first, 16, row), line)
                sides[side] = part if row == 0 else sides[side] + part
        west_edge[tile] = sides[0].astype(jnp.bfloat16)
        east_edge[tile] = sides[1].astype(jnp.bfloat16)

    await_halo("ocean_halo", ocean_out, ocean_first, ocean_last)
    await_halo("atmos_halo", atmos_out, atmos_first, atmos_last)
    for name, near in (("atmos_fields", near_atmos), ("ocean_fields", near_ocean)):
        each_neighbour(
            lambda band, sector: field_copy(name, near, band, sector, False).wait_send()
        )
    for name, out, first, last in (
        ("ocean_halo", ocean_out, ocean_first, ocean_last),
        ("atmos_halo", atmos_out, atmos_first, atmos_last),
    ):
        each_neighbour(
            lambda band, sector: halo_copy(name, out, first, last, band, sector, True).wait_send()
        )

    @pl.when(is_top)
    def _():
        for step in range(1, lon_count):
            fold_copy(step, True).wait_send()


def front(
    atmos_state,
    ocean_state,
    land_sea,
    fold_partner,
    ocean_pairs,
    ocean_counts,
    ocean_weights,
    atmos_pairs,
    atmos_counts,
    atmos_weights,
    flux_map,
    surface_map,
    flux_inject,
    surface_inject,
):
    lat_count, lon_count = lax.axis_size("lat"), lax.axis_size("lon")
    vmem = pl.BlockSpec(memory_space=pltpu.VMEM)
    smem = pl.BlockSpec(memory_space=pltpu.SMEM)
    anywhere = pl.BlockSpec(memory_space=pl.ANY)

    def out_shapes(state):
        rows, cols, channels = state.shape
        return [
            jax.ShapeDtypeStruct(shape, jnp.bfloat16)
            for shape in (
                (rows, cols, channels),
                (3, cols, channels),
                (3, cols, channels),
                (rows // 4 + 2, 16, channels),
                (rows // 4 + 2, 16, channels),
            )
        ]

    def edge_scratch(state):
        return pltpu.VMEM((state.shape[0] // 4, 16, state.shape[2]), jnp.bfloat16)

    copies = 32 + lon_count - 1
    cols = atmos_state.shape[1]
    ocean_channels = ocean_state.shape[2]
    outs = pl.pallas_call(
        functools.partial(front_kernel, lat_count, lon_count),
        out_shape=tuple(out_shapes(atmos_state) + out_shapes(ocean_state)),
        in_specs=[vmem, vmem, vmem, vmem, smem, smem, anywhere, smem, smem, anywhere] + [vmem] * 4,
        out_specs=(vmem,) * 10,
        scratch_shapes=[
            pltpu.VMEM((9, atmos_state.shape[0] // 2, NFIELD, BCELLS), jnp.bfloat16),
            pltpu.VMEM((9, ocean_state.shape[0] // 2, NFIELD, BCELLS), jnp.bfloat16),
            pltpu.VMEM(ocean_weights.shape, jnp.bfloat16),
            pltpu.VMEM(atmos_weights.shape, jnp.bfloat16),
            edge_scratch(atmos_state),
            edge_scratch(atmos_state),
            edge_scratch(ocean_state),
            edge_scratch(ocean_state),
            pltpu.VMEM((3, cols, ocean_channels), jnp.bfloat16),
            pltpu.VMEM((3, lon_count * cols, ocean_channels), jnp.bfloat16),
            pltpu.SemaphoreType.DMA((copies,)),
            pltpu.SemaphoreType.DMA((copies,)),
            pltpu.SemaphoreType.DMA((2,)),
        ],
        compiler_params=pltpu.CompilerParams(
            collective_id=1, has_side_effects=True, vmem_limit_bytes=60 * 1024 * 1024
        ),
    )(
        atmos_state,
        ocean_state,
        land_sea,
        fold_partner.reshape(1, -1),
        ocean_pairs.reshape(-1, PAIRS).T,
        ocean_counts.T,
        ocean_weights,
        atmos_pairs.reshape(-1, PAIRS).T,
        atmos_counts.T,
        atmos_weights,
        flux_map.T,
        surface_map.T,
        flux_inject,
        surface_inject,
    )
    return outs[:5], outs[5:]


def shards(
    atmos_state,
    ocean_state,
    atmos_cotangent,
    ocean_cotangent,
    land_sea,
    fold_partner,
    ocean_pairs,
    ocean_counts,
    ocean_weights,
    atmos_pairs,
    atmos_counts,
    atmos_weights,
    flux_map,
    surface_map,
    flux_inject,
    surface_inject,
    atmos_kernel,
    atmos_gain,
    atmos_w_in,
    atmos_w_out,
    ocean_kernel,
    ocean_gain,
    ocean_w_in,
    ocean_w_out,
):
    atmos_halo, ocean_halo = front(
        atmos_state,
        ocean_state,
        land_sea,
        fold_partner,
        ocean_pairs,
        ocean_counts,
        ocean_weights,
        atmos_pairs,
        atmos_counts,
        atmos_weights,
        flux_map,
        surface_map,
        flux_inject,
        surface_inject,
    )
    devices = lax.axis_size("lat") * lax.axis_size("lon")
    atmos_next, share = first_grid(
        atmos_halo, atmos_cotangent, atmos_kernel, atmos_gain, atmos_w_in, atmos_w_out, devices
    )
    ocean_next, packed = last_grid(
        ocean_halo,
        ocean_cotangent,
        land_sea,
        share,
        ocean_kernel,
        ocean_gain,
        ocean_w_in,
        ocean_w_out,
    )
    widths = (atmos_w_in.shape, ocean_w_in.shape)
    return (atmos_next, *unpack(ocean_next, packed, widths))


def solution(mesh):
    return jax.shard_map(
        shards,
        mesh=mesh,
        in_specs=(
            P("lat", "lon", None),
            P("lat", "lon", None),
            P("lat", "lon", None),
            P("lat", "lon", None),
            P("lat", "lon"),
            P(),
            P("lat", "lon", None),
            P("lat", "lon"),
            P("lat", "lon", None, None, None),
            P("lat", "lon", None),
            P("lat", "lon"),
            P("lat", "lon", None, None, None),
            P(),
            P(),
            P(),
            P(),
            P(),
            P(),
            P(),
            P(),
            P(),
            P(),
            P(),
            P(),
        ),
        out_specs=(
            P("lat", "lon", None),
            P("lat", "lon", None),
            P(),
            P(),
            P(),
            P(),
            P(),
            P(),
            P(),
            P(),
        ),
        check_vma=False,
    )
```

```python
import functools

import jax
import jax.numpy as jnp
from jax import lax
from jax.experimental import pallas as pl
from jax.experimental.pallas import tpu as pltpu
from jax.sharding import PartitionSpec as P

NFIELD = 16
BCELLS = 128
PAIRS = 4
LANES = 128
SMALL = 64
EDGE = 4
MESH = pl.DeviceIdType.MESH
epsilon = 1e-06
TANH_SCALE = 0.7978845608028654
TANH_CUBIC = 0.044715


def dot(left, right, dims=((1,), (0,))):
    return lax.dot_general(left, right, (dims, ((), ())), preferred_element_type=jnp.float32)


def shift_phase(halo, shifted, rows, cols):
    inner, south, north, west, east = halo

    def one_tile(tile, line_of, live):
        left = west[tile].astype(jnp.float32)
        right = east[tile].astype(jnp.float32)
        for slot in live:
            wide = jnp.concatenate(
                [
                    left[4 * slot : 4 * slot + 4],
                    line_of(slot).astype(jnp.float32),
                    right[4 * slot : 4 * slot + 4],
                ],
                axis=0,
            )
            for tap_col in range(7):
                shifted[tap_col, 4 * tile + slot - 1] = wide[tap_col + 1 : tap_col + 1 + cols].astype(
                    jnp.bfloat16
                )

    def middle_tile(tile, carry):
        one_tile(tile, lambda slot: inner[4 * tile + slot - 4], range(4))
        return carry

    one_tile(0, lambda slot: south[slot - 1], range(1, 4))
    lax.fori_loop(1, rows // 4 + 1, middle_tile, 0)
    one_tile(rows // 4 + 1, lambda slot: north[slot], range(3))


def conv_phase(shifted, kernel_ref, banded, conv, rows, cols, channels):
    pair_step = 8
    across = lax.broadcasted_iota(jnp.int32, (LANES, LANES), 0)
    down = lax.broadcasted_iota(jnp.int32, (LANES, LANES), 1)
    eye = across == down
    for lane in range(0, channels, LANES):
        for tap_col in range(7):
            for step in range(4):
                for low in range(2):
                    for out in range(2):
                        tap_row = 2 * step + low - out
                        if 0 <= tap_row < 7:
                            tap = kernel_ref[pl.ds(tap_row * 7 + tap_col, 1), lane : lane + LANES]
                            block = jnp.where(eye, tap, 0.0).astype(jnp.bfloat16)
                        else:
                            block = jnp.zeros((LANES, LANES), jnp.bfloat16)
                        banded[
                            tap_col * 4 + step,
                            low * LANES : low * LANES + LANES,
                            out * LANES : out * LANES + LANES,
                        ] = block

        def one_chunk(index, carry):
            total = None
            for tap_col in range(7):
                for step in range(4):
                    window = shifted[
                        tap_col,
                        pl.ds(2 * (index * pair_step + step), 2 * pair_step),
                        :,
                        lane : lane + LANES,
                    ].reshape(pair_step, 2, cols, LANES)
                    left = jnp.concatenate(
                        [
                            window[:, 0].reshape(pair_step * cols, LANES),
                            window[:, 1].reshape(pair_step * cols, LANES),
                        ],
                        axis=1,
                    )
                    part = dot(left, banded[tap_col * 4 + step])
                    total = part if total is None else total + part
            for out in range(2):
                conv[pl.ds(index * pair_step, pair_step), out, :, lane : lane + LANES] = total[
                    :, out * LANES : out * LANES + LANES
                ].reshape(pair_step, cols, LANES)
            return carry

        for index in range(rows // 2 // pair_step):
            lax.fori_loop(index, index + 1, one_chunk, 0)
            yield


def grid_work(
    halo, cot_ref, land_ref, kernel_ref, gain_ref, w_in_ref, w_out_ref, next_ref, packed_ref, banded, scratch
):
    taps, w_in_sum, w_out_sum, small_sum, shifted, conv, slope = scratch
    rows, cols, channels = halo[0].shape
    hidden_width = w_in_ref.shape[1]
    row_step = 8
    cells = row_step * cols
    chunk = 256
    shift_phase(halo, shifted, rows, cols)
    yield
    taps[...] = kernel_ref[...].astype(jnp.float32)
    yield from conv_phase(shifted, taps, banded, conv, rows, cols, channels)
    w_in_sum[...] = jnp.zeros_like(w_in_sum)
    w_out_sum[...] = jnp.zeros_like(w_out_sum)
    small_sum[...] = jnp.zeros_like(small_sum)
    gain = gain_ref[...].astype(jnp.float32)

    def one_block(index, gain_total):
        value = conv[pl.ds(index * (row_step // 2), row_step // 2)].reshape(cells, channels)
        centre = value - jnp.mean(value, axis=-1, keepdims=True)
        inv = lax.rsqrt(jnp.mean(centre * centre, axis=-1, keepdims=True) + epsilon)
        unit = centre * inv
        normed = (unit * gain).astype(jnp.bfloat16)
        where = pl.ds(index * cells, cells)
        upstream = cot_ref[where, :]
        if land_ref is not None:
            turned = land_ref[pl.ds(pl.multiple_of(index * row_step, 8), row_step), :].astype(jnp.float32).T
            keep = jnp.concatenate(
                [jnp.broadcast_to(turned[:, row : row + 1], (cols, channels)) for row in range(row_step)],
                axis=0,
            )
            upstream = upstream * keep.astype(jnp.bfloat16)
        normed_t = normed.T
        upstream_t = upstream.T
        update = None
        back = None
        for at in range(0, hidden_width, chunk):
            w_in = w_in_ref[:, at : at + chunk]
            w_out = w_out_ref[at : at + chunk, :]
            pre = dot(normed, w_in)
            grad_hidden = dot(upstream, w_out, ((1,), (1,)))
            square = pre * pre
            gate = 0.5 + 0.5 * jnp.tanh(pre * (TANH_SCALE + (TANH_SCALE * TANH_CUBIC) * square))
            active = pre * gate
            slope_part = 2 * TANH_SCALE + (6 * TANH_SCALE * TANH_CUBIC) * square
            grad_pre = (grad_hidden * (gate + active * (1.0 - gate) * slope_part)).astype(jnp.bfloat16)
            active = active.astype(jnp.bfloat16)
            part = dot(active, w_out)
            update = part if update is None else update + part
            part = dot(grad_pre, w_in, ((1,), (1,)))
            back = part if back is None else back + part
            for total, part in (
                (w_out_sum, dot(upstream_t, active)),
                (w_in_sum, dot(normed_t, grad_pre)),
            ):
                for lane in range(0, chunk, LANES):
                    total[(at + lane) // LANES] += part[:, lane : lane + LANES]
        inside = shifted[3, pl.ds(index * row_step + 3, row_step)].reshape(cells, channels)
        result = inside.astype(jnp.float32) + update
        if land_ref is not None:
            result = result * keep
        next_ref[where, :] = result.astype(jnp.bfloat16)
        gain_total = gain_total + jnp.sum((back * unit).reshape(cells // 8, 8, channels), axis=0)
        back = back * gain
        level = jnp.mean(back, axis=-1, keepdims=True)
        tilt = jnp.mean(back * unit, axis=-1, keepdims=True)
        slope[pl.ds(index * row_step, row_step)] = (
            (inv * (back - level - unit * tilt)).astype(jnp.bfloat16).reshape(row_step, cols, channels)
        )
        return gain_total

    blocks = rows // row_step
    gain_total = jnp.zeros((8, channels), jnp.float32)
    for start in range(0, blocks, 2):
        gain_total = lax.fori_loop(start, min(start + 2, blocks), one_block, gain_total)
        yield
    small_sum[49:50, :] = jnp.sum(gain_total, axis=0, keepdims=True)
    at_row = 0
    for total in (w_in_sum, w_out_sum):
        for block in range(hidden_width // LANES):
            packed_ref[at_row : at_row + channels, :] = total[block].astype(jnp.bfloat16)
            at_row += channels
    if at_row < packed_ref.shape[0]:
        spare = packed_ref.shape[0] - at_row
        packed_ref[at_row:, :] = jnp.zeros((spare, LANES), jnp.bfloat16)


def tap_work(packed_ref, scratch):
    small_sum, shifted, _, slope = scratch[3:]
    rows, cols, channels = slope.shape
    for lane in range(0, channels, LANES):
        for tap_row in range(7):

            def one_row(row, totals):
                grad = slope[row, :, lane : lane + LANES]
                sums = []
                for tap_col in range(7):
                    product = grad * shifted[tap_col, row + tap_row, :, lane : lane + LANES]
                    pieces = [product[at : at + 16] for at in range(0, cols, 16)]
                    while len(pieces) > 1:
                        pieces = [a + b for a, b in zip(pieces[::2], pieces[1::2])]
                    wide = pieces[0].astype(jnp.float32)
                    sums.append(totals[tap_col] + wide[:8] + wide[8:])
                return tuple(sums)

            totals = lax.fori_loop(
                0, rows, one_row, tuple(jnp.zeros((8, LANES), jnp.float32) for _ in range(7)), unroll=4
            )
            for tap_col in range(7):
                small_sum[pl.ds(tap_row * 7 + tap_col, 1), lane : lane + LANES] = jnp.sum(
                    totals[tap_col], axis=0, keepdims=True
                )
            if tap_row % 2:
                yield
    for lane in range(0, channels, LANES):
        at_row = lane // LANES * SMALL
        packed_ref[at_row : at_row + SMALL, :] = small_sum[:, lane : lane + LANES].astype(jnp.bfloat16)


def grid_scratch(state, hidden_width):
    rows, cols, channels = state.shape
    return [
        pltpu.VMEM((49, channels), jnp.float32),
        pltpu.VMEM((hidden_width // LANES, channels, LANES), jnp.float32),
        pltpu.VMEM((hidden_width // LANES, channels, LANES), jnp.float32),
        pltpu.VMEM((SMALL, channels), jnp.float32),
        pltpu.VMEM((7, rows + 6, cols, channels), jnp.bfloat16),
        pltpu.VMEM((rows // 2, 2, cols, channels), jnp.float32),
        pltpu.VMEM((rows, cols, channels), jnp.bfloat16),
    ]


def packed_rows(channels, hidden_width, devices):
    rows = 2 * (hidden_width // LANES) * channels
    return rows + -rows % (16 * devices)


def unpack_kernel(widths, *refs):
    count = len(widths)
    states, outs = refs[:count], refs[3 * count :]
    for state, out in zip(states, outs[:count]):
        out[...] = state[...]
    outs = outs[count:]
    for number, (channels, hidden_width) in enumerate(widths):
        packed_ref, small_ref = refs[count + number], refs[2 * count + number]
        at = 0
        kernel_out, gain_out, w_in_out, w_out_out = outs[4 * number : 4 * number + 4]
        for block in range(hidden_width // LANES):
            w_in_out[:, block * LANES : block * LANES + LANES] = packed_ref[at : at + channels, :].astype(
                jnp.float32
            )
            at += channels
        for block in range(hidden_width // LANES):
            w_out_out[block * LANES : block * LANES + LANES, :] = (
                packed_ref[at : at + channels, :].astype(jnp.float32).T
            )
            at += channels
        for lane in range(0, channels, LANES):
            at = lane // LANES * SMALL
            small = small_ref[at : at + SMALL, :].astype(jnp.float32)
            kernel_out[:, lane : lane + LANES] = small[:49]
            gain_out[:, lane : lane + LANES] = small[49:50]


def unpack(states, packed, smalls, widths):
    shapes = []
    for channels, hidden_width in widths:
        shapes += [(49, channels), (1, channels), (channels, hidden_width), (hidden_width, channels)]
    vmem = pl.BlockSpec(memory_space=pltpu.VMEM)
    outs = pl.pallas_call(
        functools.partial(unpack_kernel, widths),
        out_shape=(
            *(jax.ShapeDtypeStruct(state.shape, state.dtype) for state in states),
            *(jax.ShapeDtypeStruct(shape, jnp.float32) for shape in shapes),
        ),
        in_specs=[vmem] * (3 * len(widths)),
        out_specs=(vmem,) * (len(states) + len(shapes)),
        compiler_params=pltpu.CompilerParams(vmem_limit_bytes=60 * 1024 * 1024),
    )(*states, *packed, *smalls)
    return [out.reshape(-1) if out.shape[0] == 1 else out for out in outs]


def aligned(index):
    return pl.multiple_of(index, 16)


def greet(partners):
    barrier = pltpu.get_barrier_semaphore()
    for partner in partners:
        pl.semaphore_signal(barrier, inc=1, device_id=partner, device_id_type=MESH)
    pl.semaphore_wait(barrier, len(partners))


def sum_plan(lon_count):
    spans = []
    span = 2
    while span < lon_count:
        spans.append(span)
        span *= 2
    return (spans, spans[::-1])


def sum_work(lat_count, lon_count, share_ref, full_ref, scratch):
    length = share_ref.shape[0]
    plan = sum_plan(lon_count)
    steps = len(plan[0])
    half, quarter = length // 2, length // 4
    first, lat_send, lat_recv, comb = scratch[:4]
    sends = [scratch[4 + part * steps : 4 + part * steps + steps] for part in range(2)]
    recvs = [scratch[4 + (2 + part) * steps : 4 + (2 + part) * steps + steps] for part in range(2)]
    totals = [scratch[4 + (4 + part) * steps : 4 + (4 + part) * steps + steps] for part in range(2)]
    send_sem, recv_sem = scratch[-2:]
    lat, lon = lax.axis_index("lat"), lax.axis_index("lon")
    core = lon % 2

    def flipped(span):
        bit = (lon // span) % 2
        return (lat, lon + span - 2 * span * bit), bit

    peers = [((lat + step) % lat_count, lon) for step in range(1, lat_count)]
    push = pusher(send_sem, recv_sem)
    pending = []
    opening = []
    for part in range(2):
        opening.append(
            push(
                share_ref.at[pl.ds(aligned((1 - core) * half + part * quarter), quarter), :],
                first.at[part],
                flipped(1)[0],
            )
        )
    active = [None, None]
    yield
    for part in range(2):
        opening[part].wait_recv()
        pending.append(opening[part])
        device, bit = flipped(plan[part][0])
        size = quarter // 2
        own = core * half + part * quarter

        def summed(start):
            return share_ref[pl.ds(aligned(own + start), size), :].astype(jnp.float32) + first[
                part, pl.ds(aligned(start), size), :
            ].astype(jnp.float32)

        sends[part][0][...] = summed((1 - bit) * size).astype(jnp.bfloat16)
        active[part] = push(sends[part][0], recvs[part][0], device)
        totals[part][0][...] = summed(bit * size)
    size = quarter // 2
    for step in range(steps):
        yield
        for part in range(2):
            active[part].wait_recv()
            pending.append(active[part])
            recv, total = recvs[part][step], totals[part][step]
            if step + 1 == steps:
                comb[part * size : part * size + size, :] = total[...] + recv[...].astype(jnp.float32)
                continue
            device, bit = flipped(plan[part][step + 1])
            rest = size // 2

            def joined(start):
                where = pl.ds(aligned(start), rest)
                return total[where, :] + recv[where, :].astype(jnp.float32)

            sends[part][step + 1][...] = joined((1 - bit) * rest).astype(jnp.bfloat16)
            active[part] = push(sends[part][step + 1], recvs[part][step + 1], device)
            totals[part][step + 1][...] = joined(bit * rest)
        if step + 1 < steps:
            size //= 2
    bases = []
    for part in range(2):
        base = core * half + part * quarter
        extent = quarter
        levels = []
        for span in plan[part]:
            extent //= 2
            base = base + ((lon // span) % 2) * extent
            levels.append((base, extent, span))
        bases.append(levels)
    chunk = 2 * size // lat_count
    lat_send[...] = comb[...].astype(jnp.bfloat16)
    arriving = []
    for step in range(1, lat_count):
        peer = (lat + step) % lat_count
        arriving.append(
            push(
                lat_send.at[pl.ds(aligned(peer * chunk), chunk), :],
                lat_recv.at[step - 1],
                (peer, lon),
            )
        )
    yield
    total = comb[pl.ds(aligned(lat * chunk), chunk), :]
    for step, copy in enumerate(arriving):
        copy.wait_recv()
        pending.append(copy)
        total = total + lat_recv[step].astype(jnp.float32)
    upper = (2 * lat) // lat_count
    low_base, high_base = bases[0][-1][0], bases[1][-1][0]
    place = low_base + upper * (high_base - low_base) + (lat - upper * (lat_count // 2)) * chunk
    mine = pl.ds(aligned(place), chunk)
    full_ref[mine, :] = total.astype(jnp.bfloat16)
    arriving = [push(full_ref.at[mine, :], full_ref.at[mine, :], peer) for peer in peers]
    yield
    for copy in arriving:
        copy.wait_recv()
        pending.append(copy)
    for step in reversed(range(steps)):
        arriving = []
        for part in range(2):
            base, extent, span = bases[part][step]
            region = full_ref.at[pl.ds(aligned(base), extent), :]
            arriving.append(push(region, region, flipped(span)[0]))
        yield
        for copy in arriving:
            copy.wait_recv()
            pending.append(copy)
    arriving = []
    for part in range(2):
        region = full_ref.at[pl.ds(aligned(core * half + part * quarter), quarter), :]
        arriving.append(push(region, region, flipped(1)[0]))
    yield
    for copy in arriving:
        copy.wait_recv()
        pending.append(copy)
    for copy in pending:
        copy.wait_send()


def sum_scratch(length, lat_count, lon_count):
    steps = len(sum_plan(lon_count)[0])
    sizes = [length // 4 // 2 ** (step + 1) for step in range(steps)]
    chunk = 2 * sizes[-1] // lat_count
    copies = 2 + 2 * steps + (lat_count - 1) * 2 + 2 * steps + 2
    narrow = [pltpu.VMEM((size, LANES), jnp.bfloat16) for size in sizes]
    wide = [pltpu.VMEM((size, LANES), jnp.float32) for size in sizes]
    return [
        pltpu.VMEM((2, length // 4, LANES), jnp.bfloat16),
        pltpu.VMEM((2 * sizes[-1], LANES), jnp.bfloat16),
        pltpu.VMEM((lat_count - 1, chunk, LANES), jnp.bfloat16),
        pltpu.VMEM((2 * sizes[-1], LANES), jnp.float32),
        *(narrow * 4),
        *(wide * 2),
        pltpu.SemaphoreType.DMA((copies,)),
        pltpu.SemaphoreType.DMA((copies,)),
    ]


def pusher(send_sem, recv_sem):
    count = [0]

    def push(source, target, device):
        number = count[0]
        count[0] += 1
        copy = pltpu.make_async_remote_copy(
            src_ref=source,
            dst_ref=target,
            send_sem=send_sem.at[number],
            recv_sem=recv_sem.at[number],
            device_id=device,
            device_id_type=MESH,
        )
        copy.start()
        return copy

    return push


def flat_work(lat_count, lon_count, share_ref, full_ref, scratch):
    lon_recv, lat_send, lat_recv, send_sem, recv_sem = scratch
    lat, lon = lax.axis_index("lat"), lax.axis_index("lon")
    push = pusher(send_sem, recv_sem)
    chunk = share_ref.shape[0] // lon_count
    part = chunk // lat_count
    lons = [(lon + step) % lon_count for step in range(1, lon_count)]
    lats = [(lat + step) % lat_count for step in range(1, lat_count)]
    done = []
    copies = [
        push(share_ref.at[pl.ds(aligned(peer * chunk), chunk), :], lon_recv.at[step], (lat, peer))
        for step, peer in enumerate(lons)
    ]
    yield
    total = share_ref[pl.ds(aligned(lon * chunk), chunk), :].astype(jnp.float32)
    for step, copy in enumerate(copies):
        copy.wait_recv()
        total = total + lon_recv[step].astype(jnp.float32)
    done += copies
    lat_send[...] = total.astype(jnp.bfloat16)
    copies = [
        push(lat_send.at[pl.ds(aligned(peer * part), part), :], lat_recv.at[step], (peer, lon))
        for step, peer in enumerate(lats)
    ]
    yield
    total = lat_send[pl.ds(aligned(lat * part), part), :].astype(jnp.float32)
    for step, copy in enumerate(copies):
        copy.wait_recv()
        total = total + lat_recv[step].astype(jnp.float32)
    done += copies
    mine = pl.ds(aligned(lon * chunk + lat * part), part)
    full_ref[mine, :] = total.astype(jnp.bfloat16)
    copies = [push(full_ref.at[mine, :], full_ref.at[mine, :], (peer, lon)) for peer in lats]
    yield
    for copy in copies:
        copy.wait_recv()
    done += copies
    region = pl.ds(aligned(lon * chunk), chunk)
    copies = [push(full_ref.at[region, :], full_ref.at[region, :], (lat, peer)) for peer in lons]
    yield
    for copy in copies:
        copy.wait_recv()
    done += copies
    for copy in done:
        copy.wait_send()


def flat_scratch(length, lat_count, lon_count):
    chunk = length // lon_count
    copies = 2 * (lat_count + lon_count - 2)
    return [
        pltpu.VMEM((lon_count - 1, chunk, LANES), jnp.bfloat16),
        pltpu.VMEM((chunk, LANES), jnp.bfloat16),
        pltpu.VMEM((lat_count - 1, chunk // lat_count, LANES), jnp.bfloat16),
        pltpu.SemaphoreType.DMA((copies,)),
        pltpu.SemaphoreType.DMA((copies,)),
    ]


def small_work(lat_count, lon_count, share_ref, full_ref, scratch):
    lon_terms, lat_terms, middle, send_sem, recv_sem = scratch
    lat, lon = lax.axis_index("lat"), lax.axis_index("lon")
    push = pusher(send_sem, recv_sem)
    copies = []
    for step in range(1, lon_count):
        copies.append(push(share_ref, lon_terms.at[lon], (lat, (lon + step) % lon_count)))
    lon_terms[lon] = share_ref[...]
    yield
    for copy in copies:
        copy.wait_recv()
    total = lon_terms[0].astype(jnp.float32)
    for term in range(1, lon_count):
        total = total + lon_terms[term].astype(jnp.float32)
    middle[...] = total.astype(jnp.bfloat16)
    for step in range(1, lat_count):
        copies.append(push(middle, lat_terms.at[lat], ((lat + step) % lat_count, lon)))
    lat_terms[lat] = middle[...]
    yield
    for copy in copies[lon_count - 1 :]:
        copy.wait_recv()
    total = lat_terms[0].astype(jnp.float32)
    for term in range(1, lat_count):
        total = total + lat_terms[term].astype(jnp.float32)
    full_ref[...] = total.astype(jnp.bfloat16)
    for copy in copies:
        copy.wait_send()


def small_scratch(length, lat_count, lon_count):
    copies = lat_count + lon_count - 2
    return [
        pltpu.VMEM((lon_count, length, LANES), jnp.bfloat16),
        pltpu.VMEM((lat_count, length, LANES), jnp.bfloat16),
        pltpu.VMEM((length, LANES), jnp.bfloat16),
        pltpu.SemaphoreType.DMA((copies,)),
        pltpu.SemaphoreType.DMA((copies,)),
    ]


def grids_kernel(lat_count, lon_count, sizes, *refs):
    atmos_halo, ocean_halo = refs[:5], refs[5:10]
    atmos_args, ocean_args, land = refs[10:15], refs[15:20], refs[20]
    atmos_next, ocean_next, atmos_full, ocean_full, atmos_small, ocean_small = refs[21:27]
    rest = list(refs[27:])
    parts = []
    for size in sizes:
        parts.append(rest[:size])
        rest = rest[size:]
    atmos_part, ocean_part, atmos_sum, ocean_sum, atmos_small_sum, ocean_small_sum = parts
    banded, atmos_share, ocean_share, atmos_few, ocean_few = rest
    lat, lon = lax.axis_index("lat"), lax.axis_index("lon")
    greet(
        [((lat + step) % lat_count, lon) for step in range(1, lat_count)]
        + [(lat, (lon + step) % lon_count) for step in range(1, lon_count)]
    )
    active = []

    def along(work):
        for _ in work:
            for sums in active:
                next(sums, None)

    def begin(work, *args):
        sums = work(lat_count, lon_count, *args)
        next(sums)
        active.append(sums)

    def first_part(halo, args, mask, result, share, part):
        cot, kernel, gain, w_in, w_out = args
        return grid_work(halo, cot, mask, kernel, gain, w_in, w_out, result, share, banded, part)

    along(first_part(atmos_halo, atmos_args, None, atmos_next, atmos_share, atmos_part))
    begin(sum_work, atmos_share, atmos_full, atmos_sum)
    along(first_part(ocean_halo, ocean_args, land, ocean_next, ocean_share, ocean_part))
    begin(flat_work, ocean_share, ocean_full, ocean_sum)
    along(tap_work(atmos_few, atmos_part))
    begin(small_work, atmos_few, atmos_small, atmos_small_sum)
    along(tap_work(ocean_few, ocean_part))
    begin(small_work, ocean_few, ocean_small, ocean_small_sum)
    for sums in active:
        for _ in sums:
            pass


def run_grids(atmos_halo, ocean_halo, land_sea, atmos_args, ocean_args):
    lat_count, lon_count = lax.axis_size("lat"), lax.axis_size("lon")
    vmem = pl.BlockSpec(memory_space=pltpu.VMEM)
    flat, states, shares, smalls, parts = [], [], [], [], []
    for cotangent, kernel, gain, w_in, w_out in (atmos_args, ocean_args):
        rows, cols, channels = cotangent.shape
        flat += [cotangent.reshape(rows * cols, channels), kernel, gain.reshape(1, channels), w_in, w_out]
        states.append((rows * cols, channels))
        shares.append((packed_rows(*w_in.shape, lat_count * lon_count), LANES))
        smalls.append((channels // LANES * SMALL, LANES))
        parts.append(grid_scratch(cotangent, w_in.shape[1]))
    parts.append(sum_scratch(shares[0][0], lat_count, lon_count))
    parts.append(flat_scratch(shares[1][0], lat_count, lon_count))
    parts += [small_scratch(small[0], lat_count, lon_count) for small in smalls]
    narrow = shares + smalls
    args = (*atmos_halo, *ocean_halo, *flat, land_sea)
    outs = pl.pallas_call(
        functools.partial(grids_kernel, lat_count, lon_count, tuple(len(part) for part in parts)),
        out_shape=tuple(jax.ShapeDtypeStruct(shape, jnp.bfloat16) for shape in states + narrow),
        in_specs=[vmem] * len(args),
        out_specs=(vmem,) * (len(states) + len(narrow)),
        scratch_shapes=[
            *(piece for part in parts for piece in part),
            pltpu.VMEM((28, 2 * LANES, 2 * LANES), jnp.bfloat16),
            *(pltpu.VMEM(shape, jnp.bfloat16) for shape in narrow),
        ],
        compiler_params=pltpu.CompilerParams(
            collective_id=2, has_side_effects=True, vmem_limit_bytes=60 * 1024 * 1024
        ),
    )(*args)
    return outs[:2], outs[2:4], outs[4:]


def to_tiles(pieces):
    return jnp.concatenate([piece.astype(jnp.float32) for piece in pieces], axis=0).astype(jnp.bfloat16)


def front_kernel(lat_count, lon_count, *refs):
    (
        atmos_ref,
        ocean_ref,
        land_ref,
        fold_ref,
        ocean_pairs,
        ocean_counts,
        ocean_weights_hbm,
        atmos_pairs,
        atmos_counts,
        atmos_weights_hbm,
        flux_map,
        surface_map,
        flux_inject,
        surface_inject,
    ) = refs[:14]
    atmos_out, ocean_out = refs[14:19], refs[19:24]
    (
        near_atmos,
        near_ocean,
        ocean_weights,
        atmos_weights,
        atmos_first,
        atmos_last,
        ocean_first,
        ocean_last,
        top_rows,
        circle_rows,
        send_sem,
        recv_sem,
        local_sem,
    ) = refs[24:]
    lat, lon = lax.axis_index("lat"), lax.axis_index("lon")
    east, west = (lon + 1) % lon_count, (lon + lon_count - 1) % lon_count
    has_south, has_north = lat > 0, lat < lat_count - 1
    beside = {-1: west, 0: lon, 1: east}
    cols = atmos_ref.shape[1]

    weight_copies = [
        pltpu.make_async_copy(ocean_weights_hbm, ocean_weights, local_sem.at[0]),
        pltpu.make_async_copy(atmos_weights_hbm, atmos_weights, local_sem.at[1]),
    ]
    for copy in weight_copies:
        copy.start()

    barrier = pltpu.get_barrier_semaphore()
    for step in range(1, lon_count):
        pl.semaphore_signal(
            barrier, inc=1, device_id=(lat, (lon + step) % lon_count), device_id_type=MESH
        )
    for band, there in ((-1, has_south), (1, has_north)):

        @pl.when(there)
        def _():
            for sector in (-1, 0, 1):
                pl.semaphore_signal(
                    barrier, inc=1, device_id=(lat + band, beside[sector]), device_id_type=MESH
                )

    pl.semaphore_wait(
        barrier, lon_count - 1 + 3 * has_south.astype(jnp.int32) + 3 * has_north.astype(jnp.int32)
    )

    numbers = {}

    def remote(name, source, target, device):
        number = numbers.setdefault(name, len(numbers))
        return pltpu.make_async_remote_copy(
            src_ref=source,
            dst_ref=target,
            send_sem=send_sem.at[number],
            recv_sem=recv_sem.at[number],
            device_id=device,
            device_id_type=MESH,
        )

    def each_neighbour(action):
        for band, there in ((-1, has_south), (0, None), (1, has_north)):
            for sector in (-1, 0, 1):
                if band == 0 and sector == 0:
                    continue
                if there is None:
                    action(band, sector)
                else:
                    pl.when(there)(functools.partial(action, band, sector))

    def field_copy(name, near, band, sector, waiting):
        own = near.at[4]
        return remote(
            (name, band, sector),
            own,
            near.at[(1 - band) * 3 + 1 - sector],
            (lat + band, beside[sector]),
        )

    def send_fields(name, near):
        each_neighbour(lambda band, sector: field_copy(name, near, band, sector, False).start())

    def await_fields(name, near):
        each_neighbour(
            lambda band, sector: remote(
                (name, -band, -sector),
                near.at[4],
                near.at[(1 + band) * 3 + 1 + sector],
                (lat + band, beside[sector]),
            ).wait_recv()
        )

    def fields(source, projection, near, masked):
        channels = source.shape[2]
        turned = projection[...]

        def one_block(block, carry):
            cells = source[pl.ds(2 * block, 2)].reshape(BCELLS, channels)
            values = dot(turned, cells, ((1,), (1,)))
            if masked:
                keep = jnp.concatenate(
                    [land_ref[pl.ds(2 * block, 1), :], land_ref[pl.ds(2 * block + 1, 1), :]], axis=1
                )
                values = values * keep.astype(jnp.float32)
            near[4, block] = values.astype(jnp.bfloat16)
            return carry

        lax.fori_loop(0, source.shape[0] // 2, one_block, 0, unroll=4)

    fields(atmos_ref, flux_map, near_atmos, False)
    send_fields("atmos_fields", near_atmos)
    fields(ocean_ref, surface_map, near_ocean, True)
    send_fields("ocean_fields", near_ocean)

    def remap(near, pairs, counts, weights, state, projection, target):
        source_count = near.shape[1]
        channels = state.shape[2]
        inject = projection[...]

        def one_block(block, carry):
            count = counts[0, block]
            picked = []
            for entry in range(PAIRS):
                number = pairs[entry, block]
                owner = number // source_count
                local = number - owner * source_count
                band = owner // lon_count
                sector = owner - band * lon_count - lon + 1 + lon_count
                sector = lax.rem(sector, lon_count)
                slot = jnp.clip((band - lat + 1) * 3 + sector, 0, 8)
                value = near[slot, local]
                if entry:
                    value = jnp.where(entry < count, value, jnp.zeros_like(value))
                picked.append(value)
            left = jnp.concatenate(picked, axis=1)
            mixed = dot(left, weights[block, 0].reshape(PAIRS * BCELLS, BCELLS))
            mixed = mixed.astype(jnp.bfloat16).astype(jnp.float32).T.astype(jnp.bfloat16)
            added = dot(mixed, inject)
            cells = state[pl.ds(2 * block, 2)].reshape(BCELLS, channels).astype(jnp.float32)
            target[pl.ds(2 * block, 2)] = (
                (cells + added).astype(jnp.bfloat16).reshape(2, state.shape[1], channels)
            )
            return carry

        lax.fori_loop(0, state.shape[0] // 2, one_block, 0, unroll=2)

    def edges(target, first, last):
        channels = target.shape[2]

        def one_tile(tile, carry):
            rows = target[pl.ds(4 * tile, 4)].astype(jnp.float32)
            first[tile] = to_tiles([rows[row, :EDGE] for row in range(4)])
            last[tile] = to_tiles([rows[row, cols - EDGE :] for row in range(4)])
            return carry

        lax.fori_loop(0, target.shape[0] // 4, one_tile, 0, unroll=2)

    def halo_copy(name, out, first, last, band, sector, to_neighbour):
        target, south, north, west_edge, east_edge = out
        rows = target.shape[0]
        tiles = rows // 4
        if sector == 0:
            source = target.at[rows - 3 : rows] if band == 1 else target.at[0:3]
            place = south if band == 1 else north
        else:
            edge = last if sector == 1 else first
            place = west_edge if sector == 1 else east_edge
            if band == 0:
                source, place = edge, place.at[1 : tiles + 1]
            elif band == 1:
                source, place = edge.at[tiles - 1], place.at[0]
            else:
                source, place = edge.at[0], place.at[tiles + 1]
        flip = 1 if to_neighbour else -1
        return remote(
            (name, band, sector), source, place, (lat + flip * band, beside[flip * sector])
        )

    def send_halo(name, out, first, last):
        each_neighbour(
            lambda band, sector: halo_copy(name, out, first, last, band, sector, True).start()
        )

    def await_halo(name, out, first, last):
        each_neighbour(
            lambda band, sector: halo_copy(name, out, first, last, -band, -sector, False).wait_recv()
        )

    def blank(out, at_north):
        target, south, north, west_edge, east_edge = out
        rim = north if at_north else south
        tile = target.shape[0] // 4 + 1 if at_north else 0
        rim[...] = jnp.zeros_like(rim)
        west_edge[tile] = jnp.zeros(west_edge.shape[1:], jnp.bfloat16)
        east_edge[tile] = jnp.zeros(east_edge.shape[1:], jnp.bfloat16)

    pl.when(jnp.logical_not(has_south))(lambda: blank(atmos_out, False))
    pl.when(jnp.logical_not(has_south))(lambda: blank(ocean_out, False))
    pl.when(jnp.logical_not(has_north))(lambda: blank(atmos_out, True))

    await_fields("atmos_fields", near_atmos)
    weight_copies[0].wait()
    remap(near_atmos, ocean_pairs, ocean_counts, ocean_weights, ocean_ref, flux_inject, ocean_out[0])
    edges(ocean_out[0], ocean_first, ocean_last)
    send_halo("ocean_halo", ocean_out, ocean_first, ocean_last)
    is_top = jnp.logical_not(has_north)
    top_at = ocean_out[0].shape[0] - 3

    def fold_copy(step, to_peer):
        flip = step if to_peer else lon_count - step
        return remote(
            ("fold", step),
            top_rows,
            circle_rows.at[:, pl.ds(pl.multiple_of(((lon if to_peer else (lon + flip) % lon_count)) * cols, 16), cols), :],
            (lat, (lon + flip) % lon_count),
        )

    @pl.when(is_top)
    def _():
        for row in range(3):
            top_rows[row] = ocean_out[0][top_at + 2 - row]
        for step in range(1, lon_count):
            fold_copy(step, True).start()
        own = pl.ds(pl.multiple_of(lon * cols, 16), cols)
        for row in range(3):
            circle_rows[row, own, :] = top_rows[row]

    await_fields("ocean_fields", near_ocean)
    weight_copies[1].wait()
    remap(near_ocean, atmos_pairs, atmos_counts, atmos_weights, atmos_ref, surface_inject, atmos_out[0])
    edges(atmos_out[0], atmos_first, atmos_last)
    send_halo("atmos_halo", atmos_out, atmos_first, atmos_last)

    @pl.when(is_top)
    def _():
        for step in range(1, lon_count):
            fold_copy(step, False).wait_recv()
        length = lon_count * cols
        partner = fold_ref[...]

        def chosen(first, count, repeat):
            place = lax.broadcasted_iota(jnp.int32, (count, length), 0)
            if repeat is not None:
                wanted = lax.rem(lon * cols + first + length + lax.rem(place, EDGE), length)
                live = place // EDGE == repeat
                return jnp.where(live & (partner == wanted), 1.0, 0.0).astype(jnp.bfloat16)
            return jnp.where(partner == lon * cols + place, 1.0, 0.0).astype(jnp.bfloat16)

        _, _, north, west_edge, east_edge = ocean_out
        tile = ocean_out[0].shape[0] // 4 + 1
        middle = chosen(0, cols, None)
        sides = [None, None]
        for row in range(3):
            line = circle_rows[row]
            north[row] = dot(middle, line).astype(jnp.bfloat16)
            for side, first in enumerate((-EDGE, cols)):
                part = dot(chosen(first, 16, row), line)
                sides[side] = part if row == 0 else sides[side] + part
        west_edge[tile] = sides[0].astype(jnp.bfloat16)
        east_edge[tile] = sides[1].astype(jnp.bfloat16)

    await_halo("ocean_halo", ocean_out, ocean_first, ocean_last)
    await_halo("atmos_halo", atmos_out, atmos_first, atmos_last)
    for name, near in (("atmos_fields", near_atmos), ("ocean_fields", near_ocean)):
        each_neighbour(
            lambda band, sector: field_copy(name, near, band, sector, False).wait_send()
        )
    for name, out, first, last in (
        ("ocean_halo", ocean_out, ocean_first, ocean_last),
        ("atmos_halo", atmos_out, atmos_first, atmos_last),
    ):
        each_neighbour(
            lambda band, sector: halo_copy(name, out, first, last, band, sector, True).wait_send()
        )

    @pl.when(is_top)
    def _():
        for step in range(1, lon_count):
            fold_copy(step, True).wait_send()


def front(
    atmos_state,
    ocean_state,
    land_sea,
    fold_partner,
    ocean_pairs,
    ocean_counts,
    ocean_weights,
    atmos_pairs,
    atmos_counts,
    atmos_weights,
    flux_map,
    surface_map,
    flux_inject,
    surface_inject,
):
    lat_count, lon_count = lax.axis_size("lat"), lax.axis_size("lon")
    vmem = pl.BlockSpec(memory_space=pltpu.VMEM)
    smem = pl.BlockSpec(memory_space=pltpu.SMEM)
    anywhere = pl.BlockSpec(memory_space=pl.ANY)

    def out_shapes(state):
        rows, cols, channels = state.shape
        return [
            jax.ShapeDtypeStruct(shape, jnp.bfloat16)
            for shape in (
                (rows, cols, channels),
                (3, cols, channels),
                (3, cols, channels),
                (rows // 4 + 2, 16, channels),
                (rows // 4 + 2, 16, channels),
            )
        ]

    def edge_scratch(state):
        return pltpu.VMEM((state.shape[0] // 4, 16, state.shape[2]), jnp.bfloat16)

    copies = 32 + lon_count - 1
    cols = atmos_state.shape[1]
    ocean_channels = ocean_state.shape[2]
    outs = pl.pallas_call(
        functools.partial(front_kernel, lat_count, lon_count),
        out_shape=tuple(out_shapes(atmos_state) + out_shapes(ocean_state)),
        in_specs=[vmem, vmem, vmem, vmem, smem, smem, anywhere, smem, smem, anywhere] + [vmem] * 4,
        out_specs=(vmem,) * 10,
        scratch_shapes=[
            pltpu.VMEM((9, atmos_state.shape[0] // 2, NFIELD, BCELLS), jnp.bfloat16),
            pltpu.VMEM((9, ocean_state.shape[0] // 2, NFIELD, BCELLS), jnp.bfloat16),
            pltpu.VMEM(ocean_weights.shape, jnp.bfloat16),
            pltpu.VMEM(atmos_weights.shape, jnp.bfloat16),
            edge_scratch(atmos_state),
            edge_scratch(atmos_state),
            edge_scratch(ocean_state),
            edge_scratch(ocean_state),
            pltpu.VMEM((3, cols, ocean_channels), jnp.bfloat16),
            pltpu.VMEM((3, lon_count * cols, ocean_channels), jnp.bfloat16),
            pltpu.SemaphoreType.DMA((copies,)),
            pltpu.SemaphoreType.DMA((copies,)),
            pltpu.SemaphoreType.DMA((2,)),
        ],
        compiler_params=pltpu.CompilerParams(
            collective_id=1, has_side_effects=True, vmem_limit_bytes=60 * 1024 * 1024
        ),
    )(
        atmos_state,
        ocean_state,
        land_sea,
        fold_partner.reshape(1, -1),
        ocean_pairs.reshape(-1, PAIRS).T,
        ocean_counts.T,
        ocean_weights,
        atmos_pairs.reshape(-1, PAIRS).T,
        atmos_counts.T,
        atmos_weights,
        flux_map.T,
        surface_map.T,
        flux_inject,
        surface_inject,
    )
    return outs[:5], outs[5:]


def shards(
    atmos_state,
    ocean_state,
    atmos_cotangent,
    ocean_cotangent,
    land_sea,
    fold_partner,
    ocean_pairs,
    ocean_counts,
    ocean_weights,
    atmos_pairs,
    atmos_counts,
    atmos_weights,
    flux_map,
    surface_map,
    flux_inject,
    surface_inject,
    atmos_kernel,
    atmos_gain,
    atmos_w_in,
    atmos_w_out,
    ocean_kernel,
    ocean_gain,
    ocean_w_in,
    ocean_w_out,
):
    atmos_halo, ocean_halo = front(
        atmos_state,
        ocean_state,
        land_sea,
        fold_partner,
        ocean_pairs,
        ocean_counts,
        ocean_weights,
        atmos_pairs,
        atmos_counts,
        atmos_weights,
        flux_map,
        surface_map,
        flux_inject,
        surface_inject,
    )
    states, packed, smalls = run_grids(
        atmos_halo,
        ocean_halo,
        land_sea,
        (atmos_cotangent, atmos_kernel, atmos_gain, atmos_w_in, atmos_w_out),
        (ocean_cotangent, ocean_kernel, ocean_gain, ocean_w_in, ocean_w_out),
    )
    outs = unpack(states, packed, smalls, (atmos_w_in.shape, ocean_w_in.shape))
    return (outs[0].reshape(atmos_state.shape), outs[1].reshape(ocean_state.shape), *outs[2:])


def solution(mesh):
    return jax.shard_map(
        shards,
        mesh=mesh,
        in_specs=(
            P("lat", "lon", None),
            P("lat", "lon", None),
            P("lat", "lon", None),
            P("lat", "lon", None),
            P("lat", "lon"),
            P(),
            P("lat", "lon", None),
            P("lat", "lon"),
            P("lat", "lon", None, None, None),
            P("lat", "lon", None),
            P("lat", "lon"),
            P("lat", "lon", None, None, None),
            P(),
            P(),
            P(),
            P(),
            P(),
            P(),
            P(),
            P(),
            P(),
            P(),
            P(),
            P(),
        ),
        out_specs=(
            P("lat", "lon", None),
            P("lat", "lon", None),
            P(),
            P(),
            P(),
            P(),
            P(),
            P(),
            P(),
            P(),
        ),
        check_vma=False,
    )
```

```python
import functools

import jax
import jax.numpy as jnp
from jax import lax
from jax.experimental import pallas as pl
from jax.experimental.pallas import tpu as pltpu
from jax.sharding import PartitionSpec as P

NFIELD = 16
BCELLS = 128
PAIRS = 4
LANES = 128
SMALL = 64
EDGE = 4
MESH = pl.DeviceIdType.MESH
epsilon = 1e-06
TANH_SCALE = 0.7978845608028654
TANH_CUBIC = 0.044715


def dot(left, right, dims=((1,), (0,))):
    return lax.dot_general(left, right, (dims, ((), ())), preferred_element_type=jnp.float32)


def shift_phase(halo, shifted, rows, cols):
    inner, south, north, west, east = halo

    def one_tile(tile, line_of, live):
        left = west[tile].astype(jnp.float32)
        right = east[tile].astype(jnp.float32)
        for slot in live:
            wide = jnp.concatenate(
                [
                    left[4 * slot : 4 * slot + 4],
                    line_of(slot).astype(jnp.float32),
                    right[4 * slot : 4 * slot + 4],
                ],
                axis=0,
            )
            for tap_col in range(7):
                shifted[tap_col, 4 * tile + slot - 1] = wide[tap_col + 1 : tap_col + 1 + cols].astype(
                    jnp.bfloat16
                )

    def middle_tile(tile, carry):
        one_tile(tile, lambda slot: inner[4 * tile + slot - 4], range(4))
        return carry

    one_tile(0, lambda slot: south[slot - 1], range(1, 4))
    lax.fori_loop(1, rows // 4 + 1, middle_tile, 0)
    one_tile(rows // 4 + 1, lambda slot: north[slot], range(3))


def conv_phase(shifted, kernel_ref, banded, conv, rows, cols, channels):
    pair_step = 8
    across = lax.broadcasted_iota(jnp.int32, (LANES, LANES), 0)
    down = lax.broadcasted_iota(jnp.int32, (LANES, LANES), 1)
    eye = across == down
    for lane in range(0, channels, LANES):
        for tap_col in range(7):
            for step in range(4):
                for low in range(2):
                    for out in range(2):
                        tap_row = 2 * step + low - out
                        if 0 <= tap_row < 7:
                            tap = kernel_ref[pl.ds(tap_row * 7 + tap_col, 1), lane : lane + LANES]
                            block = jnp.where(eye, tap, 0.0).astype(jnp.bfloat16)
                        else:
                            block = jnp.zeros((LANES, LANES), jnp.bfloat16)
                        banded[
                            tap_col * 4 + step,
                            low * LANES : low * LANES + LANES,
                            out * LANES : out * LANES + LANES,
                        ] = block

        def one_chunk(index, carry):
            total = None
            for tap_col in range(7):
                for step in range(4):
                    window = shifted[
                        tap_col,
                        pl.ds(2 * (index * pair_step + step), 2 * pair_step),
                        :,
                        lane : lane + LANES,
                    ].reshape(pair_step, 2, cols, LANES)
                    left = jnp.concatenate(
                        [
                            window[:, 0].reshape(pair_step * cols, LANES),
                            window[:, 1].reshape(pair_step * cols, LANES),
                        ],
                        axis=1,
                    )
                    part = dot(left, banded[tap_col * 4 + step])
                    total = part if total is None else total + part
            for out in range(2):
                conv[pl.ds(index * pair_step, pair_step), out, :, lane : lane + LANES] = total[
                    :, out * LANES : out * LANES + LANES
                ].reshape(pair_step, cols, LANES)
            return carry

        for index in range(rows // 2 // pair_step):
            lax.fori_loop(index, index + 1, one_chunk, 0)
            yield


def grid_work(
    halo, cot_ref, land_ref, kernel_ref, gain_ref, w_in_ref, w_out_ref, next_ref, packed_ref, banded, scratch
):
    taps, w_in_sum, w_out_sum, small_sum, shifted, conv, slope = scratch
    rows, cols, channels = halo[0].shape
    hidden_width = w_in_ref.shape[1]
    row_step = 8
    cells = row_step * cols
    chunk = 256
    shift_phase(halo, shifted, rows, cols)
    yield
    taps[...] = kernel_ref[...].astype(jnp.float32)
    yield from conv_phase(shifted, taps, banded, conv, rows, cols, channels)
    w_in_sum[...] = jnp.zeros_like(w_in_sum)
    w_out_sum[...] = jnp.zeros_like(w_out_sum)
    small_sum[...] = jnp.zeros_like(small_sum)
    gain = gain_ref[...].astype(jnp.float32)

    def one_block(index, gain_total):
        value = conv[pl.ds(index * (row_step // 2), row_step // 2)].reshape(cells, channels)
        centre = value - jnp.mean(value, axis=-1, keepdims=True)
        inv = lax.rsqrt(jnp.mean(centre * centre, axis=-1, keepdims=True) + epsilon)
        unit = centre * inv
        normed = (unit * gain).astype(jnp.bfloat16)
        where = pl.ds(index * cells, cells)
        upstream = cot_ref[where, :]
        if land_ref is not None:
            turned = land_ref[pl.ds(pl.multiple_of(index * row_step, 8), row_step), :].astype(jnp.float32).T
            keep = jnp.concatenate(
                [jnp.broadcast_to(turned[:, row : row + 1], (cols, channels)) for row in range(row_step)],
                axis=0,
            )
            upstream = upstream * keep.astype(jnp.bfloat16)
        normed_t = normed.T
        upstream_t = upstream.T
        update = None
        back = None
        for at in range(0, hidden_width, chunk):
            w_in = w_in_ref[:, at : at + chunk]
            w_out = w_out_ref[at : at + chunk, :]
            pre = dot(normed, w_in)
            grad_hidden = dot(upstream, w_out, ((1,), (1,)))
            square = pre * pre
            gate = 0.5 + 0.5 * jnp.tanh(pre * (TANH_SCALE + (TANH_SCALE * TANH_CUBIC) * square))
            active = pre * gate
            slope_part = 2 * TANH_SCALE + (6 * TANH_SCALE * TANH_CUBIC) * square
            grad_pre = (grad_hidden * (gate + active * (1.0 - gate) * slope_part)).astype(jnp.bfloat16)
            active = active.astype(jnp.bfloat16)
            part = dot(active, w_out)
            update = part if update is None else update + part
            part = dot(grad_pre, w_in, ((1,), (1,)))
            back = part if back is None else back + part
            for total, part in (
                (w_out_sum, dot(upstream_t, active)),
                (w_in_sum, dot(normed_t, grad_pre)),
            ):
                for lane in range(0, chunk, LANES):
                    total[(at + lane) // LANES] += part[:, lane : lane + LANES]
        inside = shifted[3, pl.ds(index * row_step + 3, row_step)].reshape(cells, channels)
        result = inside.astype(jnp.float32) + update
        if land_ref is not None:
            result = result * keep
        next_ref[where, :] = result.astype(jnp.bfloat16)
        gain_total = gain_total + jnp.sum((back * unit).reshape(cells // 8, 8, channels), axis=0)
        back = back * gain
        level = jnp.mean(back, axis=-1, keepdims=True)
        tilt = jnp.mean(back * unit, axis=-1, keepdims=True)
        slope[pl.ds(index * row_step, row_step)] = (
            (inv * (back - level - unit * tilt)).astype(jnp.bfloat16).reshape(row_step, cols, channels)
        )
        return gain_total

    blocks = rows // row_step
    gain_total = jnp.zeros((8, channels), jnp.float32)
    for start in range(0, blocks, 2):
        gain_total = lax.fori_loop(start, min(start + 2, blocks), one_block, gain_total)
        yield
    small_sum[49:50, :] = jnp.sum(gain_total, axis=0, keepdims=True)
    at_row = 0
    for total in (w_in_sum, w_out_sum):
        for block in range(hidden_width // LANES):
            packed_ref[at_row : at_row + channels, :] = total[block].astype(jnp.bfloat16)
            at_row += channels
    if at_row < packed_ref.shape[0]:
        spare = packed_ref.shape[0] - at_row
        packed_ref[at_row:, :] = jnp.zeros((spare, LANES), jnp.bfloat16)


def tap_work(packed_ref, scratch):
    small_sum, shifted, _, slope = scratch[3:]
    rows, cols, channels = slope.shape
    for lane in range(0, channels, LANES):
        for tap_row in range(7):

            def one_row(row, totals):
                grad = slope[row, :, lane : lane + LANES]
                sums = []
                for tap_col in range(7):
                    product = grad * shifted[tap_col, row + tap_row, :, lane : lane + LANES]
                    pieces = [product[at : at + 16] for at in range(0, cols, 16)]
                    while len(pieces) > 1:
                        pieces = [a + b for a, b in zip(pieces[::2], pieces[1::2])]
                    wide = pieces[0].astype(jnp.float32)
                    sums.append(totals[tap_col] + wide[:8] + wide[8:])
                return tuple(sums)

            totals = lax.fori_loop(
                0, rows, one_row, tuple(jnp.zeros((8, LANES), jnp.float32) for _ in range(7)), unroll=4
            )
            for tap_col in range(7):
                small_sum[pl.ds(tap_row * 7 + tap_col, 1), lane : lane + LANES] = jnp.sum(
                    totals[tap_col], axis=0, keepdims=True
                )
            yield
    for lane in range(0, channels, LANES):
        at_row = lane // LANES * SMALL
        packed_ref[at_row : at_row + SMALL, :] = small_sum[:, lane : lane + LANES].astype(jnp.bfloat16)


def grid_scratch(state, hidden_width):
    rows, cols, channels = state.shape
    return [
        pltpu.VMEM((49, channels), jnp.float32),
        pltpu.VMEM((hidden_width // LANES, channels, LANES), jnp.float32),
        pltpu.VMEM((hidden_width // LANES, channels, LANES), jnp.float32),
        pltpu.VMEM((SMALL, channels), jnp.float32),
        pltpu.VMEM((7, rows + 6, cols, channels), jnp.bfloat16),
        pltpu.VMEM((rows // 2, 2, cols, channels), jnp.float32),
        pltpu.VMEM((rows, cols, channels), jnp.bfloat16),
    ]


def packed_rows(channels, hidden_width, devices):
    rows = 2 * (hidden_width // LANES) * channels
    return rows + -rows % (16 * devices)


def unpack_kernel(widths, *refs):
    count = len(widths)
    states, outs = refs[:count], refs[3 * count :]
    for state, out in zip(states, outs[:count]):
        out[...] = state[...]
    outs = outs[count:]
    for number, (channels, hidden_width) in enumerate(widths):
        packed_ref, small_ref = refs[count + number], refs[2 * count + number]
        at = 0
        kernel_out, gain_out, w_in_out, w_out_out = outs[4 * number : 4 * number + 4]
        for block in range(hidden_width // LANES):
            w_in_out[:, block * LANES : block * LANES + LANES] = packed_ref[at : at + channels, :].astype(
                jnp.float32
            )
            at += channels
        for block in range(hidden_width // LANES):
            w_out_out[block * LANES : block * LANES + LANES, :] = (
                packed_ref[at : at + channels, :].astype(jnp.float32).T
            )
            at += channels
        for lane in range(0, channels, LANES):
            at = lane // LANES * SMALL
            small = small_ref[at : at + SMALL, :].astype(jnp.float32)
            kernel_out[:, lane : lane + LANES] = small[:49]
            gain_out[:, lane : lane + LANES] = small[49:50]


def unpack(states, packed, smalls, widths):
    shapes = []
    for channels, hidden_width in widths:
        shapes += [(49, channels), (1, channels), (channels, hidden_width), (hidden_width, channels)]
    vmem = pl.BlockSpec(memory_space=pltpu.VMEM)
    outs = pl.pallas_call(
        functools.partial(unpack_kernel, widths),
        out_shape=(
            *(jax.ShapeDtypeStruct(state.shape, state.dtype) for state in states),
            *(jax.ShapeDtypeStruct(shape, jnp.float32) for shape in shapes),
        ),
        in_specs=[vmem] * (3 * len(widths)),
        out_specs=(vmem,) * (len(states) + len(shapes)),
        compiler_params=pltpu.CompilerParams(vmem_limit_bytes=60 * 1024 * 1024),
    )(*states, *packed, *smalls)
    return [out.reshape(-1) if out.shape[0] == 1 else out for out in outs]


def aligned(index):
    return pl.multiple_of(index, 16)


def greet(partners):
    barrier = pltpu.get_barrier_semaphore()
    for partner in partners:
        pl.semaphore_signal(barrier, inc=1, device_id=partner, device_id_type=MESH)
    return lambda: pl.semaphore_wait(barrier, len(partners))


def sum_plan(lon_count):
    spans = []
    span = 2
    while span < lon_count:
        spans.append(span)
        span *= 2
    return (spans, spans[::-1])


def sum_work(lat_count, lon_count, share_ref, full_ref, scratch):
    length = share_ref.shape[0]
    plan = sum_plan(lon_count)
    steps = len(plan[0])
    half, quarter = length // 2, length // 4
    first, lat_send, lat_recv, comb = scratch[:4]
    sends = [scratch[4 + part * steps : 4 + part * steps + steps] for part in range(2)]
    recvs = [scratch[4 + (2 + part) * steps : 4 + (2 + part) * steps + steps] for part in range(2)]
    totals = [scratch[4 + (4 + part) * steps : 4 + (4 + part) * steps + steps] for part in range(2)]
    send_sem, recv_sem = scratch[-2:]
    lat, lon = lax.axis_index("lat"), lax.axis_index("lon")
    core = lon % 2

    def flipped(span):
        bit = (lon // span) % 2
        return (lat, lon + span - 2 * span * bit), bit

    peers = [((lat + step) % lat_count, lon) for step in range(1, lat_count)]
    push = pusher(send_sem, recv_sem)
    pending = []
    opening = []
    for part in range(2):
        opening.append(
            push(
                share_ref.at[pl.ds(aligned((1 - core) * half + part * quarter), quarter), :],
                first.at[part],
                flipped(1)[0],
            )
        )
    active = [None, None]
    yield
    for part in range(2):
        opening[part].wait_recv()
        pending.append(opening[part])
        device, bit = flipped(plan[part][0])
        size = quarter // 2
        own = core * half + part * quarter

        def summed(start):
            return share_ref[pl.ds(aligned(own + start), size), :].astype(jnp.float32) + first[
                part, pl.ds(aligned(start), size), :
            ].astype(jnp.float32)

        sends[part][0][...] = summed((1 - bit) * size).astype(jnp.bfloat16)
        active[part] = push(sends[part][0], recvs[part][0], device)
        totals[part][0][...] = summed(bit * size)
    size = quarter // 2
    for step in range(steps):
        yield
        for part in range(2):
            active[part].wait_recv()
            pending.append(active[part])
            recv, total = recvs[part][step], totals[part][step]
            if step + 1 == steps:
                comb[part * size : part * size + size, :] = total[...] + recv[...].astype(jnp.float32)
                continue
            device, bit = flipped(plan[part][step + 1])
            rest = size // 2

            def joined(start):
                where = pl.ds(aligned(start), rest)
                return total[where, :] + recv[where, :].astype(jnp.float32)

            sends[part][step + 1][...] = joined((1 - bit) * rest).astype(jnp.bfloat16)
            active[part] = push(sends[part][step + 1], recvs[part][step + 1], device)
            totals[part][step + 1][...] = joined(bit * rest)
        if step + 1 < steps:
            size //= 2
    bases = []
    for part in range(2):
        base = core * half + part * quarter
        extent = quarter
        levels = []
        for span in plan[part]:
            extent //= 2
            base = base + ((lon // span) % 2) * extent
            levels.append((base, extent, span))
        bases.append(levels)
    chunk = 2 * size // lat_count
    lat_send[...] = comb[...].astype(jnp.bfloat16)
    arriving = []
    for step in range(1, lat_count):
        peer = (lat + step) % lat_count
        arriving.append(
            push(
                lat_send.at[pl.ds(aligned(peer * chunk), chunk), :],
                lat_recv.at[step - 1],
                (peer, lon),
            )
        )
    yield
    total = comb[pl.ds(aligned(lat * chunk), chunk), :]
    for step, copy in enumerate(arriving):
        copy.wait_recv()
        pending.append(copy)
        total = total + lat_recv[step].astype(jnp.float32)
    upper = (2 * lat) // lat_count
    low_base, high_base = bases[0][-1][0], bases[1][-1][0]
    place = low_base + upper * (high_base - low_base) + (lat - upper * (lat_count // 2)) * chunk
    mine = pl.ds(aligned(place), chunk)
    full_ref[mine, :] = total.astype(jnp.bfloat16)
    arriving = [push(full_ref.at[mine, :], full_ref.at[mine, :], peer) for peer in peers]
    yield
    for copy in arriving:
        copy.wait_recv()
        pending.append(copy)
    for step in reversed(range(steps)):
        arriving = []
        for part in range(2):
            base, extent, span = bases[part][step]
            region = full_ref.at[pl.ds(aligned(base), extent), :]
            arriving.append(push(region, region, flipped(span)[0]))
        yield
        for copy in arriving:
            copy.wait_recv()
            pending.append(copy)
    arriving = []
    for part in range(2):
        region = full_ref.at[pl.ds(aligned(core * half + part * quarter), quarter), :]
        arriving.append(push(region, region, flipped(1)[0]))
    yield
    for copy in arriving:
        copy.wait_recv()
        pending.append(copy)
    for copy in pending:
        copy.wait_send()


def sum_scratch(length, lat_count, lon_count):
    steps = len(sum_plan(lon_count)[0])
    sizes = [length // 4 // 2 ** (step + 1) for step in range(steps)]
    chunk = 2 * sizes[-1] // lat_count
    copies = 2 + 2 * steps + (lat_count - 1) * 2 + 2 * steps + 2
    narrow = [pltpu.VMEM((size, LANES), jnp.bfloat16) for size in sizes]
    wide = [pltpu.VMEM((size, LANES), jnp.float32) for size in sizes]
    return [
        pltpu.VMEM((2, length // 4, LANES), jnp.bfloat16),
        pltpu.VMEM((2 * sizes[-1], LANES), jnp.bfloat16),
        pltpu.VMEM((lat_count - 1, chunk, LANES), jnp.bfloat16),
        pltpu.VMEM((2 * sizes[-1], LANES), jnp.float32),
        *(narrow * 4),
        *(wide * 2),
        pltpu.SemaphoreType.DMA((copies,)),
        pltpu.SemaphoreType.DMA((copies,)),
    ]


def pusher(send_sem, recv_sem):
    count = [0]

    def push(source, target, device):
        number = count[0]
        count[0] += 1
        copy = pltpu.make_async_remote_copy(
            src_ref=source,
            dst_ref=target,
            send_sem=send_sem.at[number],
            recv_sem=recv_sem.at[number],
            device_id=device,
            device_id_type=MESH,
        )
        copy.start()
        return copy

    return push


def flat_work(lat_count, lon_count, share_ref, full_ref, scratch):
    lon_recv, lat_send, lat_recv, send_sem, recv_sem = scratch
    lat, lon = lax.axis_index("lat"), lax.axis_index("lon")
    push = pusher(send_sem, recv_sem)
    chunk = share_ref.shape[0] // lon_count
    part = chunk // lat_count
    lons = [(lon + step) % lon_count for step in range(1, lon_count)]
    lats = [(lat + step) % lat_count for step in range(1, lat_count)]
    done = []
    copies = [
        push(share_ref.at[pl.ds(aligned(peer * chunk), chunk), :], lon_recv.at[step], (lat, peer))
        for step, peer in enumerate(lons)
    ]
    yield
    total = share_ref[pl.ds(aligned(lon * chunk), chunk), :].astype(jnp.float32)
    for step, copy in enumerate(copies):
        copy.wait_recv()
        total = total + lon_recv[step].astype(jnp.float32)
    done += copies
    lat_send[...] = total.astype(jnp.bfloat16)
    copies = [
        push(lat_send.at[pl.ds(aligned(peer * part), part), :], lat_recv.at[step], (peer, lon))
        for step, peer in enumerate(lats)
    ]
    yield
    total = lat_send[pl.ds(aligned(lat * part), part), :].astype(jnp.float32)
    for step, copy in enumerate(copies):
        copy.wait_recv()
        total = total + lat_recv[step].astype(jnp.float32)
    done += copies
    mine = pl.ds(aligned(lon * chunk + lat * part), part)
    full_ref[mine, :] = total.astype(jnp.bfloat16)
    copies = [push(full_ref.at[mine, :], full_ref.at[mine, :], (peer, lon)) for peer in lats]
    yield
    for copy in copies:
        copy.wait_recv()
    done += copies
    region = pl.ds(aligned(lon * chunk), chunk)
    copies = [push(full_ref.at[region, :], full_ref.at[region, :], (lat, peer)) for peer in lons]
    yield
    for copy in copies:
        copy.wait_recv()
    done += copies
    for copy in done:
        copy.wait_send()


def flat_scratch(length, lat_count, lon_count):
    chunk = length // lon_count
    copies = 2 * (lat_count + lon_count - 2)
    return [
        pltpu.VMEM((lon_count - 1, chunk, LANES), jnp.bfloat16),
        pltpu.VMEM((chunk, LANES), jnp.bfloat16),
        pltpu.VMEM((lat_count - 1, chunk // lat_count, LANES), jnp.bfloat16),
        pltpu.SemaphoreType.DMA((copies,)),
        pltpu.SemaphoreType.DMA((copies,)),
    ]


def small_work(lat_count, lon_count, share_ref, full_ref, scratch):
    lon_terms, lat_terms, middle, send_sem, recv_sem = scratch
    lat, lon = lax.axis_index("lat"), lax.axis_index("lon")
    push = pusher(send_sem, recv_sem)
    copies = []
    for step in range(1, lon_count):
        copies.append(push(share_ref, lon_terms.at[lon], (lat, (lon + step) % lon_count)))
    lon_terms[lon] = share_ref[...]
    yield
    for copy in copies:
        copy.wait_recv()
    total = lon_terms[0].astype(jnp.float32)
    for term in range(1, lon_count):
        total = total + lon_terms[term].astype(jnp.float32)
    middle[...] = total.astype(jnp.bfloat16)
    for step in range(1, lat_count):
        copies.append(push(middle, lat_terms.at[lat], ((lat + step) % lat_count, lon)))
    lat_terms[lat] = middle[...]
    yield
    for copy in copies[lon_count - 1 :]:
        copy.wait_recv()
    total = lat_terms[0].astype(jnp.float32)
    for term in range(1, lat_count):
        total = total + lat_terms[term].astype(jnp.float32)
    full_ref[...] = total.astype(jnp.bfloat16)
    for copy in copies:
        copy.wait_send()


def small_scratch(length, lat_count, lon_count):
    copies = lat_count + lon_count - 2
    return [
        pltpu.VMEM((lon_count, length, LANES), jnp.bfloat16),
        pltpu.VMEM((lat_count, length, LANES), jnp.bfloat16),
        pltpu.VMEM((length, LANES), jnp.bfloat16),
        pltpu.SemaphoreType.DMA((copies,)),
        pltpu.SemaphoreType.DMA((copies,)),
    ]


def grids_kernel(lat_count, lon_count, sizes, *refs):
    atmos_halo, ocean_halo = refs[:5], refs[5:10]
    atmos_args, ocean_args, land = refs[10:15], refs[15:20], refs[20]
    atmos_next, ocean_next, atmos_full, ocean_full, atmos_small, ocean_small = refs[21:27]
    rest = list(refs[27:])
    parts = []
    for size in sizes:
        parts.append(rest[:size])
        rest = rest[size:]
    atmos_part, ocean_part, atmos_sum, ocean_sum, atmos_small_sum, ocean_small_sum = parts
    banded, atmos_share, ocean_share, atmos_few, ocean_few = rest
    lat, lon = lax.axis_index("lat"), lax.axis_index("lon")
    met = greet(
        [((lat + step) % lat_count, lon) for step in range(1, lat_count)]
        + [(lat, (lon + step) % lon_count) for step in range(1, lon_count)]
    )

    def along(work, *plan):
        for number, _ in enumerate(work):
            for sums, places in plan:
                if number in places:
                    next(sums, None)

    def begin(work, *args):
        sums = work(lat_count, lon_count, *args)
        next(sums)
        return sums

    def first_part(halo, args, mask, result, share, part):
        cot, kernel, gain, w_in, w_out = args
        return grid_work(halo, cot, mask, kernel, gain, w_in, w_out, result, share, banded, part)

    along(first_part(atmos_halo, atmos_args, None, atmos_next, atmos_share, atmos_part))
    met()
    first = begin(sum_work, atmos_share, atmos_full, atmos_sum)
    along(
        first_part(ocean_halo, ocean_args, land, ocean_next, ocean_share, ocean_part),
        (first, (1, 3, 4, 5, 6)),
    )
    second = begin(flat_work, ocean_share, ocean_full, ocean_sum)
    along(tap_work(atmos_few, atmos_part), (first, (4, 10)), (second, (6, 12)))
    third = begin(small_work, atmos_few, atmos_small, atmos_small_sum)
    along(tap_work(ocean_few, ocean_part), (first, (1,)), (second, (3, 6)), (third, (4, 6)))
    last = begin(small_work, ocean_few, ocean_small, ocean_small_sum)
    for sums in (first, second, third, last):
        for _ in sums:
            pass


def run_grids(atmos_halo, ocean_halo, land_sea, atmos_args, ocean_args):
    lat_count, lon_count = lax.axis_size("lat"), lax.axis_size("lon")
    vmem = pl.BlockSpec(memory_space=pltpu.VMEM)
    flat, states, shares, smalls, parts = [], [], [], [], []
    for cotangent, kernel, gain, w_in, w_out in (atmos_args, ocean_args):
        rows, cols, channels = cotangent.shape
        flat += [cotangent.reshape(rows * cols, channels), kernel, gain.reshape(1, channels), w_in, w_out]
        states.append((rows * cols, channels))
        shares.append((packed_rows(*w_in.shape, lat_count * lon_count), LANES))
        smalls.append((channels // LANES * SMALL, LANES))
        parts.append(grid_scratch(cotangent, w_in.shape[1]))
    parts.append(sum_scratch(shares[0][0], lat_count, lon_count))
    parts.append(flat_scratch(shares[1][0], lat_count, lon_count))
    parts += [small_scratch(small[0], lat_count, lon_count) for small in smalls]
    narrow = shares + smalls
    args = (*atmos_halo, *ocean_halo, *flat, land_sea)
    outs = pl.pallas_call(
        functools.partial(grids_kernel, lat_count, lon_count, tuple(len(part) for part in parts)),
        out_shape=tuple(jax.ShapeDtypeStruct(shape, jnp.bfloat16) for shape in states + narrow),
        in_specs=[vmem] * len(args),
        out_specs=(vmem,) * (len(states) + len(narrow)),
        scratch_shapes=[
            *(piece for part in parts for piece in part),
            pltpu.VMEM((28, 2 * LANES, 2 * LANES), jnp.bfloat16),
            *(pltpu.VMEM(shape, jnp.bfloat16) for shape in narrow),
        ],
        compiler_params=pltpu.CompilerParams(
            collective_id=2, has_side_effects=True, vmem_limit_bytes=60 * 1024 * 1024
        ),
    )(*args)
    return outs[:2], outs[2:4], outs[4:]


def to_tiles(pieces):
    return jnp.concatenate([piece.astype(jnp.float32) for piece in pieces], axis=0).astype(jnp.bfloat16)


def front_kernel(lat_count, lon_count, *refs):
    (
        atmos_ref,
        ocean_ref,
        land_ref,
        fold_ref,
        ocean_pairs,
        ocean_counts,
        ocean_weights_hbm,
        atmos_pairs,
        atmos_counts,
        atmos_weights_hbm,
        flux_map,
        surface_map,
        flux_inject,
        surface_inject,
    ) = refs[:14]
    atmos_out, ocean_out = refs[14:19], refs[19:24]
    (
        near_atmos,
        near_ocean,
        ocean_weights,
        atmos_weights,
        atmos_first,
        atmos_last,
        ocean_first,
        ocean_last,
        top_rows,
        circle_rows,
        send_sem,
        recv_sem,
        local_sem,
    ) = refs[24:]
    lat, lon = lax.axis_index("lat"), lax.axis_index("lon")
    east, west = (lon + 1) % lon_count, (lon + lon_count - 1) % lon_count
    has_south, has_north = lat > 0, lat < lat_count - 1
    beside = {-1: west, 0: lon, 1: east}
    cols = atmos_ref.shape[1]

    weight_copies = [
        pltpu.make_async_copy(ocean_weights_hbm, ocean_weights, local_sem.at[0]),
        pltpu.make_async_copy(atmos_weights_hbm, atmos_weights, local_sem.at[1]),
    ]
    for copy in weight_copies:
        copy.start()

    barrier = pltpu.get_barrier_semaphore()
    for step in range(1, lon_count):
        pl.semaphore_signal(
            barrier, inc=1, device_id=(lat, (lon + step) % lon_count), device_id_type=MESH
        )
    for band, there in ((-1, has_south), (1, has_north)):

        @pl.when(there)
        def _():
            for sector in (-1, 0, 1):
                pl.semaphore_signal(
                    barrier, inc=1, device_id=(lat + band, beside[sector]), device_id_type=MESH
                )

    numbers = {}

    def remote(name, source, target, device):
        number = numbers.setdefault(name, len(numbers))
        return pltpu.make_async_remote_copy(
            src_ref=source,
            dst_ref=target,
            send_sem=send_sem.at[number],
            recv_sem=recv_sem.at[number],
            device_id=device,
            device_id_type=MESH,
        )

    def each_neighbour(action):
        for band, there in ((-1, has_south), (0, None), (1, has_north)):
            for sector in (-1, 0, 1):
                if band == 0 and sector == 0:
                    continue
                if there is None:
                    action(band, sector)
                else:
                    pl.when(there)(functools.partial(action, band, sector))

    def field_copy(name, near, band, sector, waiting):
        own = near.at[4]
        return remote(
            (name, band, sector),
            own,
            near.at[(1 - band) * 3 + 1 - sector],
            (lat + band, beside[sector]),
        )

    def send_fields(name, near):
        each_neighbour(lambda band, sector: field_copy(name, near, band, sector, False).start())

    def await_fields(name, near):
        each_neighbour(
            lambda band, sector: remote(
                (name, -band, -sector),
                near.at[4],
                near.at[(1 + band) * 3 + 1 + sector],
                (lat + band, beside[sector]),
            ).wait_recv()
        )

    def fields(source, projection, near, masked):
        channels = source.shape[2]
        turned = projection[...]

        def one_block(block, carry):
            cells = source[pl.ds(2 * block, 2)].reshape(BCELLS, channels)
            values = dot(turned, cells, ((1,), (1,)))
            if masked:
                keep = jnp.concatenate(
                    [land_ref[pl.ds(2 * block, 1), :], land_ref[pl.ds(2 * block + 1, 1), :]], axis=1
                )
                values = values * keep.astype(jnp.float32)
            near[4, block] = values.astype(jnp.bfloat16)
            return carry

        lax.fori_loop(0, source.shape[0] // 2, one_block, 0, unroll=8)

    fields(atmos_ref, flux_map, near_atmos, False)
    pl.semaphore_wait(
        barrier, lon_count - 1 + 3 * has_south.astype(jnp.int32) + 3 * has_north.astype(jnp.int32)
    )
    send_fields("atmos_fields", near_atmos)
    fields(ocean_ref, surface_map, near_ocean, True)
    send_fields("ocean_fields", near_ocean)

    def remap(near, pairs, counts, weights, state, projection, target):
        source_count = near.shape[1]
        channels = state.shape[2]
        inject = projection[...]

        def one_block(block, carry):
            count = counts[0, block]
            picked = []
            for entry in range(PAIRS):
                number = pairs[entry, block]
                owner = lax.div(number, source_count)
                local = number - owner * source_count
                band = lax.div(owner, lon_count)
                sector = owner - band * lon_count - lon + 1 + lon_count
                sector = lax.rem(sector, lon_count)
                slot = jnp.clip((band - lat + 1) * 3 + sector, 0, 8)
                value = near[slot, local]
                if entry:
                    value = jnp.where(entry < count, value, jnp.zeros_like(value))
                picked.append(value)
            left = jnp.concatenate(picked, axis=1)
            mixed = dot(left, weights[block, 0].reshape(PAIRS * BCELLS, BCELLS))
            mixed = mixed.astype(jnp.bfloat16).astype(jnp.float32).T.astype(jnp.bfloat16)
            added = dot(mixed, inject)
            cells = state[pl.ds(2 * block, 2)].reshape(BCELLS, channels).astype(jnp.float32)
            target[pl.ds(2 * block, 2)] = (
                (cells + added).astype(jnp.bfloat16).reshape(2, state.shape[1], channels)
            )
            return carry

        lax.fori_loop(0, state.shape[0] // 2, one_block, 0, unroll=8)

    def edges(target, first, last):
        channels = target.shape[2]

        def one_tile(tile, carry):
            rows = target[pl.ds(4 * tile, 4)].astype(jnp.float32)
            first[tile] = to_tiles([rows[row, :EDGE] for row in range(4)])
            last[tile] = to_tiles([rows[row, cols - EDGE :] for row in range(4)])
            return carry

        lax.fori_loop(0, target.shape[0] // 4, one_tile, 0, unroll=4)

    def halo_copy(name, out, first, last, band, sector, to_neighbour):
        target, south, north, west_edge, east_edge = out
        rows = target.shape[0]
        tiles = rows // 4
        if sector == 0:
            source = target.at[rows - 3 : rows] if band == 1 else target.at[0:3]
            place = south if band == 1 else north
        else:
            edge = last if sector == 1 else first
            place = west_edge if sector == 1 else east_edge
            if band == 0:
                source, place = edge, place.at[1 : tiles + 1]
            elif band == 1:
                source, place = edge.at[tiles - 1], place.at[0]
            else:
                source, place = edge.at[0], place.at[tiles + 1]
        flip = 1 if to_neighbour else -1
        return remote(
            (name, band, sector), source, place, (lat + flip * band, beside[flip * sector])
        )

    def send_halo(name, out, first, last):
        each_neighbour(
            lambda band, sector: halo_copy(name, out, first, last, band, sector, True).start()
        )

    def await_halo(name, out, first, last):
        each_neighbour(
            lambda band, sector: halo_copy(name, out, first, last, -band, -sector, False).wait_recv()
        )

    def blank(out, at_north):
        target, south, north, west_edge, east_edge = out
        rim = north if at_north else south
        tile = target.shape[0] // 4 + 1 if at_north else 0
        rim[...] = jnp.zeros_like(rim)
        west_edge[tile] = jnp.zeros(west_edge.shape[1:], jnp.bfloat16)
        east_edge[tile] = jnp.zeros(east_edge.shape[1:], jnp.bfloat16)

    pl.when(jnp.logical_not(has_south))(lambda: blank(atmos_out, False))
    pl.when(jnp.logical_not(has_south))(lambda: blank(ocean_out, False))
    pl.when(jnp.logical_not(has_north))(lambda: blank(atmos_out, True))

    await_fields("atmos_fields", near_atmos)
    weight_copies[0].wait()
    remap(near_atmos, ocean_pairs, ocean_counts, ocean_weights, ocean_ref, flux_inject, ocean_out[0])
    edges(ocean_out[0], ocean_first, ocean_last)
    send_halo("ocean_halo", ocean_out, ocean_first, ocean_last)
    is_top = jnp.logical_not(has_north)
    top_at = ocean_out[0].shape[0] - 3

    def fold_copy(step, to_peer):
        flip = step if to_peer else lon_count - step
        return remote(
            ("fold", step),
            top_rows,
            circle_rows.at[:, pl.ds(pl.multiple_of(((lon if to_peer else (lon + flip) % lon_count)) * cols, 16), cols), :],
            (lat, (lon + flip) % lon_count),
        )

    @pl.when(is_top)
    def _():
        for row in range(3):
            top_rows[row] = ocean_out[0][top_at + 2 - row]
        for step in range(1, lon_count):
            fold_copy(step, True).start()
        own = pl.ds(pl.multiple_of(lon * cols, 16), cols)
        for row in range(3):
            circle_rows[row, own, :] = top_rows[row]

    await_fields("ocean_fields", near_ocean)
    weight_copies[1].wait()
    remap(near_ocean, atmos_pairs, atmos_counts, atmos_weights, atmos_ref, surface_inject, atmos_out[0])
    edges(atmos_out[0], atmos_first, atmos_last)
    send_halo("atmos_halo", atmos_out, atmos_first, atmos_last)

    @pl.when(is_top)
    def _():
        for step in range(1, lon_count):
            fold_copy(step, False).wait_recv()
        length = lon_count * cols
        partner = fold_ref[...]

        def chosen(first, count, repeat):
            place = lax.broadcasted_iota(jnp.int32, (count, length), 0)
            if repeat is not None:
                wanted = lax.rem(lon * cols + first + length + lax.rem(place, EDGE), length)
                live = place // EDGE == repeat
                return jnp.where(live & (partner == wanted), 1.0, 0.0).astype(jnp.bfloat16)
            return jnp.where(partner == lon * cols + place, 1.0, 0.0).astype(jnp.bfloat16)

        _, _, north, west_edge, east_edge = ocean_out
        tile = ocean_out[0].shape[0] // 4 + 1
        middle = chosen(0, cols, None)
        sides = [None, None]
        for row in range(3):
            line = circle_rows[row]
            north[row] = dot(middle, line).astype(jnp.bfloat16)
            for side, first in enumerate((-EDGE, cols)):
                part = dot(chosen(first, 16, row), line)
                sides[side] = part if row == 0 else sides[side] + part
        west_edge[tile] = sides[0].astype(jnp.bfloat16)
        east_edge[tile] = sides[1].astype(jnp.bfloat16)

    await_halo("ocean_halo", ocean_out, ocean_first, ocean_last)
    await_halo("atmos_halo", atmos_out, atmos_first, atmos_last)
    for name, near in (("atmos_fields", near_atmos), ("ocean_fields", near_ocean)):
        each_neighbour(
            lambda band, sector: field_copy(name, near, band, sector, False).wait_send()
        )
    for name, out, first, last in (
        ("ocean_halo", ocean_out, ocean_first, ocean_last),
        ("atmos_halo", atmos_out, atmos_first, atmos_last),
    ):
        each_neighbour(
            lambda band, sector: halo_copy(name, out, first, last, band, sector, True).wait_send()
        )

    @pl.when(is_top)
    def _():
        for step in range(1, lon_count):
            fold_copy(step, True).wait_send()


def front(
    atmos_state,
    ocean_state,
    land_sea,
    fold_partner,
    ocean_pairs,
    ocean_counts,
    ocean_weights,
    atmos_pairs,
    atmos_counts,
    atmos_weights,
    flux_map,
    surface_map,
    flux_inject,
    surface_inject,
):
    lat_count, lon_count = lax.axis_size("lat"), lax.axis_size("lon")
    vmem = pl.BlockSpec(memory_space=pltpu.VMEM)
    smem = pl.BlockSpec(memory_space=pltpu.SMEM)
    anywhere = pl.BlockSpec(memory_space=pl.ANY)

    def out_shapes(state):
        rows, cols, channels = state.shape
        return [
            jax.ShapeDtypeStruct(shape, jnp.bfloat16)
            for shape in (
                (rows, cols, channels),
                (3, cols, channels),
                (3, cols, channels),
                (rows // 4 + 2, 16, channels),
                (rows // 4 + 2, 16, channels),
            )
        ]

    def edge_scratch(state):
        return pltpu.VMEM((state.shape[0] // 4, 16, state.shape[2]), jnp.bfloat16)

    copies = 32 + lon_count - 1
    cols = atmos_state.shape[1]
    ocean_channels = ocean_state.shape[2]
    outs = pl.pallas_call(
        functools.partial(front_kernel, lat_count, lon_count),
        out_shape=tuple(out_shapes(atmos_state) + out_shapes(ocean_state)),
        in_specs=[vmem, vmem, vmem, vmem, smem, smem, anywhere, smem, smem, anywhere] + [vmem] * 4,
        out_specs=(vmem,) * 10,
        scratch_shapes=[
            pltpu.VMEM((9, atmos_state.shape[0] // 2, NFIELD, BCELLS), jnp.bfloat16),
            pltpu.VMEM((9, ocean_state.shape[0] // 2, NFIELD, BCELLS), jnp.bfloat16),
            pltpu.VMEM(ocean_weights.shape, jnp.bfloat16),
            pltpu.VMEM(atmos_weights.shape, jnp.bfloat16),
            edge_scratch(atmos_state),
            edge_scratch(atmos_state),
            edge_scratch(ocean_state),
            edge_scratch(ocean_state),
            pltpu.VMEM((3, cols, ocean_channels), jnp.bfloat16),
            pltpu.VMEM((3, lon_count * cols, ocean_channels), jnp.bfloat16),
            pltpu.SemaphoreType.DMA((copies,)),
            pltpu.SemaphoreType.DMA((copies,)),
            pltpu.SemaphoreType.DMA((2,)),
        ],
        compiler_params=pltpu.CompilerParams(
            collective_id=1, has_side_effects=True, vmem_limit_bytes=60 * 1024 * 1024
        ),
    )(
        atmos_state,
        ocean_state,
        land_sea,
        fold_partner.reshape(1, -1),
        ocean_pairs.reshape(-1, PAIRS).T,
        ocean_counts.T,
        ocean_weights,
        atmos_pairs.reshape(-1, PAIRS).T,
        atmos_counts.T,
        atmos_weights,
        flux_map.T,
        surface_map.T,
        flux_inject,
        surface_inject,
    )
    return outs[:5], outs[5:]


def shards(
    atmos_state,
    ocean_state,
    atmos_cotangent,
    ocean_cotangent,
    land_sea,
    fold_partner,
    ocean_pairs,
    ocean_counts,
    ocean_weights,
    atmos_pairs,
    atmos_counts,
    atmos_weights,
    flux_map,
    surface_map,
    flux_inject,
    surface_inject,
    atmos_kernel,
    atmos_gain,
    atmos_w_in,
    atmos_w_out,
    ocean_kernel,
    ocean_gain,
    ocean_w_in,
    ocean_w_out,
):
    atmos_halo, ocean_halo = front(
        atmos_state,
        ocean_state,
        land_sea,
        fold_partner,
        ocean_pairs,
        ocean_counts,
        ocean_weights,
        atmos_pairs,
        atmos_counts,
        atmos_weights,
        flux_map,
        surface_map,
        flux_inject,
        surface_inject,
    )
    states, packed, smalls = run_grids(
        atmos_halo,
        ocean_halo,
        land_sea,
        (atmos_cotangent, atmos_kernel, atmos_gain, atmos_w_in, atmos_w_out),
        (ocean_cotangent, ocean_kernel, ocean_gain, ocean_w_in, ocean_w_out),
    )
    outs = unpack(states, packed, smalls, (atmos_w_in.shape, ocean_w_in.shape))
    return (outs[0].reshape(atmos_state.shape), outs[1].reshape(ocean_state.shape), *outs[2:])


def solution(mesh):
    return jax.shard_map(
        shards,
        mesh=mesh,
        in_specs=(
            P("lat", "lon", None),
            P("lat", "lon", None),
            P("lat", "lon", None),
            P("lat", "lon", None),
            P("lat", "lon"),
            P(),
            P("lat", "lon", None),
            P("lat", "lon"),
            P("lat", "lon", None, None, None),
            P("lat", "lon", None),
            P("lat", "lon"),
            P("lat", "lon", None, None, None),
            P(),
            P(),
            P(),
            P(),
            P(),
            P(),
            P(),
            P(),
            P(),
            P(),
            P(),
            P(),
        ),
        out_specs=(
            P("lat", "lon", None),
            P("lat", "lon", None),
            P(),
            P(),
            P(),
            P(),
            P(),
            P(),
            P(),
            P(),
        ),
        check_vma=False,
    )
```

```python
import functools

import jax
import jax.numpy as jnp
from jax import lax
from jax.experimental import pallas as pl
from jax.experimental.pallas import tpu as pltpu
from jax.sharding import PartitionSpec as P

NFIELD = 16
BCELLS = 128
PAIRS = 4
LANES = 128
SMALL = 64
EDGE = 4
MESH = pl.DeviceIdType.MESH
epsilon = 1e-06
TANH_SCALE = 0.7978845608028654
TANH_CUBIC = 0.044715


def dot(left, right, dims=((1,), (0,))):
    return lax.dot_general(left, right, (dims, ((), ())), preferred_element_type=jnp.float32)


def shift_phase(halo, shifted, rows, cols):
    inner, south, north, west, east = halo

    def one_tile(tile, line_of, live):
        left = west[tile].astype(jnp.float32)
        right = east[tile].astype(jnp.float32)
        for slot in live:
            wide = jnp.concatenate(
                [
                    left[4 * slot : 4 * slot + 4],
                    line_of(slot).astype(jnp.float32),
                    right[4 * slot : 4 * slot + 4],
                ],
                axis=0,
            )
            for tap_col in range(7):
                shifted[tap_col, 4 * tile + slot - 1] = wide[tap_col + 1 : tap_col + 1 + cols].astype(
                    jnp.bfloat16
                )

    def middle_tile(tile, carry):
        one_tile(tile, lambda slot: inner[4 * tile + slot - 4], range(4))
        return carry

    one_tile(0, lambda slot: south[slot - 1], range(1, 4))
    lax.fori_loop(1, rows // 4 + 1, middle_tile, 0)
    one_tile(rows // 4 + 1, lambda slot: north[slot], range(3))


def conv_phase(shifted, kernel_ref, banded, conv, rows, cols, channels, split):
    pair_step = 4
    across = lax.broadcasted_iota(jnp.int32, (LANES, LANES), 0)
    down = lax.broadcasted_iota(jnp.int32, (LANES, LANES), 1)
    eye = across == down
    for lane in range(0, channels, LANES):
        for tap_col in range(7):
            for step in range(4):
                for low in range(2):
                    for out in range(2):
                        tap_row = 2 * step + low - out
                        if 0 <= tap_row < 7:
                            tap = kernel_ref[pl.ds(tap_row * 7 + tap_col, 1), lane : lane + LANES]
                            block = jnp.where(eye, tap, 0.0).astype(jnp.bfloat16)
                        else:
                            block = jnp.zeros((LANES, LANES), jnp.bfloat16)
                        banded[
                            tap_col * 4 + step,
                            low * LANES : low * LANES + LANES,
                            out * LANES : out * LANES + LANES,
                        ] = block

        def one_chunk(index, carry):
            total = None
            for tap_col in range(7):
                for step in range(4):
                    window = shifted[
                        tap_col,
                        pl.ds(2 * (index * pair_step + step), 2 * pair_step),
                        :,
                        lane : lane + LANES,
                    ].reshape(pair_step, 2, cols, LANES)
                    left = jnp.concatenate(
                        [
                            window[:, 0].reshape(pair_step * cols, LANES),
                            window[:, 1].reshape(pair_step * cols, LANES),
                        ],
                        axis=1,
                    )
                    part = dot(left, banded[tap_col * 4 + step])
                    total = part if total is None else total + part
            for out in range(2):
                conv[pl.ds(index * pair_step, pair_step), out, :, lane : lane + LANES] = total[
                    :, out * LANES : out * LANES + LANES
                ].reshape(pair_step, cols, LANES)
            return carry

        chunks = rows // 2 // pair_step
        run = 1 if split else chunks
        for start in range(0, chunks, run):
            lax.fori_loop(start, start + run, one_chunk, 0)
            yield


def grid_work(
    halo, cot_ref, land_ref, kernel_ref, gain_ref, w_in_ref, w_out_ref, next_ref, packed_ref, banded, scratch
):
    taps, w_in_sum, w_out_sum, small_sum, shifted, conv, slope = scratch
    rows, cols, channels = halo[0].shape
    hidden_width = w_in_ref.shape[1]
    split = land_ref is not None
    row_step = 16
    cells = row_step * cols
    chunk = 256
    shift_phase(halo, shifted, rows, cols)
    yield
    taps[...] = kernel_ref[...].astype(jnp.float32)
    yield from conv_phase(shifted, taps, banded, conv, rows, cols, channels, split)
    w_in_sum[...] = jnp.zeros_like(w_in_sum)
    w_out_sum[...] = jnp.zeros_like(w_out_sum)
    small_sum[...] = jnp.zeros_like(small_sum)
    gain = jnp.concatenate(
        [gain_ref[row : row + 1, :].astype(jnp.float32) for row in range(channels // LANES)], axis=1
    )

    def one_block(index, gain_total):
        value = conv[pl.ds(index * (row_step // 2), row_step // 2)].reshape(cells, channels)
        centre = value - jnp.mean(value, axis=-1, keepdims=True)
        inv = lax.rsqrt(jnp.mean(centre * centre, axis=-1, keepdims=True) + epsilon)
        unit = centre * inv
        normed = (unit * gain).astype(jnp.bfloat16)
        where = pl.ds(index * cells, cells)
        upstream = cot_ref[where, :]
        if land_ref is not None:
            turned = land_ref[pl.ds(pl.multiple_of(index * row_step, 8), row_step), :].astype(jnp.float32).T
            keep = jnp.concatenate(
                [jnp.broadcast_to(turned[:, row : row + 1], (cols, channels)) for row in range(row_step)],
                axis=0,
            )
            upstream = upstream * keep.astype(jnp.bfloat16)
        normed_t = normed.T
        upstream_t = upstream.T
        update = None
        back = None
        for at in range(0, hidden_width, chunk):
            w_in = w_in_ref[:, at : at + chunk]
            w_out = w_out_ref[at : at + chunk, :]
            pre = dot(normed, w_in)
            grad_hidden = dot(upstream, w_out, ((1,), (1,)))
            square = pre * pre
            gate = 0.5 + 0.5 * jnp.tanh(pre * (TANH_SCALE + (TANH_SCALE * TANH_CUBIC) * square))
            active = pre * gate
            slope_part = 2 * TANH_SCALE + (6 * TANH_SCALE * TANH_CUBIC) * square
            grad_pre = (grad_hidden * (gate + active * (1.0 - gate) * slope_part)).astype(jnp.bfloat16)
            active = active.astype(jnp.bfloat16)
            part = dot(active, w_out)
            update = part if update is None else update + part
            part = dot(grad_pre, w_in, ((1,), (1,)))
            back = part if back is None else back + part
            for total, part in (
                (w_out_sum, dot(upstream_t, active)),
                (w_in_sum, dot(normed_t, grad_pre)),
            ):
                for lane in range(0, chunk, LANES):
                    total[(at + lane) // LANES] += part[:, lane : lane + LANES]
        inside = shifted[3, pl.ds(index * row_step + 3, row_step)].reshape(cells, channels)
        result = inside.astype(jnp.float32) + update
        if land_ref is not None:
            result = result * keep
        next_ref[where, :] = result.astype(jnp.bfloat16)
        gain_total = gain_total + jnp.sum((back * unit).reshape(cells // 8, 8, channels), axis=0)
        back = back * gain
        level = jnp.mean(back, axis=-1, keepdims=True)
        tilt = jnp.mean(back * unit, axis=-1, keepdims=True)
        slope[pl.ds(index * row_step, row_step)] = (
            (inv * (back - level - unit * tilt)).astype(jnp.bfloat16).reshape(row_step, cols, channels)
        )
        return gain_total

    blocks = rows // row_step
    gain_total = jnp.zeros((8, channels), jnp.float32)
    run = 1 if split else blocks
    for start in range(0, blocks, run):
        gain_total = lax.fori_loop(start, start + run, one_block, gain_total)
        yield
    small_sum[49:50, :] = jnp.sum(gain_total, axis=0, keepdims=True)
    at_row = 0
    for total in (w_in_sum, w_out_sum):
        for block in range(hidden_width // LANES):
            packed_ref[at_row : at_row + channels, :] = total[block].astype(jnp.bfloat16)
            at_row += channels
    if at_row < packed_ref.shape[0]:
        spare = packed_ref.shape[0] - at_row
        packed_ref[at_row:, :] = jnp.zeros((spare, LANES), jnp.bfloat16)


def tap_work(packed_ref, scratch):
    small_sum, shifted, _, slope = scratch[3:]
    rows, cols, channels = slope.shape
    for lane in range(0, channels, LANES):
        for tap_row in range(7):

            def one_row(row, totals):
                grad = slope[row, :, lane : lane + LANES]
                sums = []
                for tap_col in range(7):
                    product = grad * shifted[tap_col, row + tap_row, :, lane : lane + LANES]
                    pieces = [product[at : at + 16] for at in range(0, cols, 16)]
                    while len(pieces) > 1:
                        pieces = [a + b for a, b in zip(pieces[::2], pieces[1::2])]
                    wide = pieces[0].astype(jnp.float32)
                    sums.append(totals[tap_col] + wide[:8] + wide[8:])
                return tuple(sums)

            totals = lax.fori_loop(
                0, rows, one_row, tuple(jnp.zeros((8, LANES), jnp.float32) for _ in range(7)), unroll=8
            )
            for tap_col in range(7):
                small_sum[pl.ds(tap_row * 7 + tap_col, 1), lane : lane + LANES] = jnp.sum(
                    totals[tap_col], axis=0, keepdims=True
                )
            yield
    for lane in range(0, channels, LANES):
        at_row = lane // LANES * SMALL
        packed_ref[at_row : at_row + SMALL, :] = small_sum[:, lane : lane + LANES].astype(jnp.bfloat16)


def grid_scratch(state, hidden_width):
    rows, cols, channels = state.shape
    return [
        pltpu.VMEM((49, channels), jnp.float32),
        pltpu.VMEM((hidden_width // LANES, channels, LANES), jnp.float32),
        pltpu.VMEM((hidden_width // LANES, channels, LANES), jnp.float32),
        pltpu.VMEM((SMALL, channels), jnp.float32),
        pltpu.VMEM((7, rows + 6, cols, channels), jnp.bfloat16),
        pltpu.VMEM((rows // 2, 2, cols, channels), jnp.float32),
        pltpu.VMEM((rows, cols, channels), jnp.bfloat16),
    ]


def packed_rows(channels, hidden_width, devices):
    rows = 2 * (hidden_width // LANES) * channels
    return rows + -rows % (16 * devices)


def unpack_kernel(widths, *refs):
    count = len(widths)
    states, outs, held = refs[:count], refs[3 * count : -count - 1], refs[-count - 1 : -1]
    sem = refs[-1]
    loads = [pltpu.make_async_copy(state, room, sem.at[at]) for at, (state, room) in enumerate(zip(states, held))]
    stores = [
        pltpu.make_async_copy(room, out, sem.at[count + at])
        for at, (room, out) in enumerate(zip(held, outs[:count]))
    ]
    for copy in loads:
        copy.start()
    outs = outs[count:]
    for number, (channels, hidden_width) in enumerate(widths):
        packed_ref, small_ref = refs[count + number], refs[2 * count + number]
        at = 0
        kernel_out, gain_out, w_in_out, w_out_out = outs[4 * number : 4 * number + 4]
        for block in range(hidden_width // LANES):
            w_in_out[:, block * LANES : block * LANES + LANES] = packed_ref[at : at + channels, :].astype(
                jnp.float32
            )
            at += channels
        for block in range(hidden_width // LANES):
            w_out_out[block * LANES : block * LANES + LANES, :] = (
                packed_ref[at : at + channels, :].astype(jnp.float32).T
            )
            at += channels
        for lane in range(0, channels, LANES):
            at = lane // LANES * SMALL
            small = small_ref[at : at + SMALL, :].astype(jnp.float32)
            kernel_out[:, lane : lane + LANES] = small[:49]
            gain_out[:, lane : lane + LANES] = small[49:50]
        loads[number].wait()
        stores[number].start()
    for copy in stores:
        copy.wait()


def unpack(states, packed, smalls, widths):
    shapes = []
    for channels, hidden_width in widths:
        shapes += [(49, channels), (1, channels), (channels, hidden_width), (hidden_width, channels)]
    vmem = pl.BlockSpec(memory_space=pltpu.VMEM)
    anywhere = pl.BlockSpec(memory_space=pl.ANY)
    outs = pl.pallas_call(
        functools.partial(unpack_kernel, widths),
        out_shape=(
            *(jax.ShapeDtypeStruct(state.shape, state.dtype) for state in states),
            *(jax.ShapeDtypeStruct(shape, jnp.float32) for shape in shapes),
        ),
        in_specs=[anywhere] * len(states) + [vmem] * (2 * len(widths)),
        out_specs=(*([anywhere] * len(states)), *([vmem] * len(shapes))),
        scratch_shapes=[
            *(pltpu.VMEM(state.shape, state.dtype) for state in states),
            pltpu.SemaphoreType.DMA((2 * len(states),)),
        ],
        compiler_params=pltpu.CompilerParams(vmem_limit_bytes=60 * 1024 * 1024),
    )(*states, *packed, *smalls)
    return [out.reshape(-1) if out.shape[0] == 1 else out for out in outs]


def aligned(index):
    return pl.multiple_of(index, 16)


def greet(partners):
    barrier = pltpu.get_barrier_semaphore()
    for partner in partners:
        pl.semaphore_signal(barrier, inc=1, device_id=partner, device_id_type=MESH)
    return lambda: pl.semaphore_wait(barrier, len(partners))


def sum_plan(lon_count):
    spans = []
    span = 2
    while span < lon_count:
        spans.append(span)
        span *= 2
    return (spans, spans[::-1])


def sum_work(lat_count, lon_count, share_ref, full_ref, scratch):
    length = share_ref.shape[0]
    plan = sum_plan(lon_count)
    steps = len(plan[0])
    half, quarter = length // 2, length // 4
    first, lat_send, lat_recv, comb = scratch[:4]
    sends = [scratch[4 + part * steps : 4 + part * steps + steps] for part in range(2)]
    recvs = [scratch[4 + (2 + part) * steps : 4 + (2 + part) * steps + steps] for part in range(2)]
    totals = [scratch[4 + (4 + part) * steps : 4 + (4 + part) * steps + steps] for part in range(2)]
    send_sem, recv_sem = scratch[-2:]
    lat, lon = lax.axis_index("lat"), lax.axis_index("lon")
    core = lon % 2

    def flipped(span):
        bit = (lon // span) % 2
        return (lat, lon + span - 2 * span * bit), bit

    peers = [((lat + step) % lat_count, lon) for step in range(1, lat_count)]
    push = pusher(send_sem, recv_sem)
    pending = []
    opening = []
    for part in range(2):
        opening.append(
            push(
                share_ref.at[pl.ds(aligned((1 - core) * half + part * quarter), quarter), :],
                first.at[part],
                flipped(1)[0],
            )
        )
    active = [None, None]
    yield
    for part in range(2):
        opening[part].wait_recv()
        pending.append(opening[part])
        device, bit = flipped(plan[part][0])
        size = quarter // 2
        own = core * half + part * quarter

        def summed(start):
            return share_ref[pl.ds(aligned(own + start), size), :].astype(jnp.float32) + first[
                part, pl.ds(aligned(start), size), :
            ].astype(jnp.float32)

        sends[part][0][...] = summed((1 - bit) * size).astype(jnp.bfloat16)
        active[part] = push(sends[part][0], recvs[part][0], device)
        totals[part][0][...] = summed(bit * size)
    size = quarter // 2
    for step in range(steps):
        yield
        for part in range(2):
            active[part].wait_recv()
            pending.append(active[part])
            recv, total = recvs[part][step], totals[part][step]
            if step + 1 == steps:
                comb[part * size : part * size + size, :] = total[...] + recv[...].astype(jnp.float32)
                continue
            device, bit = flipped(plan[part][step + 1])
            rest = size // 2

            def joined(start):
                where = pl.ds(aligned(start), rest)
                return total[where, :] + recv[where, :].astype(jnp.float32)

            sends[part][step + 1][...] = joined((1 - bit) * rest).astype(jnp.bfloat16)
            active[part] = push(sends[part][step + 1], recvs[part][step + 1], device)
            totals[part][step + 1][...] = joined(bit * rest)
        if step + 1 < steps:
            size //= 2
    bases = []
    for part in range(2):
        base = core * half + part * quarter
        extent = quarter
        levels = []
        for span in plan[part]:
            extent //= 2
            base = base + ((lon // span) % 2) * extent
            levels.append((base, extent, span))
        bases.append(levels)
    chunk = 2 * size // lat_count
    lat_send[...] = comb[...].astype(jnp.bfloat16)
    arriving = []
    for step in range(1, lat_count):
        peer = (lat + step) % lat_count
        arriving.append(
            push(
                lat_send.at[pl.ds(aligned(peer * chunk), chunk), :],
                lat_recv.at[step - 1],
                (peer, lon),
            )
        )
    yield
    total = comb[pl.ds(aligned(lat * chunk), chunk), :]
    for step, copy in enumerate(arriving):
        copy.wait_recv()
        pending.append(copy)
        total = total + lat_recv[step].astype(jnp.float32)
    upper = (2 * lat) // lat_count
    low_base, high_base = bases[0][-1][0], bases[1][-1][0]
    place = low_base + upper * (high_base - low_base) + (lat - upper * (lat_count // 2)) * chunk
    mine = pl.ds(aligned(place), chunk)
    full_ref[mine, :] = total.astype(jnp.bfloat16)
    arriving = [push(full_ref.at[mine, :], full_ref.at[mine, :], peer) for peer in peers]
    yield
    for copy in arriving:
        copy.wait_recv()
        pending.append(copy)
    for step in reversed(range(steps)):
        arriving = []
        for part in range(2):
            base, extent, span = bases[part][step]
            region = full_ref.at[pl.ds(aligned(base), extent), :]
            arriving.append(push(region, region, flipped(span)[0]))
        yield
        for copy in arriving:
            copy.wait_recv()
            pending.append(copy)
    arriving = []
    for part in range(2):
        region = full_ref.at[pl.ds(aligned(core * half + part * quarter), quarter), :]
        arriving.append(push(region, region, flipped(1)[0]))
    yield
    for copy in arriving:
        copy.wait_recv()
        pending.append(copy)
    for copy in pending:
        copy.wait_send()


def sum_scratch(length, lat_count, lon_count):
    steps = len(sum_plan(lon_count)[0])
    sizes = [length // 4 // 2 ** (step + 1) for step in range(steps)]
    chunk = 2 * sizes[-1] // lat_count
    copies = 2 + 2 * steps + (lat_count - 1) * 2 + 2 * steps + 2
    narrow = [pltpu.VMEM((size, LANES), jnp.bfloat16) for size in sizes]
    wide = [pltpu.VMEM((size, LANES), jnp.float32) for size in sizes]
    return [
        pltpu.VMEM((2, length // 4, LANES), jnp.bfloat16),
        pltpu.VMEM((2 * sizes[-1], LANES), jnp.bfloat16),
        pltpu.VMEM((lat_count - 1, chunk, LANES), jnp.bfloat16),
        pltpu.VMEM((2 * sizes[-1], LANES), jnp.float32),
        *(narrow * 4),
        *(wide * 2),
        pltpu.SemaphoreType.DMA((copies,)),
        pltpu.SemaphoreType.DMA((copies,)),
    ]


def pusher(send_sem, recv_sem):
    count = [0]

    def push(source, target, device):
        number = count[0]
        count[0] += 1
        copy = pltpu.make_async_remote_copy(
            src_ref=source,
            dst_ref=target,
            send_sem=send_sem.at[number],
            recv_sem=recv_sem.at[number],
            device_id=device,
            device_id_type=MESH,
        )
        copy.start()
        return copy

    return push


def flat_work(lat_count, lon_count, share_ref, full_ref, scratch):
    lon_recv, lat_send, lat_recv, send_sem, recv_sem = scratch
    lat, lon = lax.axis_index("lat"), lax.axis_index("lon")
    push = pusher(send_sem, recv_sem)
    chunk = share_ref.shape[0] // lon_count
    part = chunk // lat_count
    lons = [(lon + step) % lon_count for step in range(1, lon_count)]
    lats = [(lat + step) % lat_count for step in range(1, lat_count)]
    done = []
    copies = [
        push(share_ref.at[pl.ds(aligned(peer * chunk), chunk), :], lon_recv.at[step], (lat, peer))
        for step, peer in enumerate(lons)
    ]
    yield
    total = share_ref[pl.ds(aligned(lon * chunk), chunk), :].astype(jnp.float32)
    for step, copy in enumerate(copies):
        copy.wait_recv()
        total = total + lon_recv[step].astype(jnp.float32)
    done += copies
    lat_send[...] = total.astype(jnp.bfloat16)
    copies = [
        push(lat_send.at[pl.ds(aligned(peer * part), part), :], lat_recv.at[step], (peer, lon))
        for step, peer in enumerate(lats)
    ]
    yield
    total = lat_send[pl.ds(aligned(lat * part), part), :].astype(jnp.float32)
    for step, copy in enumerate(copies):
        copy.wait_recv()
        total = total + lat_recv[step].astype(jnp.float32)
    done += copies
    mine = pl.ds(aligned(lon * chunk + lat * part), part)
    full_ref[mine, :] = total.astype(jnp.bfloat16)
    copies = [push(full_ref.at[mine, :], full_ref.at[mine, :], (peer, lon)) for peer in lats]
    yield
    for copy in copies:
        copy.wait_recv()
    done += copies
    region = pl.ds(aligned(lon * chunk), chunk)
    copies = [push(full_ref.at[region, :], full_ref.at[region, :], (lat, peer)) for peer in lons]
    yield
    for copy in copies:
        copy.wait_recv()
    done += copies
    for copy in done:
        copy.wait_send()


def flat_scratch(length, lat_count, lon_count):
    chunk = length // lon_count
    copies = 2 * (lat_count + lon_count - 2)
    return [
        pltpu.VMEM((lon_count - 1, chunk, LANES), jnp.bfloat16),
        pltpu.VMEM((chunk, LANES), jnp.bfloat16),
        pltpu.VMEM((lat_count - 1, chunk // lat_count, LANES), jnp.bfloat16),
        pltpu.SemaphoreType.DMA((copies,)),
        pltpu.SemaphoreType.DMA((copies,)),
    ]


def small_work(lat_count, lon_count, share_ref, full_ref, scratch):
    lon_terms, lat_terms, middle, send_sem, recv_sem = scratch
    lat, lon = lax.axis_index("lat"), lax.axis_index("lon")
    push = pusher(send_sem, recv_sem)
    copies = []
    for step in range(1, lon_count):
        copies.append(push(share_ref, lon_terms.at[lon], (lat, (lon + step) % lon_count)))
    lon_terms[lon] = share_ref[...]
    yield
    for copy in copies:
        copy.wait_recv()
    total = lon_terms[0].astype(jnp.float32)
    for term in range(1, lon_count):
        total = total + lon_terms[term].astype(jnp.float32)
    middle[...] = total.astype(jnp.bfloat16)
    for step in range(1, lat_count):
        copies.append(push(middle, lat_terms.at[lat], ((lat + step) % lat_count, lon)))
    lat_terms[lat] = middle[...]
    yield
    for copy in copies[lon_count - 1 :]:
        copy.wait_recv()
    total = lat_terms[0].astype(jnp.float32)
    for term in range(1, lat_count):
        total = total + lat_terms[term].astype(jnp.float32)
    full_ref[...] = total.astype(jnp.bfloat16)
    for copy in copies:
        copy.wait_send()


def small_scratch(length, lat_count, lon_count):
    copies = lat_count + lon_count - 2
    return [
        pltpu.VMEM((lon_count, length, LANES), jnp.bfloat16),
        pltpu.VMEM((lat_count, length, LANES), jnp.bfloat16),
        pltpu.VMEM((length, LANES), jnp.bfloat16),
        pltpu.SemaphoreType.DMA((copies,)),
        pltpu.SemaphoreType.DMA((copies,)),
    ]


def grids_kernel(lat_count, lon_count, sizes, *refs):
    atmos_halo, ocean_halo = refs[:5], refs[5:10]
    atmos_args, ocean_args, land = refs[10:15], refs[15:20], refs[20]
    atmos_next, ocean_next, atmos_full, ocean_full, atmos_small, ocean_small = refs[21:27]
    rest = list(refs[27:])
    parts = []
    for size in sizes:
        parts.append(rest[:size])
        rest = rest[size:]
    atmos_part, ocean_part, atmos_sum, ocean_sum, atmos_small_sum, ocean_small_sum = parts
    banded, atmos_share, ocean_share, atmos_few, ocean_few = rest
    lat, lon = lax.axis_index("lat"), lax.axis_index("lon")
    met = greet(
        [((lat + step) % lat_count, lon) for step in range(1, lat_count)]
        + [(lat, (lon + step) % lon_count) for step in range(1, lon_count)]
    )

    def along(work, *plan):
        for number, _ in enumerate(work):
            for sums, places in plan:
                if number in places:
                    next(sums, None)

    def begin(work, *args):
        sums = work(lat_count, lon_count, *args)
        next(sums)
        return sums

    def first_part(halo, args, mask, result, share, part):
        cot, kernel, gain, w_in, w_out = args
        return grid_work(halo, cot, mask, kernel, gain, w_in, w_out, result, share, banded, part)

    along(first_part(atmos_halo, atmos_args, None, atmos_next, atmos_share, atmos_part))
    met()
    first = begin(sum_work, atmos_share, atmos_full, atmos_sum)
    along(
        first_part(ocean_halo, ocean_args, land, ocean_next, ocean_share, ocean_part),
        (first, (2, 6, 7, 8, 9)),
    )
    second = begin(flat_work, ocean_share, ocean_full, ocean_sum)
    along(tap_work(atmos_few, atmos_part), (first, (4, 9)), (second, (5, 10)))
    third = begin(small_work, atmos_few, atmos_small, atmos_small_sum)
    along(tap_work(ocean_few, ocean_part), (second, (1,)), (third, (4,)))
    last = begin(small_work, ocean_few, ocean_small, ocean_small_sum)
    next(last)
    for sums in (first, second, third, last):
        for _ in sums:
            pass


def run_grids(atmos_halo, ocean_halo, land_sea, atmos_args, ocean_args):
    lat_count, lon_count = lax.axis_size("lat"), lax.axis_size("lon")
    vmem = pl.BlockSpec(memory_space=pltpu.VMEM)
    flat, states, shares, smalls, parts = [], [], [], [], []
    for cotangent, kernel, gain, w_in, w_out in (atmos_args, ocean_args):
        rows, cols, channels = cotangent.shape
        flat += [cotangent.reshape(rows * cols, channels), kernel, gain.reshape(-1, LANES), w_in, w_out]
        states.append((rows * cols, channels))
        shares.append((packed_rows(*w_in.shape, lat_count * lon_count), LANES))
        smalls.append((channels // LANES * SMALL, LANES))
        parts.append(grid_scratch(cotangent, w_in.shape[1]))
    parts.append(sum_scratch(shares[0][0], lat_count, lon_count))
    parts.append(flat_scratch(shares[1][0], lat_count, lon_count))
    parts += [small_scratch(small[0], lat_count, lon_count) for small in smalls]
    narrow = shares + smalls
    args = (*atmos_halo, *ocean_halo, *flat, land_sea)
    outs = pl.pallas_call(
        functools.partial(grids_kernel, lat_count, lon_count, tuple(len(part) for part in parts)),
        out_shape=tuple(jax.ShapeDtypeStruct(shape, jnp.bfloat16) for shape in states + narrow),
        in_specs=[vmem] * len(args),
        out_specs=(vmem,) * (len(states) + len(narrow)),
        scratch_shapes=[
            *(piece for part in parts for piece in part),
            pltpu.VMEM((28, 2 * LANES, 2 * LANES), jnp.bfloat16),
            *(pltpu.VMEM(shape, jnp.bfloat16) for shape in narrow),
        ],
        compiler_params=pltpu.CompilerParams(
            collective_id=2, has_side_effects=True, vmem_limit_bytes=60 * 1024 * 1024
        ),
    )(*args)
    return outs[:2], outs[2:4], outs[4:]


def to_tiles(pieces):
    return jnp.concatenate([piece.astype(jnp.float32) for piece in pieces], axis=0).astype(jnp.bfloat16)


def front_kernel(lat_count, lon_count, *refs):
    (
        atmos_ref,
        ocean_ref,
        land_ref,
        fold_ref,
        ocean_pairs,
        ocean_counts,
        ocean_weights_hbm,
        atmos_pairs,
        atmos_counts,
        atmos_weights_hbm,
        flux_map,
        surface_map,
        flux_inject,
        surface_inject,
    ) = refs[:14]
    atmos_out, ocean_out = refs[14:19], refs[19:24]
    (
        near_atmos,
        near_ocean,
        ocean_weights,
        atmos_weights,
        atmos_first,
        atmos_last,
        ocean_first,
        ocean_last,
        top_rows,
        circle_rows,
        send_sem,
        recv_sem,
        local_sem,
    ) = refs[24:]
    lat, lon = lax.axis_index("lat"), lax.axis_index("lon")
    east, west = (lon + 1) % lon_count, (lon + lon_count - 1) % lon_count
    has_south, has_north = lat > 0, lat < lat_count - 1
    beside = {-1: west, 0: lon, 1: east}
    cols = atmos_ref.shape[1]

    weight_copies = [
        pltpu.make_async_copy(ocean_weights_hbm, ocean_weights, local_sem.at[0]),
        pltpu.make_async_copy(atmos_weights_hbm, atmos_weights, local_sem.at[1]),
    ]
    for copy in weight_copies:
        copy.start()

    barrier = pltpu.get_barrier_semaphore()
    for step in range(1, lon_count):
        pl.semaphore_signal(
            barrier, inc=1, device_id=(lat, (lon + step) % lon_count), device_id_type=MESH
        )
    for band, there in ((-1, has_south), (1, has_north)):

        @pl.when(there)
        def _():
            for sector in (-1, 0, 1):
                pl.semaphore_signal(
                    barrier, inc=1, device_id=(lat + band, beside[sector]), device_id_type=MESH
                )

    numbers = {}

    def remote(name, source, target, device):
        number = numbers.setdefault(name, len(numbers))
        return pltpu.make_async_remote_copy(
            src_ref=source,
            dst_ref=target,
            send_sem=send_sem.at[number],
            recv_sem=recv_sem.at[number],
            device_id=device,
            device_id_type=MESH,
        )

    def each_neighbour(action):
        for band, there in ((-1, has_south), (0, None), (1, has_north)):
            for sector in (-1, 0, 1):
                if band == 0 and sector == 0:
                    continue
                if there is None:
                    action(band, sector)
                else:
                    pl.when(there)(functools.partial(action, band, sector))

    def field_copy(name, near, band, sector, waiting):
        own = near.at[4]
        return remote(
            (name, band, sector),
            own,
            near.at[(1 - band) * 3 + 1 - sector],
            (lat + band, beside[sector]),
        )

    def send_fields(name, near):
        each_neighbour(lambda band, sector: field_copy(name, near, band, sector, False).start())

    def await_fields(name, near):
        each_neighbour(
            lambda band, sector: remote(
                (name, -band, -sector),
                near.at[4],
                near.at[(1 + band) * 3 + 1 + sector],
                (lat + band, beside[sector]),
            ).wait_recv()
        )

    def fields(source, projection, near, masked):
        channels = source.shape[2]
        turned = projection[...]

        def one_block(block, carry):
            cells = source[pl.ds(2 * block, 2)].reshape(BCELLS, channels)
            values = dot(turned, cells, ((1,), (1,)))
            if masked:
                keep = jnp.concatenate(
                    [land_ref[pl.ds(2 * block, 1), :], land_ref[pl.ds(2 * block + 1, 1), :]], axis=1
                )
                values = values * keep.astype(jnp.float32)
            near[4, block] = values.astype(jnp.bfloat16)
            return carry

        lax.fori_loop(0, source.shape[0] // 2, one_block, 0, unroll=8)

    fields(atmos_ref, flux_map, near_atmos, False)
    pl.semaphore_wait(
        barrier, lon_count - 1 + 3 * has_south.astype(jnp.int32) + 3 * has_north.astype(jnp.int32)
    )
    send_fields("atmos_fields", near_atmos)
    fields(ocean_ref, surface_map, near_ocean, True)
    send_fields("ocean_fields", near_ocean)

    def remap(near, pairs, counts, weights, state, projection, target):
        source_count = near.shape[1]
        channels = state.shape[2]
        inject = projection[...]

        def one_block(block, carry):
            count = counts[0, block]
            picked = []
            for entry in range(PAIRS):
                number = pairs[entry, block]
                owner = lax.div(number, source_count)
                local = number - owner * source_count
                band = lax.div(owner, lon_count)
                sector = owner - band * lon_count - lon + 1 + lon_count
                sector = lax.rem(sector, lon_count)
                slot = jnp.clip((band - lat + 1) * 3 + sector, 0, 8)
                value = near[slot, local]
                if entry:
                    value = jnp.where(entry < count, value, jnp.zeros_like(value))
                picked.append(value)
            left = jnp.concatenate(picked, axis=1)
            mixed = dot(left, weights[block, 0].reshape(PAIRS * BCELLS, BCELLS))
            mixed = mixed.astype(jnp.bfloat16).astype(jnp.float32).T.astype(jnp.bfloat16)
            added = dot(mixed, inject)
            cells = state[pl.ds(2 * block, 2)].reshape(BCELLS, channels).astype(jnp.float32)
            target[pl.ds(2 * block, 2)] = (
                (cells + added).astype(jnp.bfloat16).reshape(2, state.shape[1], channels)
            )
            return carry

        lax.fori_loop(0, state.shape[0] // 2, one_block, 0, unroll=8)

    def edges(target, first, last):
        channels = target.shape[2]

        def one_tile(tile, carry):
            rows = target[pl.ds(4 * tile, 4)].astype(jnp.float32)
            first[tile] = to_tiles([rows[row, :EDGE] for row in range(4)])
            last[tile] = to_tiles([rows[row, cols - EDGE :] for row in range(4)])
            return carry

        lax.fori_loop(0, target.shape[0] // 4, one_tile, 0, unroll=4)

    def halo_copy(name, out, first, last, band, sector, to_neighbour):
        target, south, north, west_edge, east_edge = out
        rows = target.shape[0]
        tiles = rows // 4
        if sector == 0:
            source = target.at[rows - 3 : rows] if band == 1 else target.at[0:3]
            place = south if band == 1 else north
        else:
            edge = last if sector == 1 else first
            place = west_edge if sector == 1 else east_edge
            if band == 0:
                source, place = edge, place.at[1 : tiles + 1]
            elif band == 1:
                source, place = edge.at[tiles - 1], place.at[0]
            else:
                source, place = edge.at[0], place.at[tiles + 1]
        flip = 1 if to_neighbour else -1
        return remote(
            (name, band, sector), source, place, (lat + flip * band, beside[flip * sector])
        )

    def send_halo(name, out, first, last):
        each_neighbour(
            lambda band, sector: halo_copy(name, out, first, last, band, sector, True).start()
        )

    def await_halo(name, out, first, last):
        each_neighbour(
            lambda band, sector: halo_copy(name, out, first, last, -band, -sector, False).wait_recv()
        )

    def blank(out, at_north):
        target, south, north, west_edge, east_edge = out
        rim = north if at_north else south
        tile = target.shape[0] // 4 + 1 if at_north else 0
        rim[...] = jnp.zeros_like(rim)
        west_edge[tile] = jnp.zeros(west_edge.shape[1:], jnp.bfloat16)
        east_edge[tile] = jnp.zeros(east_edge.shape[1:], jnp.bfloat16)

    pl.when(jnp.logical_not(has_south))(lambda: blank(atmos_out, False))
    pl.when(jnp.logical_not(has_south))(lambda: blank(ocean_out, False))
    pl.when(jnp.logical_not(has_north))(lambda: blank(atmos_out, True))

    await_fields("atmos_fields", near_atmos)
    weight_copies[0].wait()
    remap(near_atmos, ocean_pairs, ocean_counts, ocean_weights, ocean_ref, flux_inject, ocean_out[0])
    edges(ocean_out[0], ocean_first, ocean_last)
    send_halo("ocean_halo", ocean_out, ocean_first, ocean_last)
    is_top = jnp.logical_not(has_north)
    top_at = ocean_out[0].shape[0] - 3

    def fold_copy(step, to_peer):
        flip = step if to_peer else lon_count - step
        return remote(
            ("fold", step),
            top_rows,
            circle_rows.at[:, pl.ds(pl.multiple_of(((lon if to_peer else (lon + flip) % lon_count)) * cols, 16), cols), :],
            (lat, (lon + flip) % lon_count),
        )

    @pl.when(is_top)
    def _():
        for row in range(3):
            top_rows[row] = ocean_out[0][top_at + 2 - row]
        for step in range(1, lon_count):
            fold_copy(step, True).start()
        own = pl.ds(pl.multiple_of(lon * cols, 16), cols)
        for row in range(3):
            circle_rows[row, own, :] = top_rows[row]

    await_fields("ocean_fields", near_ocean)
    weight_copies[1].wait()
    remap(near_ocean, atmos_pairs, atmos_counts, atmos_weights, atmos_ref, surface_inject, atmos_out[0])
    edges(atmos_out[0], atmos_first, atmos_last)
    send_halo("atmos_halo", atmos_out, atmos_first, atmos_last)

    @pl.when(is_top)
    def _():
        for step in range(1, lon_count):
            fold_copy(step, False).wait_recv()
        length = lon_count * cols
        partner = fold_ref[...]

        def chosen(first, count, repeat):
            place = lax.broadcasted_iota(jnp.int32, (count, length), 0)
            if repeat is not None:
                wanted = lax.rem(lon * cols + first + length + lax.rem(place, EDGE), length)
                live = place // EDGE == repeat
                return jnp.where(live & (partner == wanted), 1.0, 0.0).astype(jnp.bfloat16)
            return jnp.where(partner == lon * cols + place, 1.0, 0.0).astype(jnp.bfloat16)

        _, _, north, west_edge, east_edge = ocean_out
        tile = ocean_out[0].shape[0] // 4 + 1
        middle = chosen(0, cols, None)
        sides = [None, None]
        for row in range(3):
            line = circle_rows[row]
            north[row] = dot(middle, line).astype(jnp.bfloat16)
            for side, first in enumerate((-EDGE, cols)):
                part = dot(chosen(first, 16, row), line)
                sides[side] = part if row == 0 else sides[side] + part
        west_edge[tile] = sides[0].astype(jnp.bfloat16)
        east_edge[tile] = sides[1].astype(jnp.bfloat16)

    await_halo("ocean_halo", ocean_out, ocean_first, ocean_last)
    await_halo("atmos_halo", atmos_out, atmos_first, atmos_last)
    for name, near in (("atmos_fields", near_atmos), ("ocean_fields", near_ocean)):
        each_neighbour(
            lambda band, sector: field_copy(name, near, band, sector, False).wait_send()
        )
    for name, out, first, last in (
        ("ocean_halo", ocean_out, ocean_first, ocean_last),
        ("atmos_halo", atmos_out, atmos_first, atmos_last),
    ):
        each_neighbour(
            lambda band, sector: halo_copy(name, out, first, last, band, sector, True).wait_send()
        )

    @pl.when(is_top)
    def _():
        for step in range(1, lon_count):
            fold_copy(step, True).wait_send()


def front(
    atmos_state,
    ocean_state,
    land_sea,
    fold_partner,
    ocean_pairs,
    ocean_counts,
    ocean_weights,
    atmos_pairs,
    atmos_counts,
    atmos_weights,
    flux_map,
    surface_map,
    flux_inject,
    surface_inject,
):
    lat_count, lon_count = lax.axis_size("lat"), lax.axis_size("lon")
    vmem = pl.BlockSpec(memory_space=pltpu.VMEM)
    smem = pl.BlockSpec(memory_space=pltpu.SMEM)
    anywhere = pl.BlockSpec(memory_space=pl.ANY)

    def out_shapes(state):
        rows, cols, channels = state.shape
        return [
            jax.ShapeDtypeStruct(shape, jnp.bfloat16)
            for shape in (
                (rows, cols, channels),
                (3, cols, channels),
                (3, cols, channels),
                (rows // 4 + 2, 16, channels),
                (rows // 4 + 2, 16, channels),
            )
        ]

    def edge_scratch(state):
        return pltpu.VMEM((state.shape[0] // 4, 16, state.shape[2]), jnp.bfloat16)

    copies = 32 + lon_count - 1
    cols = atmos_state.shape[1]
    ocean_channels = ocean_state.shape[2]
    outs = pl.pallas_call(
        functools.partial(front_kernel, lat_count, lon_count),
        out_shape=tuple(out_shapes(atmos_state) + out_shapes(ocean_state)),
        in_specs=[vmem, vmem, vmem, vmem, smem, smem, anywhere, smem, smem, anywhere] + [vmem] * 4,
        out_specs=(vmem,) * 10,
        scratch_shapes=[
            pltpu.VMEM((9, atmos_state.shape[0] // 2, NFIELD, BCELLS), jnp.bfloat16),
            pltpu.VMEM((9, ocean_state.shape[0] // 2, NFIELD, BCELLS), jnp.bfloat16),
            pltpu.VMEM(ocean_weights.shape, jnp.bfloat16),
            pltpu.VMEM(atmos_weights.shape, jnp.bfloat16),
            edge_scratch(atmos_state),
            edge_scratch(atmos_state),
            edge_scratch(ocean_state),
            edge_scratch(ocean_state),
            pltpu.VMEM((3, cols, ocean_channels), jnp.bfloat16),
            pltpu.VMEM((3, lon_count * cols, ocean_channels), jnp.bfloat16),
            pltpu.SemaphoreType.DMA((copies,)),
            pltpu.SemaphoreType.DMA((copies,)),
            pltpu.SemaphoreType.DMA((2,)),
        ],
        compiler_params=pltpu.CompilerParams(
            collective_id=1, has_side_effects=True, vmem_limit_bytes=60 * 1024 * 1024
        ),
    )(
        atmos_state,
        ocean_state,
        land_sea,
        fold_partner.reshape(1, -1),
        ocean_pairs.reshape(-1, PAIRS).T,
        ocean_counts.T,
        ocean_weights,
        atmos_pairs.reshape(-1, PAIRS).T,
        atmos_counts.T,
        atmos_weights,
        flux_map.T,
        surface_map.T,
        flux_inject,
        surface_inject,
    )
    return outs[:5], outs[5:]


def shards(
    atmos_state,
    ocean_state,
    atmos_cotangent,
    ocean_cotangent,
    land_sea,
    fold_partner,
    ocean_pairs,
    ocean_counts,
    ocean_weights,
    atmos_pairs,
    atmos_counts,
    atmos_weights,
    flux_map,
    surface_map,
    flux_inject,
    surface_inject,
    atmos_kernel,
    atmos_gain,
    atmos_w_in,
    atmos_w_out,
    ocean_kernel,
    ocean_gain,
    ocean_w_in,
    ocean_w_out,
):
    atmos_halo, ocean_halo = front(
        atmos_state,
        ocean_state,
        land_sea,
        fold_partner,
        ocean_pairs,
        ocean_counts,
        ocean_weights,
        atmos_pairs,
        atmos_counts,
        atmos_weights,
        flux_map,
        surface_map,
        flux_inject,
        surface_inject,
    )
    states, packed, smalls = run_grids(
        atmos_halo,
        ocean_halo,
        land_sea,
        (atmos_cotangent, atmos_kernel, atmos_gain, atmos_w_in, atmos_w_out),
        (ocean_cotangent, ocean_kernel, ocean_gain, ocean_w_in, ocean_w_out),
    )
    outs = unpack(states, packed, smalls, (atmos_w_in.shape, ocean_w_in.shape))
    return (outs[0].reshape(atmos_state.shape), outs[1].reshape(ocean_state.shape), *outs[2:])


def solution(mesh):
    return jax.shard_map(
        shards,
        mesh=mesh,
        in_specs=(
            P("lat", "lon", None),
            P("lat", "lon", None),
            P("lat", "lon", None),
            P("lat", "lon", None),
            P("lat", "lon"),
            P(),
            P("lat", "lon", None),
            P("lat", "lon"),
            P("lat", "lon", None, None, None),
            P("lat", "lon", None),
            P("lat", "lon"),
            P("lat", "lon", None, None, None),
            P(),
            P(),
            P(),
            P(),
            P(),
            P(),
            P(),
            P(),
            P(),
            P(),
            P(),
            P(),
        ),
        out_specs=(
            P("lat", "lon", None),
            P("lat", "lon", None),
            P(),
            P(),
            P(),
            P(),
            P(),
            P(),
            P(),
            P(),
        ),
        check_vma=False,
    )
```

```python
import functools

import jax
import jax.numpy as jnp
from jax import lax
from jax.experimental import pallas as pl
from jax.experimental.pallas import tpu as pltpu
from jax.sharding import PartitionSpec as P

NFIELD = 16
BCELLS = 128
PAIRS = 4
LANES = 128
SMALL = 64
EDGE = 4
MESH = pl.DeviceIdType.MESH
epsilon = 1e-06
TANH_SCALE = 0.7978845608028654
TANH_CUBIC = 0.044715


def dot(left, right, dims=((1,), (0,))):
    return lax.dot_general(left, right, (dims, ((), ())), preferred_element_type=jnp.float32)


def shift_phase(halo, shifted, rows, cols):
    inner, south, north, west, east = halo

    def one_tile(tile, line_of, live):
        left = west[tile].astype(jnp.float32)
        right = east[tile].astype(jnp.float32)
        for slot in live:
            wide = jnp.concatenate(
                [
                    left[4 * slot : 4 * slot + 4],
                    line_of(slot).astype(jnp.float32),
                    right[4 * slot : 4 * slot + 4],
                ],
                axis=0,
            )
            for tap_col in range(7):
                shifted[tap_col, 4 * tile + slot - 1] = wide[tap_col + 1 : tap_col + 1 + cols].astype(
                    jnp.bfloat16
                )

    def middle_tile(tile, carry):
        one_tile(tile, lambda slot: inner[4 * tile + slot - 4], range(4))
        return carry

    one_tile(0, lambda slot: south[slot - 1], range(1, 4))
    lax.fori_loop(1, rows // 4 + 1, middle_tile, 0)
    one_tile(rows // 4 + 1, lambda slot: north[slot], range(3))


def conv_phase(shifted, kernel_ref, banded, conv, rows, cols, channels, split):
    pair_step = 4
    across = lax.broadcasted_iota(jnp.int32, (LANES, LANES), 0)
    down = lax.broadcasted_iota(jnp.int32, (LANES, LANES), 1)
    eye = across == down
    for lane in range(0, channels, LANES):
        for tap_col in range(7):
            for step in range(4):
                for low in range(2):
                    for out in range(2):
                        tap_row = 2 * step + low - out
                        if 0 <= tap_row < 7:
                            tap = kernel_ref[pl.ds(tap_row * 7 + tap_col, 1), lane : lane + LANES]
                            block = jnp.where(eye, tap, 0.0).astype(jnp.bfloat16)
                        else:
                            block = jnp.zeros((LANES, LANES), jnp.bfloat16)
                        banded[
                            tap_col * 4 + step,
                            low * LANES : low * LANES + LANES,
                            out * LANES : out * LANES + LANES,
                        ] = block

        def one_chunk(index, carry):
            total = None
            for tap_col in range(7):
                for step in range(4):
                    window = shifted[
                        tap_col,
                        pl.ds(2 * (index * pair_step + step), 2 * pair_step),
                        :,
                        lane : lane + LANES,
                    ].reshape(pair_step, 2, cols, LANES)
                    left = jnp.concatenate(
                        [
                            window[:, 0].reshape(pair_step * cols, LANES),
                            window[:, 1].reshape(pair_step * cols, LANES),
                        ],
                        axis=1,
                    )
                    part = dot(left, banded[tap_col * 4 + step])
                    total = part if total is None else total + part
            for out in range(2):
                conv[pl.ds(index * pair_step, pair_step), out, :, lane : lane + LANES] = total[
                    :, out * LANES : out * LANES + LANES
                ].reshape(pair_step, cols, LANES)
            return carry

        chunks = rows // 2 // pair_step
        run = 1 if split else chunks
        for start in range(0, chunks, run):
            lax.fori_loop(start, start + run, one_chunk, 0)
            yield


def grid_work(
    halo, cot_ref, land_ref, kernel_ref, gain_ref, w_in_ref, w_out_ref, next_ref, packed_ref, banded, scratch
):
    taps, w_in_sum, w_out_sum, small_sum, shifted, conv, slope = scratch
    rows, cols, channels = halo[0].shape
    hidden_width = w_in_ref.shape[1]
    split = land_ref is not None
    row_step = 16
    cells = row_step * cols
    chunk = 256
    shift_phase(halo, shifted, rows, cols)
    yield
    taps[...] = kernel_ref[...].astype(jnp.float32)
    yield from conv_phase(shifted, taps, banded, conv, rows, cols, channels, split)
    w_in_sum[...] = jnp.zeros_like(w_in_sum)
    w_out_sum[...] = jnp.zeros_like(w_out_sum)
    small_sum[...] = jnp.zeros_like(small_sum)
    gain = jnp.concatenate(
        [gain_ref[row : row + 1, :].astype(jnp.float32) for row in range(channels // LANES)], axis=1
    )

    def one_block(index, gain_total):
        value = conv[pl.ds(index * (row_step // 2), row_step // 2)].reshape(cells, channels)
        centre = value - jnp.mean(value, axis=-1, keepdims=True)
        inv = lax.rsqrt(jnp.mean(centre * centre, axis=-1, keepdims=True) + epsilon)
        unit = centre * inv
        normed = (unit * gain).astype(jnp.bfloat16)
        where = pl.ds(index * cells, cells)
        upstream = cot_ref[where, :]
        if land_ref is not None:
            turned = land_ref[pl.ds(pl.multiple_of(index * row_step, 8), row_step), :].astype(jnp.float32).T
            keep = jnp.concatenate(
                [jnp.broadcast_to(turned[:, row : row + 1], (cols, channels)) for row in range(row_step)],
                axis=0,
            )
            upstream = upstream * keep.astype(jnp.bfloat16)
        normed_t = normed.T
        upstream_t = upstream.T
        update = None
        back = None
        for at in range(0, hidden_width, chunk):
            w_in = w_in_ref[:, at : at + chunk]
            w_out = w_out_ref[at : at + chunk, :]
            pre = dot(normed, w_in)
            grad_hidden = dot(upstream, w_out, ((1,), (1,)))
            square = pre * pre
            gate = 0.5 + 0.5 * jnp.tanh(pre * (TANH_SCALE + (TANH_SCALE * TANH_CUBIC) * square))
            active = pre * gate
            slope_part = 2 * TANH_SCALE + (6 * TANH_SCALE * TANH_CUBIC) * square
            grad_pre = (grad_hidden * (gate + active * (1.0 - gate) * slope_part)).astype(jnp.bfloat16)
            active = active.astype(jnp.bfloat16)
            part = dot(active, w_out)
            update = part if update is None else update + part
            part = dot(grad_pre, w_in, ((1,), (1,)))
            back = part if back is None else back + part
            for total, part in (
                (w_out_sum, dot(upstream_t, active)),
                (w_in_sum, dot(normed_t, grad_pre)),
            ):
                for lane in range(0, chunk, LANES):
                    total[(at + lane) // LANES] += part[:, lane : lane + LANES]
        inside = shifted[3, pl.ds(index * row_step + 3, row_step)].reshape(cells, channels)
        result = inside.astype(jnp.float32) + update
        if land_ref is not None:
            result = result * keep
        next_ref[where, :] = result.astype(jnp.bfloat16)
        gain_total = gain_total + jnp.sum((back * unit).reshape(cells // 8, 8, channels), axis=0)
        back = back * gain
        level = jnp.mean(back, axis=-1, keepdims=True)
        tilt = jnp.mean(back * unit, axis=-1, keepdims=True)
        slope[pl.ds(index * row_step, row_step)] = (
            (inv * (back - level - unit * tilt)).astype(jnp.bfloat16).reshape(row_step, cols, channels)
        )
        return gain_total

    blocks = rows // row_step
    gain_total = jnp.zeros((8, channels), jnp.float32)
    run = 1 if split else blocks
    for start in range(0, blocks, run):
        gain_total = lax.fori_loop(start, start + run, one_block, gain_total)
        yield
    small_sum[49:50, :] = jnp.sum(gain_total, axis=0, keepdims=True)
    at_row = 0
    for total in (w_in_sum, w_out_sum):
        for block in range(hidden_width // LANES):
            packed_ref[at_row : at_row + channels, :] = total[block].astype(jnp.bfloat16)
            at_row += channels
    if at_row < packed_ref.shape[0]:
        spare = packed_ref.shape[0] - at_row
        packed_ref[at_row:, :] = jnp.zeros((spare, LANES), jnp.bfloat16)


def tap_work(packed_ref, scratch):
    small_sum, shifted, _, slope = scratch[3:]
    rows, cols, channels = slope.shape
    for lane in range(0, channels, LANES):
        for tap_row in range(7):

            def one_row(row, totals):
                grad = slope[row, :, lane : lane + LANES]
                sums = []
                for tap_col in range(7):
                    product = grad * shifted[tap_col, row + tap_row, :, lane : lane + LANES]
                    pieces = [product[at : at + 16] for at in range(0, cols, 16)]
                    while len(pieces) > 1:
                        pieces = [a + b for a, b in zip(pieces[::2], pieces[1::2])]
                    wide = pieces[0].astype(jnp.float32)
                    sums.append(totals[tap_col] + wide[:8] + wide[8:])
                return tuple(sums)

            totals = lax.fori_loop(
                0, rows, one_row, tuple(jnp.zeros((8, LANES), jnp.float32) for _ in range(7)), unroll=8
            )
            for tap_col in range(7):
                small_sum[pl.ds(tap_row * 7 + tap_col, 1), lane : lane + LANES] = jnp.sum(
                    totals[tap_col], axis=0, keepdims=True
                )
            yield
    for lane in range(0, channels, LANES):
        at_row = lane // LANES * SMALL
        packed_ref[at_row : at_row + SMALL, :] = small_sum[:, lane : lane + LANES].astype(jnp.bfloat16)


def grid_scratch(state, hidden_width):
    rows, cols, channels = state.shape
    return [
        pltpu.VMEM((49, channels), jnp.float32),
        pltpu.VMEM((hidden_width // LANES, channels, LANES), jnp.float32),
        pltpu.VMEM((hidden_width // LANES, channels, LANES), jnp.float32),
        pltpu.VMEM((SMALL, channels), jnp.float32),
        pltpu.VMEM((7, rows + 6, cols, channels), jnp.bfloat16),
        pltpu.VMEM((rows // 2, 2, cols, channels), jnp.float32),
        pltpu.VMEM((rows, cols, channels), jnp.bfloat16),
    ]


def packed_rows(channels, hidden_width, devices):
    rows = 2 * (hidden_width // LANES) * channels
    return rows + -rows % (16 * devices)


def unpack_kernel(widths, *refs):
    count = len(widths)
    states, outs = refs[:count], refs[3 * count :]
    for state, out in zip(states, outs[:count]):
        out[...] = state[...]
    outs = outs[count:]
    for number, (channels, hidden_width) in enumerate(widths):
        packed_ref, small_ref = refs[count + number], refs[2 * count + number]
        at = 0
        kernel_out, gain_out, w_in_out, w_out_out = outs[4 * number : 4 * number + 4]
        for block in range(hidden_width // LANES):
            w_in_out[:, block * LANES : block * LANES + LANES] = packed_ref[at : at + channels, :].astype(
                jnp.float32
            )
            at += channels
        for block in range(hidden_width // LANES):
            w_out_out[block * LANES : block * LANES + LANES, :] = (
                packed_ref[at : at + channels, :].astype(jnp.float32).T
            )
            at += channels
        for lane in range(0, channels, LANES):
            at = lane // LANES * SMALL
            small = small_ref[at : at + SMALL, :].astype(jnp.float32)
            kernel_out[:, lane : lane + LANES] = small[:49]
            gain_out[:, lane : lane + LANES] = small[49:50]


def unpack(states, packed, smalls, widths):
    shapes = []
    for channels, hidden_width in widths:
        shapes += [(49, channels), (1, channels), (channels, hidden_width), (hidden_width, channels)]
    vmem = pl.BlockSpec(memory_space=pltpu.VMEM)
    outs = pl.pallas_call(
        functools.partial(unpack_kernel, widths),
        out_shape=(
            *(jax.ShapeDtypeStruct(state.shape, state.dtype) for state in states),
            *(jax.ShapeDtypeStruct(shape, jnp.float32) for shape in shapes),
        ),
        in_specs=[vmem] * (3 * len(widths)),
        out_specs=(vmem,) * (len(states) + len(shapes)),
        compiler_params=pltpu.CompilerParams(vmem_limit_bytes=60 * 1024 * 1024),
    )(*states, *packed, *smalls)
    return [out.reshape(-1) if out.shape[0] == 1 else out for out in outs]


def aligned(index):
    return pl.multiple_of(index, 16)


def greet(partners):
    barrier = pltpu.get_barrier_semaphore()
    for partner in partners:
        pl.semaphore_signal(barrier, inc=1, device_id=partner, device_id_type=MESH)
    return lambda: pl.semaphore_wait(barrier, len(partners))


def sum_plan(lon_count):
    spans = []
    span = 2
    while span < lon_count:
        spans.append(span)
        span *= 2
    return (spans, spans[::-1])


def sum_work(lat_count, lon_count, share_ref, full_ref, scratch):
    length = share_ref.shape[0]
    plan = sum_plan(lon_count)
    steps = len(plan[0])
    half, quarter = length // 2, length // 4
    first, lat_send, lat_recv, comb = scratch[:4]
    sends = [scratch[4 + part * steps : 4 + part * steps + steps] for part in range(2)]
    recvs = [scratch[4 + (2 + part) * steps : 4 + (2 + part) * steps + steps] for part in range(2)]
    totals = [scratch[4 + (4 + part) * steps : 4 + (4 + part) * steps + steps] for part in range(2)]
    send_sem, recv_sem = scratch[-2:]
    lat, lon = lax.axis_index("lat"), lax.axis_index("lon")
    core = lon % 2

    def flipped(span):
        bit = (lon // span) % 2
        return (lat, lon + span - 2 * span * bit), bit

    peers = [((lat + step) % lat_count, lon) for step in range(1, lat_count)]
    push = pusher(send_sem, recv_sem)
    pending = []
    opening = []
    for part in range(2):
        opening.append(
            push(
                share_ref.at[pl.ds(aligned((1 - core) * half + part * quarter), quarter), :],
                first.at[part],
                flipped(1)[0],
            )
        )
    active = [None, None]
    yield
    for part in range(2):
        opening[part].wait_recv()
        pending.append(opening[part])
        device, bit = flipped(plan[part][0])
        size = quarter // 2
        own = core * half + part * quarter

        def summed(start):
            return share_ref[pl.ds(aligned(own + start), size), :].astype(jnp.float32) + first[
                part, pl.ds(aligned(start), size), :
            ].astype(jnp.float32)

        sends[part][0][...] = summed((1 - bit) * size).astype(jnp.bfloat16)
        active[part] = push(sends[part][0], recvs[part][0], device)
        totals[part][0][...] = summed(bit * size)
    size = quarter // 2
    for step in range(steps):
        yield
        for part in range(2):
            active[part].wait_recv()
            pending.append(active[part])
            recv, total = recvs[part][step], totals[part][step]
            if step + 1 == steps:
                comb[part * size : part * size + size, :] = total[...] + recv[...].astype(jnp.float32)
                continue
            device, bit = flipped(plan[part][step + 1])
            rest = size // 2

            def joined(start):
                where = pl.ds(aligned(start), rest)
                return total[where, :] + recv[where, :].astype(jnp.float32)

            sends[part][step + 1][...] = joined((1 - bit) * rest).astype(jnp.bfloat16)
            active[part] = push(sends[part][step + 1], recvs[part][step + 1], device)
            totals[part][step + 1][...] = joined(bit * rest)
        if step + 1 < steps:
            size //= 2
    bases = []
    for part in range(2):
        base = core * half + part * quarter
        extent = quarter
        levels = []
        for span in plan[part]:
            extent //= 2
            base = base + ((lon // span) % 2) * extent
            levels.append((base, extent, span))
        bases.append(levels)
    chunk = 2 * size // lat_count
    lat_send[...] = comb[...].astype(jnp.bfloat16)
    arriving = []
    for step in range(1, lat_count):
        peer = (lat + step) % lat_count
        arriving.append(
            push(
                lat_send.at[pl.ds(aligned(peer * chunk), chunk), :],
                lat_recv.at[step - 1],
                (peer, lon),
            )
        )
    yield
    total = comb[pl.ds(aligned(lat * chunk), chunk), :]
    for step, copy in enumerate(arriving):
        copy.wait_recv()
        pending.append(copy)
        total = total + lat_recv[step].astype(jnp.float32)
    upper = (2 * lat) // lat_count
    low_base, high_base = bases[0][-1][0], bases[1][-1][0]
    place = low_base + upper * (high_base - low_base) + (lat - upper * (lat_count // 2)) * chunk
    mine = pl.ds(aligned(place), chunk)
    full_ref[mine, :] = total.astype(jnp.bfloat16)
    arriving = [push(full_ref.at[mine, :], full_ref.at[mine, :], peer) for peer in peers]
    yield
    for copy in arriving:
        copy.wait_recv()
        pending.append(copy)
    for step in reversed(range(steps)):
        arriving = []
        for part in range(2):
            base, extent, span = bases[part][step]
            region = full_ref.at[pl.ds(aligned(base), extent), :]
            arriving.append(push(region, region, flipped(span)[0]))
        yield
        for copy in arriving:
            copy.wait_recv()
            pending.append(copy)
    arriving = []
    for part in range(2):
        region = full_ref.at[pl.ds(aligned(core * half + part * quarter), quarter), :]
        arriving.append(push(region, region, flipped(1)[0]))
    yield
    for copy in arriving:
        copy.wait_recv()
        pending.append(copy)
    for copy in pending:
        copy.wait_send()


def sum_scratch(length, lat_count, lon_count):
    steps = len(sum_plan(lon_count)[0])
    sizes = [length // 4 // 2 ** (step + 1) for step in range(steps)]
    chunk = 2 * sizes[-1] // lat_count
    copies = 2 + 2 * steps + (lat_count - 1) * 2 + 2 * steps + 2
    narrow = [pltpu.VMEM((size, LANES), jnp.bfloat16) for size in sizes]
    wide = [pltpu.VMEM((size, LANES), jnp.float32) for size in sizes]
    return [
        pltpu.VMEM((2, length // 4, LANES), jnp.bfloat16),
        pltpu.VMEM((2 * sizes[-1], LANES), jnp.bfloat16),
        pltpu.VMEM((lat_count - 1, chunk, LANES), jnp.bfloat16),
        pltpu.VMEM((2 * sizes[-1], LANES), jnp.float32),
        *(narrow * 4),
        *(wide * 2),
        pltpu.SemaphoreType.DMA((copies,)),
        pltpu.SemaphoreType.DMA((copies,)),
    ]


def pusher(send_sem, recv_sem):
    count = [0]

    def push(source, target, device):
        number = count[0]
        count[0] += 1
        copy = pltpu.make_async_remote_copy(
            src_ref=source,
            dst_ref=target,
            send_sem=send_sem.at[number],
            recv_sem=recv_sem.at[number],
            device_id=device,
            device_id_type=MESH,
        )
        copy.start()
        return copy

    return push


def flat_work(lat_count, lon_count, share_ref, full_ref, scratch):
    lon_recv, lat_send, lat_recv, send_sem, recv_sem = scratch
    lat, lon = lax.axis_index("lat"), lax.axis_index("lon")
    push = pusher(send_sem, recv_sem)
    chunk = share_ref.shape[0] // lon_count
    part = chunk // lat_count
    lons = [(lon + step) % lon_count for step in range(1, lon_count)]
    lats = [(lat + step) % lat_count for step in range(1, lat_count)]
    done = []
    copies = [
        push(share_ref.at[pl.ds(aligned(peer * chunk), chunk), :], lon_recv.at[step], (lat, peer))
        for step, peer in enumerate(lons)
    ]
    yield
    total = share_ref[pl.ds(aligned(lon * chunk), chunk), :].astype(jnp.float32)
    for step, copy in enumerate(copies):
        copy.wait_recv()
        total = total + lon_recv[step].astype(jnp.float32)
    done += copies
    lat_send[...] = total.astype(jnp.bfloat16)
    copies = [
        push(lat_send.at[pl.ds(aligned(peer * part), part), :], lat_recv.at[step], (peer, lon))
        for step, peer in enumerate(lats)
    ]
    yield
    total = lat_send[pl.ds(aligned(lat * part), part), :].astype(jnp.float32)
    for step, copy in enumerate(copies):
        copy.wait_recv()
        total = total + lat_recv[step].astype(jnp.float32)
    done += copies
    mine = pl.ds(aligned(lon * chunk + lat * part), part)
    full_ref[mine, :] = total.astype(jnp.bfloat16)
    copies = [push(full_ref.at[mine, :], full_ref.at[mine, :], (peer, lon)) for peer in lats]
    yield
    for copy in copies:
        copy.wait_recv()
    done += copies
    region = pl.ds(aligned(lon * chunk), chunk)
    copies = [push(full_ref.at[region, :], full_ref.at[region, :], (lat, peer)) for peer in lons]
    yield
    for copy in copies:
        copy.wait_recv()
    done += copies
    for copy in done:
        copy.wait_send()


def flat_scratch(length, lat_count, lon_count):
    chunk = length // lon_count
    copies = 2 * (lat_count + lon_count - 2)
    return [
        pltpu.VMEM((lon_count - 1, chunk, LANES), jnp.bfloat16),
        pltpu.VMEM((chunk, LANES), jnp.bfloat16),
        pltpu.VMEM((lat_count - 1, chunk // lat_count, LANES), jnp.bfloat16),
        pltpu.SemaphoreType.DMA((copies,)),
        pltpu.SemaphoreType.DMA((copies,)),
    ]


def small_work(lat_count, lon_count, share_ref, full_ref, scratch):
    lon_terms, lat_terms, middle, send_sem, recv_sem = scratch
    lat, lon = lax.axis_index("lat"), lax.axis_index("lon")
    push = pusher(send_sem, recv_sem)
    copies = []
    for step in range(1, lon_count):
        copies.append(push(share_ref, lon_terms.at[lon], (lat, (lon + step) % lon_count)))
    lon_terms[lon] = share_ref[...]
    yield
    for copy in copies:
        copy.wait_recv()
    total = lon_terms[0].astype(jnp.float32)
    for term in range(1, lon_count):
        total = total + lon_terms[term].astype(jnp.float32)
    middle[...] = total.astype(jnp.bfloat16)
    for step in range(1, lat_count):
        copies.append(push(middle, lat_terms.at[lat], ((lat + step) % lat_count, lon)))
    lat_terms[lat] = middle[...]
    yield
    for copy in copies[lon_count - 1 :]:
        copy.wait_recv()
    total = lat_terms[0].astype(jnp.float32)
    for term in range(1, lat_count):
        total = total + lat_terms[term].astype(jnp.float32)
    full_ref[...] = total.astype(jnp.bfloat16)
    for copy in copies:
        copy.wait_send()


def small_scratch(length, lat_count, lon_count):
    copies = lat_count + lon_count - 2
    return [
        pltpu.VMEM((lon_count, length, LANES), jnp.bfloat16),
        pltpu.VMEM((lat_count, length, LANES), jnp.bfloat16),
        pltpu.VMEM((length, LANES), jnp.bfloat16),
        pltpu.SemaphoreType.DMA((copies,)),
        pltpu.SemaphoreType.DMA((copies,)),
    ]


def grids_kernel(lat_count, lon_count, sizes, *refs):
    atmos_halo, ocean_halo = refs[:5], refs[5:10]
    atmos_args, ocean_args, land = refs[10:15], refs[15:20], refs[20]
    atmos_next, ocean_next, atmos_full, ocean_full, atmos_small, ocean_small = refs[21:27]
    rest = list(refs[27:])
    parts = []
    for size in sizes:
        parts.append(rest[:size])
        rest = rest[size:]
    atmos_part, ocean_part, atmos_sum, ocean_sum, atmos_small_sum, ocean_small_sum = parts
    banded, atmos_share, ocean_share, atmos_few, ocean_few = rest
    lat, lon = lax.axis_index("lat"), lax.axis_index("lon")
    met = greet(
        [((lat + step) % lat_count, lon) for step in range(1, lat_count)]
        + [(lat, (lon + step) % lon_count) for step in range(1, lon_count)]
    )

    def along(work, *plan):
        for number, _ in enumerate(work):
            for sums, places in plan:
                if number in places:
                    next(sums, None)

    def begin(work, *args):
        sums = work(lat_count, lon_count, *args)
        next(sums)
        return sums

    def first_part(halo, args, mask, result, share, part):
        cot, kernel, gain, w_in, w_out = args
        return grid_work(halo, cot, mask, kernel, gain, w_in, w_out, result, share, banded, part)

    along(first_part(atmos_halo, atmos_args, None, atmos_next, atmos_share, atmos_part))
    met()
    first = begin(sum_work, atmos_share, atmos_full, atmos_sum)
    along(
        first_part(ocean_halo, ocean_args, land, ocean_next, ocean_share, ocean_part),
        (first, (3, 6, 8, 9)),
    )
    second = begin(flat_work, ocean_share, ocean_full, ocean_sum)
    along(tap_work(atmos_few, atmos_part), (first, (2, 6, 11)), (second, (5, 10)))
    third = begin(small_work, atmos_few, atmos_small, atmos_small_sum)
    along(tap_work(ocean_few, ocean_part), (second, (1,)), (third, (4,)))
    last = begin(small_work, ocean_few, ocean_small, ocean_small_sum)
    next(last)
    for sums in (first, second, third, last):
        for _ in sums:
            pass


def run_grids(atmos_halo, ocean_halo, land_sea, atmos_args, ocean_args):
    lat_count, lon_count = lax.axis_size("lat"), lax.axis_size("lon")
    vmem = pl.BlockSpec(memory_space=pltpu.VMEM)
    flat, states, shares, smalls, parts = [], [], [], [], []
    for cotangent, kernel, gain, w_in, w_out in (atmos_args, ocean_args):
        rows, cols, channels = cotangent.shape
        flat += [cotangent.reshape(rows * cols, channels), kernel, gain.reshape(-1, LANES), w_in, w_out]
        states.append((rows * cols, channels))
        shares.append((packed_rows(*w_in.shape, lat_count * lon_count), LANES))
        smalls.append((channels // LANES * SMALL, LANES))
        parts.append(grid_scratch(cotangent, w_in.shape[1]))
    parts.append(sum_scratch(shares[0][0], lat_count, lon_count))
    parts.append(flat_scratch(shares[1][0], lat_count, lon_count))
    parts += [small_scratch(small[0], lat_count, lon_count) for small in smalls]
    narrow = shares + smalls
    args = (*atmos_halo, *ocean_halo, *flat, land_sea)
    outs = pl.pallas_call(
        functools.partial(grids_kernel, lat_count, lon_count, tuple(len(part) for part in parts)),
        out_shape=tuple(jax.ShapeDtypeStruct(shape, jnp.bfloat16) for shape in states + narrow),
        in_specs=[vmem] * len(args),
        out_specs=(vmem,) * (len(states) + len(narrow)),
        scratch_shapes=[
            *(piece for part in parts for piece in part),
            pltpu.VMEM((28, 2 * LANES, 2 * LANES), jnp.bfloat16),
            *(pltpu.VMEM(shape, jnp.bfloat16) for shape in narrow),
        ],
        compiler_params=pltpu.CompilerParams(
            collective_id=2, has_side_effects=True, vmem_limit_bytes=60 * 1024 * 1024
        ),
    )(*args)
    return outs[:2], outs[2:4], outs[4:]


def to_tiles(pieces):
    return jnp.concatenate([piece.astype(jnp.float32) for piece in pieces], axis=0).astype(jnp.bfloat16)


def front_kernel(lat_count, lon_count, *refs):
    (
        atmos_ref,
        ocean_ref,
        land_ref,
        fold_ref,
        ocean_pairs,
        ocean_counts,
        ocean_weights_hbm,
        atmos_pairs,
        atmos_counts,
        atmos_weights_hbm,
        flux_map,
        surface_map,
        flux_inject,
        surface_inject,
    ) = refs[:14]
    atmos_out, ocean_out = refs[14:19], refs[19:24]
    (
        near_atmos,
        near_ocean,
        ocean_weights,
        atmos_weights,
        atmos_first,
        atmos_last,
        ocean_first,
        ocean_last,
        top_rows,
        circle_rows,
        send_sem,
        recv_sem,
        local_sem,
    ) = refs[24:]
    lat, lon = lax.axis_index("lat"), lax.axis_index("lon")
    east, west = (lon + 1) % lon_count, (lon + lon_count - 1) % lon_count
    has_south, has_north = lat > 0, lat < lat_count - 1
    beside = {-1: west, 0: lon, 1: east}
    cols = atmos_ref.shape[1]

    weight_copies = [
        pltpu.make_async_copy(ocean_weights_hbm, ocean_weights, local_sem.at[0]),
        pltpu.make_async_copy(atmos_weights_hbm, atmos_weights, local_sem.at[1]),
    ]
    for copy in weight_copies:
        copy.start()

    barrier = pltpu.get_barrier_semaphore()
    for step in range(1, lon_count):
        pl.semaphore_signal(
            barrier, inc=1, device_id=(lat, (lon + step) % lon_count), device_id_type=MESH
        )
    for band, there in ((-1, has_south), (1, has_north)):

        @pl.when(there)
        def _():
            for sector in (-1, 0, 1):
                pl.semaphore_signal(
                    barrier, inc=1, device_id=(lat + band, beside[sector]), device_id_type=MESH
                )

    numbers = {}

    def remote(name, source, target, device):
        number = numbers.setdefault(name, len(numbers))
        return pltpu.make_async_remote_copy(
            src_ref=source,
            dst_ref=target,
            send_sem=send_sem.at[number],
            recv_sem=recv_sem.at[number],
            device_id=device,
            device_id_type=MESH,
        )

    def each_neighbour(action):
        for band, there in ((-1, has_south), (0, None), (1, has_north)):
            for sector in (-1, 0, 1):
                if band == 0 and sector == 0:
                    continue
                if there is None:
                    action(band, sector)
                else:
                    pl.when(there)(functools.partial(action, band, sector))

    def field_copy(name, near, band, sector, waiting):
        own = near.at[4]
        return remote(
            (name, band, sector),
            own,
            near.at[(1 - band) * 3 + 1 - sector],
            (lat + band, beside[sector]),
        )

    def send_fields(name, near):
        each_neighbour(lambda band, sector: field_copy(name, near, band, sector, False).start())

    def await_fields(name, near):
        each_neighbour(
            lambda band, sector: remote(
                (name, -band, -sector),
                near.at[4],
                near.at[(1 + band) * 3 + 1 + sector],
                (lat + band, beside[sector]),
            ).wait_recv()
        )

    def fields(source, projection, near, masked):
        channels = source.shape[2]
        turned = projection[...]

        def one_block(block, carry):
            cells = source[pl.ds(2 * block, 2)].reshape(BCELLS, channels)
            values = dot(turned, cells, ((1,), (1,)))
            if masked:
                keep = jnp.concatenate(
                    [land_ref[pl.ds(2 * block, 1), :], land_ref[pl.ds(2 * block + 1, 1), :]], axis=1
                )
                values = values * keep.astype(jnp.float32)
            near[4, block] = values.astype(jnp.bfloat16)
            return carry

        lax.fori_loop(0, source.shape[0] // 2, one_block, 0, unroll=8)

    fields(atmos_ref, flux_map, near_atmos, False)
    pl.semaphore_wait(
        barrier, lon_count - 1 + 3 * has_south.astype(jnp.int32) + 3 * has_north.astype(jnp.int32)
    )
    send_fields("atmos_fields", near_atmos)
    fields(ocean_ref, surface_map, near_ocean, True)
    send_fields("ocean_fields", near_ocean)

    def remap(near, pairs, counts, weights, state, projection, target):
        source_count = near.shape[1]
        channels = state.shape[2]
        inject = projection[...]

        def one_block(block, carry):
            count = counts[0, block]
            picked = []
            for entry in range(PAIRS):
                number = pairs[entry, block]
                owner = lax.div(number, source_count)
                local = number - owner * source_count
                band = lax.div(owner, lon_count)
                sector = owner - band * lon_count - lon + 1 + lon_count
                sector = lax.rem(sector, lon_count)
                slot = jnp.clip((band - lat + 1) * 3 + sector, 0, 8)
                value = near[slot, local]
                if entry:
                    value = jnp.where(entry < count, value, jnp.zeros_like(value))
                picked.append(value)
            left = jnp.concatenate(picked, axis=1)
            mixed = dot(left, weights[block, 0].reshape(PAIRS * BCELLS, BCELLS))
            mixed = mixed.astype(jnp.bfloat16).astype(jnp.float32).T.astype(jnp.bfloat16)
            added = dot(mixed, inject)
            cells = state[pl.ds(2 * block, 2)].reshape(BCELLS, channels).astype(jnp.float32)
            target[pl.ds(2 * block, 2)] = (
                (cells + added).astype(jnp.bfloat16).reshape(2, state.shape[1], channels)
            )
            return carry

        lax.fori_loop(0, state.shape[0] // 2, one_block, 0, unroll=8)

    def edges(target, first, last):
        channels = target.shape[2]

        def one_tile(tile, carry):
            rows = target[pl.ds(4 * tile, 4)].astype(jnp.float32)
            first[tile] = to_tiles([rows[row, :EDGE] for row in range(4)])
            last[tile] = to_tiles([rows[row, cols - EDGE :] for row in range(4)])
            return carry

        lax.fori_loop(0, target.shape[0] // 4, one_tile, 0, unroll=4)

    def halo_copy(name, out, first, last, band, sector, to_neighbour):
        target, south, north, west_edge, east_edge = out
        rows = target.shape[0]
        tiles = rows // 4
        if sector == 0:
            source = target.at[rows - 3 : rows] if band == 1 else target.at[0:3]
            place = south if band == 1 else north
        else:
            edge = last if sector == 1 else first
            place = west_edge if sector == 1 else east_edge
            if band == 0:
                source, place = edge, place.at[1 : tiles + 1]
            elif band == 1:
                source, place = edge.at[tiles - 1], place.at[0]
            else:
                source, place = edge.at[0], place.at[tiles + 1]
        flip = 1 if to_neighbour else -1
        return remote(
            (name, band, sector), source, place, (lat + flip * band, beside[flip * sector])
        )

    def send_halo(name, out, first, last):
        each_neighbour(
            lambda band, sector: halo_copy(name, out, first, last, band, sector, True).start()
        )

    def await_halo(name, out, first, last):
        each_neighbour(
            lambda band, sector: halo_copy(name, out, first, last, -band, -sector, False).wait_recv()
        )

    def blank(out, at_north):
        target, south, north, west_edge, east_edge = out
        rim = north if at_north else south
        tile = target.shape[0] // 4 + 1 if at_north else 0
        rim[...] = jnp.zeros_like(rim)
        west_edge[tile] = jnp.zeros(west_edge.shape[1:], jnp.bfloat16)
        east_edge[tile] = jnp.zeros(east_edge.shape[1:], jnp.bfloat16)

    pl.when(jnp.logical_not(has_south))(lambda: blank(atmos_out, False))
    pl.when(jnp.logical_not(has_south))(lambda: blank(ocean_out, False))
    pl.when(jnp.logical_not(has_north))(lambda: blank(atmos_out, True))

    await_fields("atmos_fields", near_atmos)
    weight_copies[0].wait()
    remap(near_atmos, ocean_pairs, ocean_counts, ocean_weights, ocean_ref, flux_inject, ocean_out[0])
    edges(ocean_out[0], ocean_first, ocean_last)
    send_halo("ocean_halo", ocean_out, ocean_first, ocean_last)
    is_top = jnp.logical_not(has_north)
    top_at = ocean_out[0].shape[0] - 3

    def fold_copy(step, to_peer):
        flip = step if to_peer else lon_count - step
        return remote(
            ("fold", step),
            top_rows,
            circle_rows.at[:, pl.ds(pl.multiple_of(((lon if to_peer else (lon + flip) % lon_count)) * cols, 16), cols), :],
            (lat, (lon + flip) % lon_count),
        )

    @pl.when(is_top)
    def _():
        for row in range(3):
            top_rows[row] = ocean_out[0][top_at + 2 - row]
        for step in range(1, lon_count):
            fold_copy(step, True).start()
        own = pl.ds(pl.multiple_of(lon * cols, 16), cols)
        for row in range(3):
            circle_rows[row, own, :] = top_rows[row]

    await_fields("ocean_fields", near_ocean)
    weight_copies[1].wait()
    remap(near_ocean, atmos_pairs, atmos_counts, atmos_weights, atmos_ref, surface_inject, atmos_out[0])
    edges(atmos_out[0], atmos_first, atmos_last)
    send_halo("atmos_halo", atmos_out, atmos_first, atmos_last)

    @pl.when(is_top)
    def _():
        for step in range(1, lon_count):
            fold_copy(step, False).wait_recv()
        length = lon_count * cols
        partner = fold_ref[...]

        def chosen(first, count, repeat):
            place = lax.broadcasted_iota(jnp.int32, (count, length), 0)
            if repeat is not None:
                wanted = lax.rem(lon * cols + first + length + lax.rem(place, EDGE), length)
                live = place // EDGE == repeat
                return jnp.where(live & (partner == wanted), 1.0, 0.0).astype(jnp.bfloat16)
            return jnp.where(partner == lon * cols + place, 1.0, 0.0).astype(jnp.bfloat16)

        _, _, north, west_edge, east_edge = ocean_out
        tile = ocean_out[0].shape[0] // 4 + 1
        middle = chosen(0, cols, None)
        sides = [None, None]
        for row in range(3):
            line = circle_rows[row]
            north[row] = dot(middle, line).astype(jnp.bfloat16)
            for side, first in enumerate((-EDGE, cols)):
                part = dot(chosen(first, 16, row), line)
                sides[side] = part if row == 0 else sides[side] + part
        west_edge[tile] = sides[0].astype(jnp.bfloat16)
        east_edge[tile] = sides[1].astype(jnp.bfloat16)

    await_halo("ocean_halo", ocean_out, ocean_first, ocean_last)
    await_halo("atmos_halo", atmos_out, atmos_first, atmos_last)
    for name, near in (("atmos_fields", near_atmos), ("ocean_fields", near_ocean)):
        each_neighbour(
            lambda band, sector: field_copy(name, near, band, sector, False).wait_send()
        )
    for name, out, first, last in (
        ("ocean_halo", ocean_out, ocean_first, ocean_last),
        ("atmos_halo", atmos_out, atmos_first, atmos_last),
    ):
        each_neighbour(
            lambda band, sector: halo_copy(name, out, first, last, band, sector, True).wait_send()
        )

    @pl.when(is_top)
    def _():
        for step in range(1, lon_count):
            fold_copy(step, True).wait_send()


def front(
    atmos_state,
    ocean_state,
    land_sea,
    fold_partner,
    ocean_pairs,
    ocean_counts,
    ocean_weights,
    atmos_pairs,
    atmos_counts,
    atmos_weights,
    flux_map,
    surface_map,
    flux_inject,
    surface_inject,
):
    lat_count, lon_count = lax.axis_size("lat"), lax.axis_size("lon")
    vmem = pl.BlockSpec(memory_space=pltpu.VMEM)
    smem = pl.BlockSpec(memory_space=pltpu.SMEM)
    anywhere = pl.BlockSpec(memory_space=pl.ANY)

    def out_shapes(state):
        rows, cols, channels = state.shape
        return [
            jax.ShapeDtypeStruct(shape, jnp.bfloat16)
            for shape in (
                (rows, cols, channels),
                (3, cols, channels),
                (3, cols, channels),
                (rows // 4 + 2, 16, channels),
                (rows // 4 + 2, 16, channels),
            )
        ]

    def edge_scratch(state):
        return pltpu.VMEM((state.shape[0] // 4, 16, state.shape[2]), jnp.bfloat16)

    copies = 32 + lon_count - 1
    cols = atmos_state.shape[1]
    ocean_channels = ocean_state.shape[2]
    outs = pl.pallas_call(
        functools.partial(front_kernel, lat_count, lon_count),
        out_shape=tuple(out_shapes(atmos_state) + out_shapes(ocean_state)),
        in_specs=[vmem, vmem, vmem, vmem, smem, smem, anywhere, smem, smem, anywhere] + [vmem] * 4,
        out_specs=(vmem,) * 10,
        scratch_shapes=[
            pltpu.VMEM((9, atmos_state.shape[0] // 2, NFIELD, BCELLS), jnp.bfloat16),
            pltpu.VMEM((9, ocean_state.shape[0] // 2, NFIELD, BCELLS), jnp.bfloat16),
            pltpu.VMEM(ocean_weights.shape, jnp.bfloat16),
            pltpu.VMEM(atmos_weights.shape, jnp.bfloat16),
            edge_scratch(atmos_state),
            edge_scratch(atmos_state),
            edge_scratch(ocean_state),
            edge_scratch(ocean_state),
            pltpu.VMEM((3, cols, ocean_channels), jnp.bfloat16),
            pltpu.VMEM((3, lon_count * cols, ocean_channels), jnp.bfloat16),
            pltpu.SemaphoreType.DMA((copies,)),
            pltpu.SemaphoreType.DMA((copies,)),
            pltpu.SemaphoreType.DMA((2,)),
        ],
        compiler_params=pltpu.CompilerParams(
            collective_id=1, has_side_effects=True, vmem_limit_bytes=60 * 1024 * 1024
        ),
    )(
        atmos_state,
        ocean_state,
        land_sea,
        fold_partner.reshape(1, -1),
        ocean_pairs.reshape(-1, PAIRS).T,
        ocean_counts.T,
        ocean_weights,
        atmos_pairs.reshape(-1, PAIRS).T,
        atmos_counts.T,
        atmos_weights,
        flux_map.T,
        surface_map.T,
        flux_inject,
        surface_inject,
    )
    return outs[:5], outs[5:]


def shards(
    atmos_state,
    ocean_state,
    atmos_cotangent,
    ocean_cotangent,
    land_sea,
    fold_partner,
    ocean_pairs,
    ocean_counts,
    ocean_weights,
    atmos_pairs,
    atmos_counts,
    atmos_weights,
    flux_map,
    surface_map,
    flux_inject,
    surface_inject,
    atmos_kernel,
    atmos_gain,
    atmos_w_in,
    atmos_w_out,
    ocean_kernel,
    ocean_gain,
    ocean_w_in,
    ocean_w_out,
):
    atmos_halo, ocean_halo = front(
        atmos_state,
        ocean_state,
        land_sea,
        fold_partner,
        ocean_pairs,
        ocean_counts,
        ocean_weights,
        atmos_pairs,
        atmos_counts,
        atmos_weights,
        flux_map,
        surface_map,
        flux_inject,
        surface_inject,
    )
    states, packed, smalls = run_grids(
        atmos_halo,
        ocean_halo,
        land_sea,
        (atmos_cotangent, atmos_kernel, atmos_gain, atmos_w_in, atmos_w_out),
        (ocean_cotangent, ocean_kernel, ocean_gain, ocean_w_in, ocean_w_out),
    )
    outs = unpack(states, packed, smalls, (atmos_w_in.shape, ocean_w_in.shape))
    return (outs[0].reshape(atmos_state.shape), outs[1].reshape(ocean_state.shape), *outs[2:])


def solution(mesh):
    return jax.shard_map(
        shards,
        mesh=mesh,
        in_specs=(
            P("lat", "lon", None),
            P("lat", "lon", None),
            P("lat", "lon", None),
            P("lat", "lon", None),
            P("lat", "lon"),
            P(),
            P("lat", "lon", None),
            P("lat", "lon"),
            P("lat", "lon", None, None, None),
            P("lat", "lon", None),
            P("lat", "lon"),
            P("lat", "lon", None, None, None),
            P(),
            P(),
            P(),
            P(),
            P(),
            P(),
            P(),
            P(),
            P(),
            P(),
            P(),
            P(),
        ),
        out_specs=(
            P("lat", "lon", None),
            P("lat", "lon", None),
            P(),
            P(),
            P(),
            P(),
            P(),
            P(),
            P(),
            P(),
        ),
        check_vma=False,
    )
```
